32 devices in a mesh: noise: 8 (over z, x), qi: 2 (over core), kj: 2 (over y).
Axes of the slice: x: 2, y: 2, z: 4, core: 2. Of those that a mesh axis runs over, the one named last changes fastest.
Arguments:
- pair_rep: bfloat16 [128, 2, 64, 128], P('qi', None, 'kj'), may hold values from -6 to 6
- query_rows: bfloat16 [8, 128, 768], P('noise', 'qi'), may hold values from -10 to 10
- key_rows: bfloat16 [8, 2, 64, 768], P('noise', None, 'kj'), may hold values from -10 to 10
- value_rows: bfloat16 [8, 2, 64, 768], P('noise', None, 'kj'), may hold values from -6 to 6
- output_grad: bfloat16 [8, 128, 768], P('noise', 'qi'), may hold values from -24 to 24
- gain_first: float32 [128], replicated, may hold values from 0.5 to 1.5
- gate_weight: bfloat16 [128, 512], replicated, may hold values from -0.5 to 0.5
- up_weight: bfloat16 [128, 512], replicated, may hold values from -0.5 to 0.5
- down_weight: bfloat16 [512, 128], replicated, may hold values from -0.25 to 0.25
- gain_second: float32 [128], replicated, may hold values from 0.5 to 1.5
- head_weight: bfloat16 [128, 16], replicated, may hold values from -0.5 to 0.5
Outputs:
- query_grad: bfloat16 [8, 128, 768], P('noise', ('qi', 'kj'))
- key_grad: bfloat16 [8, 128, 768], P('noise', ('qi', 'kj'))
- value_grad: bfloat16 [8, 128, 768], P('noise', ('qi', 'kj'))
- pair_grad: bfloat16 [2, 8, 8, 2, 64, 128], P('qi', 'noise', None, None, 'kj')
- gate_grad: float32 [128, 512], replicated
- up_grad: float32 [128, 512], replicated
- down_grad: float32 [512, 128], replicated
- head_grad: float32 [128, 16], replicated
- first_grad: float32 [128], replicated
- second_grad: float32 [128], replicated
The draws below stay inside these ranges and needn't reach their ends.
All inputs are finite; a program needn't handle non-finite values.
Results may differ from the reference program's by a relative error of at most 0.011.
Values may be sent and summed in bfloat16 or wider, within the bound.
A program may use at most 64 MiB of HBM per device.

```python
import jax
import jax.numpy as jnp
from jax import lax

HEADS = 16
HEAD_DIM = 48
PAIR = 128
FF = 512
WIDTH = 768
TOKENS = 128
QUERY_TILE = 64
ROWS_SUB = 8
COPIES = 8
N_QI = 2


def drawn_draw(key):
    base_key = jax.random.fold_in(key, 4242)
    first_key, second_key = jax.random.split(base_key, 2)
    full_shape = (COPIES, TOKENS, HEADS, HEAD_DIM)
    queries = jnp.clip(jax.random.normal(first_key, full_shape, jnp.float32), -6.0, 6.0)
    keyset = jnp.clip(jax.random.normal(second_key, full_shape, jnp.float32), -6.0, 6.0)
    queries = queries.reshape(COPIES, TOKENS, HEADS * HEAD_DIM)
    keyset = keyset.reshape(COPIES, TOKENS // QUERY_TILE, QUERY_TILE, HEADS * HEAD_DIM)
    return (queries, keyset)


def draw_query_rows(key, part):
    return drawn_draw(key)[0].astype(jnp.bfloat16)


def draw_key_rows(key, part):
    return drawn_draw(key)[1].astype(jnp.bfloat16)


def steps_of(rng, extent, cuts, smallest, high):
    loudness, own = 1.0, jax.random.fold_in(rng, 6)
    for dim, blocks in cuts:
        draws = jnp.exp(jax.random.uniform(jax.random.fold_in(own, dim), (blocks,), jnp.float32, smallest / len(cuts), high / len(cuts)))
        loudness = loudness * jnp.repeat(draws, extent[dim] // blocks).reshape([-1 if axis == dim else 1 for axis in range(len(extent))])
    return loudness


def bell_draw(key, dims, width, limit, shards=(), kind=jnp.bfloat16):
    result = width * jax.random.normal(key, dims, jnp.float32)
    if shards:
        result = result * steps_of(key, dims, shards, -0.22, 0.18)
    return jnp.clip(result, -limit, limit).astype(kind)


def setup_inputs(seed: int = 0) -> dict:
    streams_of = jax.random.split(jax.random.key(seed), 12)
    return {
        "pair_rep": bell_draw(streams_of[0], (TOKENS, N_QI, QUERY_TILE, PAIR), 1.0, 6.0, ((0, 2), (2, 2))),
        "query_rows": draw_query_rows(jax.random.fold_in(streams_of[11], 71), 0),
        "key_rows": draw_key_rows(jax.random.fold_in(streams_of[11], 71), 0),
        "value_rows": bell_draw(streams_of[3], (COPIES, N_QI, QUERY_TILE, WIDTH), 1.0, 6.0, ((0, 8), (2, 2))),
        "output_grad": bell_draw(streams_of[4], (COPIES, TOKENS, WIDTH), (TOKENS / 32), 24.0, ((0, 8), (1, 2))),
        "gain_first": jnp.clip(1.0 + 0.1 * jax.random.normal(streams_of[5], (PAIR,), jnp.float32), 0.5, 1.5),
        "gate_weight": bell_draw(streams_of[6], (PAIR, FF), PAIR ** -0.5, 0.5),
        "up_weight": bell_draw(streams_of[7], (PAIR, FF), PAIR ** -0.5, 0.5),
        "down_weight": bell_draw(streams_of[8], (FF, PAIR), FF ** -0.5, 0.25),
        "gain_second": jnp.clip(1.0 + 0.1 * jax.random.normal(streams_of[9], (PAIR,), jnp.float32), 0.5, 1.5),
        "head_weight": bell_draw(streams_of[10], (PAIR, HEADS), PAIR ** -0.5, 0.5),
    }


epsilon = 1e-05

def layer_norm(values, gain_vec):
    center = values - lax.optimization_barrier(jnp.mean(values, axis=1, keepdims=True))
    inverse = lax.rsqrt(lax.optimization_barrier(jnp.mean(center * center, axis=1, keepdims=True)) + epsilon)
    normed = center * inverse
    return (normed, inverse, normed * gain_vec)

def norm_backward(normed_grad, normed, inverse):
    first_mean = lax.optimization_barrier(jnp.mean(normed_grad, axis=1, keepdims=True))
    second_mean = lax.optimization_barrier(jnp.mean(normed_grad * normed, axis=1, keepdims=True))
    return inverse * (normed_grad - first_mean - normed * second_mean)

def wide_einsum(form, left, right):
    return jnp.einsum(form, left.astype(jnp.float32), right.astype(jnp.float32))

def transition_forward(cells, params):
    gain_first, gate_weight, up_weight, down_weight, gain_second, head_weight = params
    inputs = cells.astype(jnp.float32)
    pre_normed, pre_inverse, pre_scaled = layer_norm(inputs, gain_first)
    pre_lowered = pre_scaled.astype(jnp.bfloat16)
    gate_pre = jnp.dot(pre_lowered, gate_weight, preferred_element_type=jnp.float32)
    up_pre = jnp.dot(pre_lowered, up_weight, preferred_element_type=jnp.float32)
    gate_sigmoid = jax.nn.sigmoid(gate_pre)
    hidden = (gate_pre * gate_sigmoid * up_pre).astype(jnp.bfloat16)
    updated = inputs + jnp.dot(hidden, down_weight, preferred_element_type=jnp.float32)
    post_normed, post_inverse, post_scaled = layer_norm(updated, gain_second)
    post_lowered = post_scaled.astype(jnp.bfloat16)
    bias_heads = wide_einsum('mc,ch->hm', post_lowered, head_weight).astype(jnp.bfloat16)
    saved_state = (pre_normed, pre_inverse, pre_lowered, gate_pre, up_pre, gate_sigmoid, hidden, post_normed, post_inverse, post_lowered)
    return (bias_heads, saved_state)

def transition_backward(saved_state, grad_heads, params):
    gain_first, gate_weight, up_weight, down_weight, gain_second, head_weight = params
    pre_normed, pre_inverse, pre_lowered, gate_pre, up_pre, gate_sigmoid, hidden, post_normed, post_inverse, post_lowered = saved_state
    grad_low = grad_heads.astype(jnp.bfloat16)
    post_scaled = wide_einsum('hm,ch->mc', grad_low, head_weight)
    head_part = wide_einsum('mc,hm->ch', post_lowered, grad_low)
    second_part = lax.optimization_barrier(jnp.sum(post_scaled * post_normed, axis=0))
    updated_grad = norm_backward(post_scaled * gain_second, post_normed, post_inverse)
    updated_low = updated_grad.astype(jnp.bfloat16)
    down_part = wide_einsum('mf,mc->fc', hidden, updated_low)
    hidden_grad = wide_einsum('mc,fc->mf', updated_low, down_weight)
    gate_low = (hidden_grad * up_pre * gate_sigmoid * (1.0 + gate_pre * (1.0 - gate_sigmoid))).astype(jnp.bfloat16)
    up_low = (hidden_grad * gate_pre * gate_sigmoid).astype(jnp.bfloat16)
    gate_part = wide_einsum('mc,mf->cf', pre_lowered, gate_low)
    up_part = wide_einsum('mc,mf->cf', pre_lowered, up_low)
    pre_scaled = wide_einsum('mf,cf->mc', gate_low, gate_weight) + wide_einsum('mf,cf->mc', up_low, up_weight)
    first_part = lax.optimization_barrier(jnp.sum(pre_scaled * pre_normed, axis=0))
    inputs_grad = norm_backward(pre_scaled * gain_first, pre_normed, pre_inverse)
    pair_low = (updated_grad + inputs_grad).astype(jnp.bfloat16)
    return (pair_low, (gate_part, up_part, down_part, head_part, first_part, second_part))

def reference(pair_rep, query_rows, key_rows, value_rows, output_grad, gain_first, gate_weight, up_weight, down_weight, gain_second, head_weight):
    params = (gain_first, gate_weight, up_weight, down_weight, gain_second, head_weight)
    score_scale = HEAD_DIM ** (-0.5)
    block_count = TOKENS // ROWS_SUB
    pair_full = pair_rep.reshape(block_count, ROWS_SUB * TOKENS, PAIR)
    bias_blocks = lax.map(lambda cells: transition_forward(cells, params)[0], pair_full)
    bias_full = bias_blocks.reshape(block_count, HEADS, ROWS_SUB, TOKENS).transpose(1, 0, 2, 3).reshape(HEADS, TOKENS, TOKENS)
    keys_all = key_rows.reshape(COPIES, TOKENS, WIDTH)
    values_all = value_rows.reshape(COPIES, TOKENS, WIDTH)

    def one_copy(running, items):
        query_copy, key_copy, value_copy, grad_copy = items
        query_tile = query_copy.astype(jnp.float32).reshape(TOKENS, HEADS, HEAD_DIM)
        keys_tile = key_copy.astype(jnp.float32).reshape(TOKENS, HEADS, HEAD_DIM)
        values_tile = value_copy.astype(jnp.float32).reshape(TOKENS, HEADS, HEAD_DIM)
        grad_tile = grad_copy.astype(jnp.float32).reshape(TOKENS, HEADS, HEAD_DIM)
        scores = jnp.einsum('qhd,khd->hqk', query_tile, keys_tile) * score_scale + bias_full.astype(jnp.float32)
        largest = lax.optimization_barrier(jnp.max(scores, axis=2, keepdims=True))
        expo = jnp.exp(scores - largest)
        attend = expo / lax.optimization_barrier(jnp.sum(expo, axis=2, keepdims=True))
        attend_grad = jnp.einsum('qhd,khd->hqk', grad_tile, values_tile)
        delta = lax.optimization_barrier(jnp.sum(attend * attend_grad, axis=2, keepdims=True))
        score_grad = attend * (attend_grad - delta)
        score_low = score_grad.astype(jnp.bfloat16).astype(jnp.float32)
        attend_low = attend.astype(jnp.bfloat16).astype(jnp.float32)
        query_out = (jnp.einsum('hqk,khd->qhd', score_low, keys_tile) * score_scale).astype(jnp.bfloat16)
        key_out = (jnp.einsum('hqk,qhd->khd', score_low, query_tile) * score_scale).astype(jnp.bfloat16)
        value_out = jnp.einsum('hqk,qhd->khd', attend_low, grad_tile).astype(jnp.bfloat16)
        return (running + score_grad, (query_out.reshape(TOKENS, WIDTH), key_out.reshape(TOKENS, WIDTH), value_out.reshape(TOKENS, WIDTH)))
    initial = jnp.zeros((HEADS, TOKENS, TOKENS), jnp.float32)
    bias_sum, outputs = lax.scan(one_copy, initial, (query_rows, keys_all, values_all, output_grad))
    query_grad, key_grad, value_grad = outputs
    grad_blocks = bias_sum.reshape(HEADS, block_count, ROWS_SUB * TOKENS).transpose(1, 0, 2)

    def one_block(running, items):
        cells, grad_heads = items
        saved_state = transition_forward(cells, params)[1]
        pair_low, weight_parts = transition_backward(saved_state, grad_heads, params)
        return (tuple((total + part for total, part in zip(running, weight_parts))), pair_low)
    zeros_init = (jnp.zeros((PAIR, FF), jnp.float32), jnp.zeros((PAIR, FF), jnp.float32), jnp.zeros((FF, PAIR), jnp.float32), jnp.zeros((PAIR, HEADS), jnp.float32), jnp.zeros((PAIR,), jnp.float32), jnp.zeros((PAIR,), jnp.float32))
    reduced, pair_blocks = lax.scan(one_block, zeros_init, (pair_full, grad_blocks))
    pair_grad = pair_blocks.reshape(N_QI, COPIES, ROWS_SUB, N_QI, QUERY_TILE, PAIR)
    factor = 1.0 / TOKENS
    return (query_grad, key_grad, value_grad, pair_grad, reduced[0] * factor, reduced[1] * factor, reduced[2] * factor, reduced[3] * factor, reduced[4] * factor, reduced[5] * factor)
```

```python
import functools
import math

import jax
import jax.numpy as jnp
from jax import lax
from jax.experimental import pallas as pl
from jax.experimental.pallas import tpu as pltpu
from jax.sharding import PartitionSpec as P

HEADS = 16
HEAD_DIM = 48
ALIGN = 8
BLOCK = 16
LANES = 128

epsilon = 1e-05
F32 = jnp.float32
BF16 = jnp.bfloat16
MESH = pl.DeviceIdType.MESH


def dot(left, right, left_dim, right_dim):
    return lax.dot_general(
        left, right, (((left_dim,), (right_dim,)), ((), ())), preferred_element_type=F32
    )


def normalize(values):
    center = values - jnp.mean(values, axis=1, keepdims=True)
    inverse = lax.rsqrt(jnp.mean(center * center, axis=1, keepdims=True) + epsilon)
    return center * inverse, inverse


def norm_backward(normed_grad, normed, inverse):
    first_mean = jnp.mean(normed_grad, axis=1, keepdims=True)
    second_mean = jnp.mean(normed_grad * normed, axis=1, keepdims=True)
    return inverse * (normed_grad - first_mean - normed * second_mean)


def place(parts_of, row):
    wave = 0
    while row >= parts_of[wave]:
        row -= parts_of[wave]
        wave += 1
    return wave, row


def kernel(
    sizes,
    pair_hbm,
    q_hbm,
    k_hbm,
    v_hbm,
    g_hbm,
    gain_first_hbm,
    gate_hbm,
    up_hbm,
    down_hbm,
    gain_second_hbm,
    head_hbm,
    query_out,
    key_out,
    value_out,
    pair_out,
    tail_out,
    q_ref,
    k_ref,
    v_ref,
    g_ref,
    gain_first_ref,
    gate_ref,
    up_ref,
    down_ref,
    gain_second_ref,
    head_ref,
    cells,
    pre_normed,
    pre_low,
    pre_low_t,
    gate_coef,
    up_coef,
    hidden,
    hidden_t,
    up_low,
    post_normed,
    post_low,
    inverses,
    bias_rows,
    bias_all,
    score,
    attend_grad,
    stats,
    grad_send,
    grad_recv,
    grad_sum,
    post_scaled,
    query_part,
    query_recv,
    kv_part,
    kv_recv,
    tail_own,
    tail_recv,
    input_sems,
    bias_send_sem,
    bias_recv_sem,
    stat_send_sem,
    stat_recv_sem,
    grad_send_sem,
    grad_recv_sem,
    query_send_sem,
    query_recv_sem,
    pair_sems,
    w_send_sem,
    w_recv_sem,
    all_send_sem,
    all_recv_sem,
    fwd_send_sem,
    fwd_recv_sem,
    tail_send_sem,
    tail_recv_sem,
    weight_out,
    w_part,
    w_core,
    w_sum,
    w_recv,
):
    n_noise, n_qi, n_kj, rows, keys, share, parts_of = sizes
    waves = len(parts_of)
    group = n_noise * n_kj
    cell_count = share * keys
    chunk = min(256, cell_count)
    scale = HEAD_DIM ** (-0.5)
    noise = lax.axis_index("noise")
    qi = lax.axis_index("qi")
    kj = lax.axis_index("kj")
    me = noise * n_kj + kj
    sibling = {"qi": 1 - qi}
    channels = cells.shape[-1]
    width = q_ref.shape[-1]
    half = keys // n_qi
    q_half = rows // n_kj
    pack = max(1, LANES // keys)
    packed = HEADS // pack

    def members(p):
        return [p + j * packed for j in range(pack)]

    def remote(src, dst, send, recv, device):
        return pltpu.make_async_remote_copy(
            src_ref=src, dst_ref=dst, send_sem=send, recv_sem=recv, device_id=device, device_id_type=MESH
        )

    def of_group(index):
        return {"noise": index // n_kj, "kj": lax.rem(index, n_kj)}

    def each(count, body):
        def step(i, carry):
            body(i)
            return carry

        lax.fori_loop(1, count, step, 0)

    forward_loads = [
        pltpu.make_async_copy(src, dst, input_sems.at[i])
        for i, (src, dst) in enumerate(
            (
                (pair_hbm.at[pl.ds(noise * share, share)], cells),
                (gain_first_hbm, gain_first_ref),
                (gate_hbm, gate_ref),
                (up_hbm, up_ref),
                (down_hbm, down_ref),
                (gain_second_hbm, gain_second_ref),
                (head_hbm, head_ref),
            )
        )
    ]
    attention_loads = [
        pltpu.make_async_copy(src, dst, input_sems.at[len(forward_loads) + i])
        for i, (src, dst) in enumerate(((q_hbm, q_ref), (k_hbm, k_ref), (g_hbm, g_ref), (v_hbm, v_ref)))
    ]
    for load in forward_loads:
        load.start()

    barrier = pltpu.get_barrier_semaphore()

    def greet(i):
        pl.semaphore_signal(
            barrier, inc=1, device_id=of_group(lax.rem(me + i, group)), device_id_type=MESH
        )

    each(group, greet)
    pl.semaphore_signal(barrier, inc=1, device_id=sibling, device_id_type=MESH)
    for load in attention_loads:
        load.start()
    for load in forward_loads:
        load.wait()

    gain_first = gain_first_ref[...]
    gain_second = gain_second_ref[...]
    head_t = head_ref[...]
    flat_cells = cells[...].reshape(cell_count, channels)
    for start in range(0, cell_count, chunk):
        at = slice(start, start + chunk)
        inputs = flat_cells[at].astype(F32)
        normed, inverse = normalize(inputs)
        lowered = (normed * gain_first).astype(BF16)
        gate_pre = dot(lowered, gate_ref[...], 1, 0)
        up_pre = dot(lowered, up_ref[...], 1, 0)
        sigmoid = jax.nn.sigmoid(gate_pre)
        silu = gate_pre * sigmoid
        low_hidden = (silu * up_pre).astype(BF16)
        updated = inputs + dot(low_hidden, down_ref[...], 1, 0)
        after, after_inverse = normalize(updated)
        after_low = (after * gain_second).astype(BF16)
        pre_normed[at] = normed
        pre_low[at] = lowered
        gate_coef[at] = up_pre * sigmoid * (1.0 + gate_pre * (1.0 - sigmoid))
        up_coef[at] = silu
        hidden[at] = low_hidden
        post_normed[at] = after
        post_low[at] = after_low
        inverses[at, 0:1] = inverse
        inverses[at, 1:2] = after_inverse
    for i in range(share):
        bias_rows[i] = dot(head_t, post_low[i * keys : (i + 1) * keys], 1, 1)
    for p in range(packed):
        bias_all[noise, p] = jnp.concatenate([bias_rows[:, h, :] for h in members(p)], 1).astype(BF16)

    pl.semaphore_wait(barrier, group)

    def bias_copy(slot, peer):
        return remote(
            bias_all.at[slot], bias_all.at[slot], bias_send_sem.at[peer], bias_recv_sem.at[slot], {"noise": peer}
        )

    each(n_noise, lambda i: bias_copy(noise, lax.rem(noise + i, n_noise)).start())

    def head_of(ref, h):
        return ref[:, h * HEAD_DIM : (h + 1) * HEAD_DIM]

    for load in attention_loads:
        load.wait()
    for h in range(HEADS):
        score[h] = dot(head_of(q_ref, h), head_of(k_ref, h), 1, 1) * scale
        attend_grad[h] = dot(head_of(g_ref, h), head_of(v_ref, h), 1, 1)

    def bias_wait(i):
        peer = lax.rem(noise + n_noise - i, n_noise)
        bias_copy(peer, peer).wait_recv()

    hidden_t[...] = hidden[...].T
    pre_low_t[...] = pre_low[...].T
    for wave, part in enumerate(parts_of):
        if part < math.prod(w_part[wave].shape[:3]):
            w_part[wave][...] = jnp.zeros(w_part[wave].shape, BF16)
    each(n_noise, bias_wait)

    for h in range(HEADS):
        bias_at = slice(h // packed * keys, (h // packed + 1) * keys)
        full = score[h] + bias_all[:, h % packed].astype(F32).reshape(rows, pack * keys)[:, bias_at]
        largest = jnp.max(full, axis=1, keepdims=True)
        expo = jnp.exp(full - largest)
        score[h] = expo
        stats[kj, :, h : h + 1] = largest
        stats[kj, :, HEADS + h : HEADS + h + 1] = jnp.sum(expo, axis=1, keepdims=True)
        stats[kj, :, 2 * HEADS + h : 2 * HEADS + h + 1] = jnp.sum(
            expo * attend_grad[h], axis=1, keepdims=True
        )

    def stat_copy(slot, peer):
        return remote(
            stats.at[slot], stats.at[slot], stat_send_sem.at[peer], stat_recv_sem.at[slot], {"kj": peer}
        )

    each(n_kj, lambda i: stat_copy(kj, lax.rem(kj + i, n_kj)).start())

    def stat_wait(i):
        peer = lax.rem(kj + n_kj - i, n_kj)
        stat_copy(peer, peer).wait_recv()

    each(n_kj, stat_wait)

    parts = [stats[j] for j in range(n_kj)]
    row_max = parts[0][:, 0:HEADS]
    for part in parts[1:]:
        row_max = jnp.maximum(row_max, part[:, 0:HEADS])
    row_sum = jnp.zeros_like(row_max)
    row_dot = jnp.zeros_like(row_max)
    for part in parts:
        weight = jnp.exp(part[:, 0:HEADS] - row_max)
        row_sum += weight * part[:, HEADS : 2 * HEADS]
        row_dot += weight * part[:, 2 * HEADS : 3 * HEADS]
    factor = jnp.exp(stats[kj, :, 0:HEADS] - row_max) / row_sum
    delta = row_dot / row_sum
    for p in range(packed):
        pieces = []
        for h in members(p):
            attend = score[h] * factor[:, h : h + 1]
            score_grad = attend * (attend_grad[h] - delta[:, h : h + 1])
            score[h] = attend
            attend_grad[h] = score_grad
            pieces.append(score_grad)
        grad_send[:, p] = jnp.concatenate(pieces, 1).reshape(n_noise, share, pack * keys).astype(BF16)

    def grad_copy(slot, peer):
        return remote(
            grad_send.at[peer], grad_recv.at[slot], grad_send_sem.at[peer], grad_recv_sem.at[slot], {"noise": peer}
        )

    each(n_noise, lambda i: grad_copy(noise, lax.rem(noise + i, n_noise)).start())

    for h in range(HEADS):
        at = slice(h * HEAD_DIM, (h + 1) * HEAD_DIM)
        value_at = slice(width + h * HEAD_DIM, width + (h + 1) * HEAD_DIM)
        score_low = attend_grad[h].astype(BF16)
        attend_low = score[h].astype(BF16)
        query_part[:, :, at] = (
            (dot(score_low, head_of(k_ref, h), 1, 0) * scale).astype(BF16).reshape(n_kj, q_half, HEAD_DIM)
        )
        kv_part[:, :, at] = (
            (dot(score_low, head_of(q_ref, h), 0, 0) * scale).astype(BF16).reshape(n_qi, half, HEAD_DIM)
        )
        kv_part[:, :, value_at] = (
            dot(attend_low, head_of(g_ref, h), 0, 0).astype(BF16).reshape(n_qi, half, HEAD_DIM)
        )

    def query_copy(slot, peer):
        return remote(
            query_part.at[peer], query_recv.at[slot], query_send_sem.at[peer], query_recv_sem.at[slot], {"kj": peer}
        )

    each(n_kj, lambda i: query_copy(kj, lax.rem(kj + i, n_kj)).start())
    kv_copy = remote(kv_part.at[1 - qi], kv_recv, pair_sems.at[0], pair_sems.at[1], sibling)
    kv_copy.start()

    def grad_wait(i):
        peer = lax.rem(noise + n_noise - i, n_noise)
        grad_copy(peer, peer).wait_recv()

    grad_sum[...] = grad_send[noise].astype(F32)

    def grad_add(i):
        grad_wait(i)
        peer = lax.rem(noise + n_noise - i, n_noise)
        grad_sum[...] += grad_recv[peer].astype(F32)

    each(n_noise, grad_add)

    head_part = jnp.zeros((HEADS, channels), F32)
    for i in range(share):
        at = slice(i * keys, (i + 1) * keys)
        grad_row = grad_sum[:, i, :]
        grad_low = jnp.concatenate([grad_row[:, j * keys : (j + 1) * keys] for j in range(pack)], 0).astype(BF16)
        post_scaled[at] = dot(grad_low, head_t, 0, 0)
        head_part += dot(grad_low, post_low[at], 1, 0)
    hidden_count = gate_ref.shape[1]
    tiles = hidden_count // channels

    def put(t, value):
        wave, first = place(parts_of, t * channels)
        block = w_part[wave].shape[2]
        count = channels // block
        owner = first // block
        w_part[wave][owner // group, owner % group : owner % group + count] = value.astype(BF16).reshape(
            count, block, channels
        )

    starts = range(0, cell_count, chunk)
    second_part = jnp.zeros((1, channels), F32)
    down_part = jnp.zeros((hidden_count, channels), F32)
    gate_part = jnp.zeros((channels, hidden_count), F32)
    for start in starts:
        at = slice(start, start + chunk)
        scaled = post_scaled[at]
        after = post_normed[at]
        second_part += jnp.sum(scaled * after, axis=0, keepdims=True)
        updated_grad = norm_backward(scaled * gain_second, after, inverses[at, 1:2])
        updated_low = updated_grad.astype(BF16)
        post_scaled[at] = updated_grad
        down_part += dot(hidden_t[:, at], updated_low, 1, 0)
        hidden_grad = dot(updated_low, down_ref[...], 1, 1)
        gate_low = (hidden_grad * gate_coef[at]).astype(BF16)
        up_low[at] = (hidden_grad * up_coef[at]).astype(BF16)
        gate_part += dot(pre_low_t[:, at], gate_low, 1, 0)
        hidden[at] = gate_low

    for t in range(tiles):
        at = slice(t * channels, (t + 1) * channels)
        put(t, down_part[at])
        put(tiles + t, gate_part[:, at])

    def core_copy(wave):
        return remote(
            w_part[wave].at[1 - qi], w_core[wave], pair_sems.at[2 + 2 * wave], pair_sems.at[3 + 2 * wave], sibling
        )

    if waves > 1:
        core_copy(0).start()

    first_part = jnp.zeros((1, channels), F32)
    up_part = jnp.zeros((channels, hidden_count), F32)
    for start in starts:
        at = slice(start, start + chunk)
        up_part += dot(pre_low_t[:, at], up_low[at], 1, 0)
        pre_scaled = dot(hidden[at], gate_ref[...], 1, 1) + dot(up_low[at], up_ref[...], 1, 1)
        first_part += jnp.sum(pre_scaled * pre_normed[at], axis=0, keepdims=True)
        post_normed[at] = pre_scaled
    for t in range(tiles):
        put(2 * tiles + t, up_part[:, t * channels : (t + 1) * channels])
    core_copy(waves - 1).start()

    tail_own[0, 0:HEADS] = head_part
    tail_own[0, HEADS : HEADS + 1] = first_part
    tail_own[0, HEADS + 1 : HEADS + 2] = second_part
    tail_own[0, HEADS + 2 :] = jnp.zeros((ALIGN - 2, channels), F32)
    tail_steps = tail_own.shape[0] - 1

    def tail_copy(step):
        peer = sibling if step == 0 else of_group(lax.bitwise_xor(me, 1 << (step - 1)))
        return remote(
            tail_own.at[step], tail_recv.at[step], tail_send_sem.at[step], tail_recv_sem.at[step], peer
        )

    def tail_next(step):
        tail_copy(step).wait_recv()
        tail_own[step + 1] = tail_own[step] + tail_recv[step]
        if step + 1 < tail_steps:
            tail_copy(step + 1).start()

    tail_copy(0).start()

    def w_copy(wave, slot, peer):
        return remote(
            w_sum[wave].at[peer],
            w_recv[wave].at[slot],
            w_send_sem.at[wave * group + peer],
            w_recv_sem.at[wave * group + slot],
            of_group(peer),
        )

    def all_copy(wave, slot, peer):
        at = weight_out[wave].at[qi, slot]
        return remote(
            at, at, all_send_sem.at[wave * group + peer], all_recv_sem.at[wave * group + slot], of_group(peer)
        )

    def fwd_copy(wave, core):
        at = weight_out[wave].at[core]
        return remote(at, at, fwd_send_sem.at[wave], fwd_recv_sem.at[wave], sibling)

    for wave in range(waves):
        core_copy(wave).wait_recv()
        w_sum[wave][...] = (w_part[wave][qi].astype(F32) + w_core[wave][...].astype(F32)).astype(BF16)
        each(group, lambda i: w_copy(wave, me, lax.rem(me + i, group)).start())
    tail_next(0)

    for start in starts:
        at = slice(start, start + chunk)
        inputs_grad = norm_backward(post_normed[at] * gain_first, pre_normed[at], inverses[at, 0:1])
        pair_out[at] = (post_scaled[at] + inputs_grad).astype(BF16)

    total = query_part[kj].astype(F32)

    def query_add(i, total):
        peer = lax.rem(kj + n_kj - i, n_kj)
        query_copy(peer, peer).wait_recv()
        return total + query_recv[peer].astype(F32)

    query_out[...] = lax.fori_loop(1, n_kj, query_add, total).astype(BF16)
    kv_copy.wait_recv()
    kv_total = kv_part[qi].astype(F32) + kv_recv[...].astype(F32)
    key_out[...] = kv_total[:, :width].astype(BF16)
    value_out[...] = kv_total[:, width:].astype(BF16)

    for wave in range(waves):

        def w_add(i, total):
            peer = lax.rem(me + group - i, group)
            w_copy(wave, peer, peer).wait_recv()
            return total + w_recv[wave][peer].astype(F32)

        total = lax.fori_loop(1, group, w_add, w_sum[wave][me].astype(F32))
        weight_out[wave][qi, me] = (total * (1.0 / (rows * n_qi))).astype(BF16)
        each(group, lambda i: all_copy(wave, me, lax.rem(me + i, group)).start())
        if 1 + wave < tail_steps:
            tail_next(1 + wave)

    for wave in range(waves):

        def all_wait(i):
            peer = lax.rem(me + group - i, group)
            all_copy(wave, peer, peer).wait_recv()

        each(group, all_wait)
        fwd_copy(wave, qi).start()
        if 1 + waves + wave < tail_steps:
            tail_next(1 + waves + wave)
    for step in range(1 + 2 * waves, tail_steps):
        tail_next(step)
    tail_out[...] = tail_own[tail_steps] * (1.0 / (rows * n_qi))

    for wave in range(waves):
        fwd_copy(wave, 1 - qi).wait_recv()
        fwd_copy(wave, qi).wait_send()

        def drain(i):
            peer = lax.rem(me + i, group)
            w_copy(wave, me, peer).wait_send()
            all_copy(wave, me, peer).wait_send()

        each(group, drain)
        core_copy(wave).wait_send()
    for step in range(tail_steps):
        tail_copy(step).wait_send()

    def drain_noise(i):
        peer = lax.rem(noise + i, n_noise)
        bias_copy(noise, peer).wait_send()
        grad_copy(noise, peer).wait_send()

    each(n_noise, drain_noise)

    def drain_kj(i):
        peer = lax.rem(kj + i, n_kj)
        stat_copy(kj, peer).wait_send()
        query_copy(kj, peer).wait_send()

    each(n_kj, drain_kj)
    kv_copy.wait_send()


def finish(
    hidden_count,
    parts_of,
    group,
    tail_ref,
    query_ref,
    key_ref,
    value_ref,
    pair_ref,
    query_out,
    key_out,
    value_out,
    pair_out,
    gate_out,
    up_out,
    down_out,
    head_out,
    first_out,
    second_out,
    gate_wide,
    up_wide,
    down_wide,
    first_wide,
    second_wide,
    sems,
    weight_ref,
):
    copies = []

    def store(src, dst):
        copy = pltpu.make_async_copy(src, dst, sems.at[len(copies)])
        copy.start()
        copies.append(copy)

    store(pair_ref, pair_out)
    store(query_ref, query_out)
    store(key_ref, key_out)
    store(value_ref, value_out)
    channels = tail_ref.shape[1]
    tiles = hidden_count // channels

    def tile(t):
        wave, first = place(parts_of, t * channels)
        block = weight_ref[wave].shape[2]
        count = channels // block
        owner = first // block
        value = weight_ref[wave][owner // group, owner % group : owner % group + count]
        return value.astype(F32).reshape(channels, channels)

    for t in range(tiles):
        down_wide[t * channels : (t + 1) * channels] = tile(t)
    store(down_wide, down_out)
    for t in range(tiles):
        gate_wide[:, t * channels : (t + 1) * channels] = tile(tiles + t)
    store(gate_wide, gate_out)
    for t in range(tiles):
        up_wide[:, t * channels : (t + 1) * channels] = tile(2 * tiles + t)
    store(up_wide, up_out)
    store(tail_ref.at[pl.ds(0, HEADS)], head_out)
    first_wide[...] = tail_ref[HEADS : HEADS + 1]
    second_wide[...] = tail_ref[HEADS + 1 : HEADS + 2]
    store(first_wide, first_out)
    store(second_wide, second_out)
    for copy in copies:
        copy.wait()


def local(
    mesh_shape,
    pair_rep,
    query_rows,
    key_rows,
    value_rows,
    output_grad,
    gain_first,
    gate_weight,
    up_weight,
    down_weight,
    gain_second,
    head_weight,
):
    n_noise, n_qi, n_kj = mesh_shape
    rows, block_count, block_rows, channels = pair_rep.shape
    keys = block_count * block_rows
    width = query_rows.shape[2]
    share = rows // n_noise
    count = share * keys
    group = n_noise * n_kj
    hidden_count = gate_weight.shape[1]
    devices = n_qi * group
    if hidden_count % (BLOCK * devices) == 0:
        parts_of = (2 * hidden_count, hidden_count)
    else:
        parts_of = (3 * hidden_count,)
    waves = tuple(
        (n_qi, group, -(-part // (BLOCK * devices)) * BLOCK, channels) for part in parts_of
    )
    tail_shape = (HEADS + ALIGN, channels)
    tail_steps = 1 + (group - 1).bit_length()
    half = keys // n_qi
    q_half = rows // n_kj
    sizes = (n_noise, n_qi, n_kj, rows, keys, share, parts_of)
    pack = max(1, LANES // keys)
    vmem = pl.BlockSpec(memory_space=pltpu.VMEM)
    dma = pltpu.SemaphoreType.DMA

    scratch = [
        pltpu.VMEM((rows, width), BF16),
        pltpu.VMEM((keys, width), BF16),
        pltpu.VMEM((keys, width), BF16),
        pltpu.VMEM((rows, width), BF16),
        pltpu.VMEM((1, channels), F32),
        pltpu.VMEM((channels, hidden_count), BF16),
        pltpu.VMEM((channels, hidden_count), BF16),
        pltpu.VMEM((hidden_count, channels), BF16),
        pltpu.VMEM((1, channels), F32),
        pltpu.VMEM((HEADS, channels), BF16),
        pltpu.VMEM((share, block_count, block_rows, channels), BF16),
        pltpu.VMEM((count, channels), F32),
        pltpu.VMEM((count, channels), BF16),
        pltpu.VMEM((channels, count), BF16),
        pltpu.VMEM((count, hidden_count), F32),
        pltpu.VMEM((count, hidden_count), F32),
        pltpu.VMEM((count, hidden_count), BF16),
        pltpu.VMEM((hidden_count, count), BF16),
        pltpu.VMEM((count, hidden_count), BF16),
        pltpu.VMEM((count, channels), F32),
        pltpu.VMEM((count, channels), BF16),
        pltpu.VMEM((count, 128), F32),
        pltpu.VMEM((share, HEADS, keys), F32),
        pltpu.VMEM((n_noise, HEADS // pack, share, pack * keys), BF16),
        pltpu.VMEM((HEADS, rows, keys), F32),
        pltpu.VMEM((HEADS, rows, keys), F32),
        pltpu.VMEM((n_kj, rows, 128), F32),
        pltpu.VMEM((n_noise, HEADS // pack, share, pack * keys), BF16),
        pltpu.VMEM((n_noise, HEADS // pack, share, pack * keys), BF16),
        pltpu.VMEM((HEADS // pack, share, pack * keys), F32),
        pltpu.VMEM((count, channels), F32),
        pltpu.VMEM((n_kj, q_half, width), BF16),
        pltpu.VMEM((n_kj, q_half, width), BF16),
        pltpu.VMEM((n_qi, half, 2 * width), BF16),
        pltpu.VMEM((half, 2 * width), BF16),
        pltpu.VMEM((1 + tail_steps, *tail_shape), F32),
        pltpu.VMEM((tail_steps, *tail_shape), F32),
        dma((11,)),
        dma((n_noise,)),
        dma((n_noise,)),
        dma((n_kj,)),
        dma((n_kj,)),
        dma((n_noise,)),
        dma((n_noise,)),
        dma((n_kj,)),
        dma((n_kj,)),
        dma((6,)),
        dma((len(waves) * group,)),
        dma((len(waves) * group,)),
        dma((len(waves) * group,)),
        dma((len(waves) * group,)),
        dma((len(waves),)),
        dma((len(waves),)),
        dma((tail_steps,)),
        dma((tail_steps,)),
    ]
    wave_scratch = [
        [pltpu.VMEM(wave[skip:], BF16) for wave in waves] for skip in (0, 1, 1, 1)
    ]
    scratch += sum(wave_scratch, [])

    def run(*refs):
        count = len(waves)
        outs = refs[16 : 16 + count]
        rest = refs[16 + count :]
        groups = [rest[len(rest) - (4 - i) * count : len(rest) - (3 - i) * count] for i in range(4)]
        kernel(sizes, *refs[:16], *rest[: len(rest) - 4 * count], outs, *groups)

    held = sum(
        math.prod(x.shape) * jnp.dtype(x.dtype).itemsize for x in scratch if x.memory_space == pltpu.VMEM
    )
    hbm = pl.BlockSpec(memory_space=pltpu.HBM)
    query_grad, key_grad, value_grad, pair_grad, tail, *weights = pl.pallas_call(
        run,
        out_shape=(
            jax.ShapeDtypeStruct((q_half, width), BF16),
            jax.ShapeDtypeStruct((half, width), BF16),
            jax.ShapeDtypeStruct((half, width), BF16),
            jax.ShapeDtypeStruct((count, channels), BF16),
            jax.ShapeDtypeStruct(tail_shape, F32),
            *(jax.ShapeDtypeStruct(wave, BF16) for wave in waves),
        ),
        in_specs=[hbm] * 11,
        out_specs=(vmem,) * (5 + len(waves)),
        scratch_shapes=scratch,
        compiler_params=pltpu.CompilerParams(
            collective_id=0, has_side_effects=True, vmem_limit_bytes=held + held // 8 + 4 * 1024 * 1024
        ),
        name="block_backward",
    )(
        *(
            pltpu.with_memory_space_constraint(x, pltpu.HBM)
            for x in (
                pair_rep,
                query_rows.reshape(rows, width),
                key_rows.reshape(keys, width),
                value_rows.reshape(keys, width),
                output_grad.reshape(rows, width),
                gain_first.reshape(1, channels),
                gate_weight,
                up_weight,
                down_weight,
                gain_second.reshape(1, channels),
                head_weight.T,
            )
        )
    )
    outputs = (query_grad, key_grad, value_grad, pair_grad)

    def finish_all(*refs):
        count = len(waves)
        finish(hidden_count, parts_of, group, *refs[:5], *refs[5 + count :], refs[5 : 5 + count])

    query_grad, key_grad, value_grad, pair_grad, gate_grad, up_grad, down_grad, head_grad, first_grad, second_grad = pl.pallas_call(
        finish_all,
        out_shape=tuple(jax.ShapeDtypeStruct(x.shape, x.dtype) for x in outputs)
        + (
            jax.ShapeDtypeStruct((channels, hidden_count), F32),
            jax.ShapeDtypeStruct((channels, hidden_count), F32),
            jax.ShapeDtypeStruct((hidden_count, channels), F32),
            jax.ShapeDtypeStruct((HEADS, channels), F32),
            jax.ShapeDtypeStruct((1, channels), F32),
            jax.ShapeDtypeStruct((1, channels), F32),
        ),
        in_specs=[vmem] * (5 + len(waves)),
        out_specs=(hbm,) * 10,
        scratch_shapes=[
            pltpu.VMEM((channels, hidden_count), F32),
            pltpu.VMEM((channels, hidden_count), F32),
            pltpu.VMEM((hidden_count, channels), F32),
            pltpu.VMEM((1, channels), F32),
            pltpu.VMEM((1, channels), F32),
            dma((10,)),
        ],
        compiler_params=pltpu.CompilerParams(vmem_limit_bytes=8 * 1024 * 1024),
        name="finish_weights",
    )(tail, *outputs, *weights)
    return (
        query_grad[None],
        key_grad[None],
        value_grad[None],
        pair_grad.reshape(1, 1, share, block_count, block_rows, channels),
        gate_grad,
        up_grad,
        down_grad,
        head_grad.T,
        first_grad.reshape(channels),
        second_grad.reshape(channels),
    )


def solution(mesh):
    mesh_shape = (mesh.shape["noise"], mesh.shape["qi"], mesh.shape["kj"])
    return jax.shard_map(
        functools.partial(local, mesh_shape),
        mesh=mesh,
        in_specs=(
            P("qi", None, "kj", None),
            P("noise", "qi", None),
            P("noise", None, "kj", None),
            P("noise", None, "kj", None),
            P("noise", "qi", None),
            P(),
            P(),
            P(),
            P(),
            P(),
            P(),
        ),
        out_specs=(
            P("noise", ("qi", "kj"), None),
            P("noise", ("qi", "kj"), None),
            P("noise", ("qi", "kj"), None),
            P("qi", "noise", None, None, "kj", None),
            P(),
            P(),
            P(),
            P(),
            P(),
            P(),
        ),
        check_vma=False,
    )
```

```python
import functools
import math

import jax
import jax.numpy as jnp
from jax import lax
from jax.experimental import pallas as pl
from jax.experimental.pallas import tpu as pltpu
from jax.sharding import PartitionSpec as P

HEADS = 16
HEAD_DIM = 48
ALIGN = 8
BLOCK = 16
LANES = 128

epsilon = 1e-05
F32 = jnp.float32
BF16 = jnp.bfloat16
MESH = pl.DeviceIdType.MESH


def dot(left, right, left_dim, right_dim):
    return lax.dot_general(
        left, right, (((left_dim,), (right_dim,)), ((), ())), preferred_element_type=F32
    )


def normalize(values):
    center = values - jnp.mean(values, axis=1, keepdims=True)
    inverse = lax.rsqrt(jnp.mean(center * center, axis=1, keepdims=True) + epsilon)
    return center * inverse, inverse


def norm_backward(normed_grad, normed, inverse):
    first_mean = jnp.mean(normed_grad, axis=1, keepdims=True)
    second_mean = jnp.mean(normed_grad * normed, axis=1, keepdims=True)
    return inverse * (normed_grad - first_mean - normed * second_mean)


def place(parts_of, row):
    wave = 0
    while row >= parts_of[wave]:
        row -= parts_of[wave]
        wave += 1
    return wave, row


def kernel(
    sizes,
    pair_hbm,
    q_hbm,
    k_hbm,
    v_hbm,
    g_hbm,
    gain_first_hbm,
    gate_hbm,
    up_hbm,
    down_hbm,
    gain_second_hbm,
    head_hbm,
    query_out,
    key_out,
    value_out,
    pair_out,
    tail_out,
    q_ref,
    k_ref,
    v_ref,
    g_ref,
    gain_first_ref,
    gate_ref,
    up_ref,
    down_ref,
    gain_second_ref,
    head_ref,
    cells,
    pre_normed,
    pre_low,
    pre_low_t,
    gate_coef,
    up_coef,
    hidden,
    hidden_t,
    up_low,
    post_normed,
    post_low,
    inverses,
    bias_rows,
    bias_send,
    bias_all,
    q_cols,
    g_cols,
    kv_send,
    kv_all,
    q_heads,
    g_heads,
    k_heads,
    score,
    attend_grad,
    score_low,
    attend_low,
    score_cat,
    grad_send,
    grad_recv,
    grad_sum,
    post_scaled,
    query_part,
    query_recv,
    kv_part,
    kv_recv,
    tail_part,
    tail_core,
    tail_sum,
    tail_recv,
    input_sems,
    bias_send_sem,
    bias_recv_sem,
    tile_send_sem,
    tile_recv_sem,
    grad_send_sem,
    grad_recv_sem,
    query_send_sem,
    query_recv_sem,
    kv_send_sem,
    kv_recv_sem,
    pair_sems,
    w_send_sem,
    w_recv_sem,
    all_send_sem,
    all_recv_sem,
    fwd_send_sem,
    fwd_recv_sem,
    tail_sems,
    tail_send_sem,
    tail_recv_sem,
    weight_out,
    w_part,
    w_core,
    w_sum,
    w_recv,
):
    n_noise, n_qi, n_kj, rows, keys, share, parts_of = sizes
    waves = len(parts_of)
    group = n_noise * n_kj
    cell_count = share * keys
    chunk = min(256, cell_count)
    scale = HEAD_DIM ** (-0.5)
    noise = lax.axis_index("noise")
    qi = lax.axis_index("qi")
    kj = lax.axis_index("kj")
    me = noise * n_kj + kj
    sibling = {"qi": 1 - qi}
    channels = cells.shape[-1]
    width = q_ref.shape[-1]
    half = keys // n_qi
    q_half = rows // n_kj
    own = HEADS // n_kj
    part = own * HEAD_DIM
    pack = min(own, max(1, LANES // keys))
    packed = own // pack

    def members(p):
        return [p + j * packed for j in range(pack)]

    def remote(src, dst, send, recv, device):
        return pltpu.make_async_remote_copy(
            src_ref=src, dst_ref=dst, send_sem=send, recv_sem=recv, device_id=device, device_id_type=MESH
        )

    def of_group(index):
        return {"noise": index // n_kj, "kj": lax.rem(index, n_kj)}

    def each(count, body):
        def step(i, carry):
            body(i)
            return carry

        lax.fori_loop(1, count, step, 0)

    forward_loads = [
        pltpu.make_async_copy(src, dst, input_sems.at[i])
        for i, (src, dst) in enumerate(
            (
                (pair_hbm.at[pl.ds(noise * share, share)], cells),
                (gain_first_hbm, gain_first_ref),
                (gate_hbm, gate_ref),
                (up_hbm, up_ref),
                (down_hbm, down_ref),
                (gain_second_hbm, gain_second_ref),
                (head_hbm, head_ref),
            )
        )
    ]
    attention_loads = [
        pltpu.make_async_copy(src, dst, input_sems.at[len(forward_loads) + i])
        for i, (src, dst) in enumerate(((q_hbm, q_ref), (k_hbm, k_ref), (g_hbm, g_ref), (v_hbm, v_ref)))
    ]
    for load in forward_loads:
        load.start()

    barrier = pltpu.get_barrier_semaphore()

    def greet(i):
        pl.semaphore_signal(
            barrier, inc=1, device_id=of_group(lax.rem(me + i, group)), device_id_type=MESH
        )

    each(group, greet)
    pl.semaphore_signal(barrier, inc=1, device_id=sibling, device_id_type=MESH)
    for load in attention_loads:
        load.start()
    for load in forward_loads:
        load.wait()

    gain_first = gain_first_ref[...]
    gain_second = gain_second_ref[...]
    head_t = head_ref[...]
    flat_cells = cells[...].reshape(cell_count, channels)
    for start in range(0, cell_count, chunk):
        at = slice(start, start + chunk)
        inputs = flat_cells[at].astype(F32)
        normed, inverse = normalize(inputs)
        lowered = (normed * gain_first).astype(BF16)
        gate_pre = dot(lowered, gate_ref[...], 1, 0)
        up_pre = dot(lowered, up_ref[...], 1, 0)
        sigmoid = jax.nn.sigmoid(gate_pre)
        silu = gate_pre * sigmoid
        low_hidden = (silu * up_pre).astype(BF16)
        updated = inputs + dot(low_hidden, down_ref[...], 1, 0)
        after, after_inverse = normalize(updated)
        after_low = (after * gain_second).astype(BF16)
        pre_normed[at] = normed
        pre_low[at] = lowered
        gate_coef[at] = up_pre * sigmoid * (1.0 + gate_pre * (1.0 - sigmoid))
        up_coef[at] = silu
        hidden[at] = low_hidden
        post_normed[at] = after
        post_low[at] = after_low
        inverses[at, 0:1] = inverse
        inverses[at, 1:2] = after_inverse
    for i in range(share):
        bias_rows[i] = dot(head_t, post_low[i * keys : (i + 1) * keys], 1, 1)
    for j in range(n_kj):
        for p in range(packed):
            bias_send[j, p] = jnp.concatenate([bias_rows[:, j * own + h, :] for h in members(p)], 1).astype(BF16)

    for load in attention_loads:
        load.wait()
    for j in range(n_kj):
        at = slice(j * part, (j + 1) * part)
        q_cols[j] = q_ref[:, at]
        g_cols[j] = g_ref[:, at]
        kv_send[j, 0] = k_ref[:, at]
        kv_send[j, 1] = v_ref[:, at]

    pl.semaphore_wait(barrier, group)

    def tile_copy(slot, peer):
        return remote(
            kv_send.at[peer], kv_all.at[slot], tile_send_sem.at[peer], tile_recv_sem.at[slot], {"kj": peer}
        )

    def bias_copy(slot, peer):
        return remote(
            bias_send.at[lax.rem(peer, n_kj)],
            bias_all.at[slot],
            bias_send_sem.at[peer],
            bias_recv_sem.at[slot],
            of_group(peer),
        )

    each(n_kj, lambda i: tile_copy(kj, lax.rem(kj + i, n_kj)).start())
    each(group, lambda i: bias_copy(me, lax.rem(me + i, group)).start())

    kv_all[kj] = kv_send[kj]
    bias_all[me] = bias_send[kj]
    lane = lax.broadcasted_iota(jnp.int32, (1, part), 1)

    def mask(h):
        inside = jnp.logical_and(lane >= h * HEAD_DIM, lane < (h + 1) * HEAD_DIM)
        return jnp.where(inside, 1.0, 0.0).astype(BF16)

    q_own = q_cols[kj]
    g_own = g_cols[kj]
    for h in range(own):
        at = slice(h * rows, (h + 1) * rows)
        q_heads[at] = q_own * mask(h)
        g_heads[at] = g_own * mask(h)
    hidden_t[...] = hidden[...].T
    pre_low_t[...] = pre_low[...].T
    for wave, count in enumerate(parts_of):
        if count < math.prod(w_part[wave].shape[:3]):
            w_part[wave][...] = jnp.zeros(w_part[wave].shape, BF16)

    def tile_wait(i):
        peer = lax.rem(kj + n_kj - i, n_kj)
        tile_copy(peer, peer).wait_recv()

    each(n_kj, tile_wait)
    k_own = kv_all[:, 0].reshape(n_kj * keys, part)
    v_own = kv_all[:, 1].reshape(n_kj * keys, part)
    score[...] = dot(q_heads[...], k_own, 1, 1) * scale
    attend_grad[...] = dot(g_heads[...], v_own, 1, 1)
    for h in range(own):
        k_heads[h * n_kj * keys : (h + 1) * n_kj * keys] = k_own * mask(h)

    def bias_wait(i):
        peer = lax.rem(me + group - i, group)
        bias_copy(peer, peer).wait_recv()

    each(group, bias_wait)

    for p in range(packed):
        blocks = [
            jnp.concatenate([bias_all[n * n_kj + j, p] for n in range(n_noise)], 0).astype(F32) for j in range(n_kj)
        ]
        grads = []
        for i, h in enumerate(members(p)):
            at = slice(h * rows, (h + 1) * rows)
            full = score[at] + jnp.concatenate([block[:, i * keys : (i + 1) * keys] for block in blocks], 1)
            expo = jnp.exp(full - jnp.max(full, axis=1, keepdims=True))
            attend = expo * (1.0 / jnp.sum(expo, axis=1, keepdims=True))
            weighed = attend_grad[at]
            score_grad = attend * (weighed - jnp.sum(attend * weighed, axis=1, keepdims=True))
            grads.append(score_grad)
            attend_low[at] = attend.astype(BF16)
            score_low[at] = score_grad.astype(BF16)
            score_cat[:, h * n_kj * keys : (h + 1) * n_kj * keys] = score_grad.astype(BF16)
        for j in range(n_kj):
            piece = jnp.concatenate([grad[:, j * keys : (j + 1) * keys] for grad in grads], 1).astype(BF16)
            for n in range(n_noise):
                grad_send[n * n_kj + j, p] = piece[n * share : (n + 1) * share]

    def grad_copy(slot, peer):
        return remote(
            grad_send.at[peer], grad_recv.at[slot], grad_send_sem.at[peer], grad_recv_sem.at[slot], of_group(peer)
        )

    each(group, lambda i: grad_copy(me, lax.rem(me + i, group)).start())

    query_all = (dot(score_cat[...], k_heads[...], 1, 0) * scale).astype(BF16)
    for j in range(n_kj):
        query_part[j] = query_all[j * q_half : (j + 1) * q_half]
    key_all = (dot(score_low[...], q_heads[...], 0, 0) * scale).astype(BF16)
    value_all = dot(attend_low[...], g_heads[...], 0, 0).astype(BF16)
    for j in range(n_kj):
        for i in range(n_qi):
            at = slice(j * keys + i * half, j * keys + (i + 1) * half)
            kv_part[i * n_kj + j, 0] = key_all[at]
            kv_part[i * n_kj + j, 1] = value_all[at]

    def query_copy(slot, peer):
        return remote(
            query_part.at[peer], query_recv.at[slot], query_send_sem.at[peer], query_recv_sem.at[slot], {"kj": peer}
        )

    def kv_copy(slot, peer):
        device = {"qi": peer // n_kj, "kj": lax.rem(peer, n_kj)}
        return remote(kv_part.at[peer], kv_recv.at[slot], kv_send_sem.at[peer], kv_recv_sem.at[slot], device)

    cell = qi * n_kj + kj
    each(n_kj, lambda i: query_copy(kj, lax.rem(kj + i, n_kj)).start())
    each(n_qi * n_kj, lambda i: kv_copy(cell, lax.rem(cell + i, n_qi * n_kj)).start())
    query_recv[kj] = query_part[kj]
    kv_recv[cell] = kv_part[cell]

    grad_recv[me] = grad_send[me]

    def grad_wait(i):
        peer = lax.rem(me + group - i, group)
        grad_copy(peer, peer).wait_recv()

    each(group, grad_wait)
    for j in range(n_kj):
        total = grad_recv[j].astype(F32)
        for n in range(1, n_noise):
            total += grad_recv[n * n_kj + j].astype(F32)
        grad_sum[j] = total

    head_part = jnp.zeros((HEADS, channels), F32)
    for i in range(share):
        at = slice(i * keys, (i + 1) * keys)
        grad_low = jnp.concatenate(
            [grad_sum[j, :, i, m * keys : (m + 1) * keys] for j in range(n_kj) for m in range(pack)], 0
        ).astype(BF16)
        post_scaled[at] = dot(grad_low, head_t, 0, 0)
        head_part += dot(grad_low, post_low[at], 1, 0)
    hidden_count = gate_ref.shape[1]
    tiles = hidden_count // channels

    def put(t, value):
        wave, first = place(parts_of, t * channels)
        block = w_part[wave].shape[2]
        count = channels // block
        owner = first // block
        w_part[wave][owner // group, owner % group : owner % group + count] = value.astype(BF16).reshape(
            count, block, channels
        )

    starts = range(0, cell_count, chunk)
    second_part = jnp.zeros((1, channels), F32)
    down_part = jnp.zeros((hidden_count, channels), F32)
    gate_part = jnp.zeros((channels, hidden_count), F32)
    for start in starts:
        at = slice(start, start + chunk)
        scaled = post_scaled[at]
        after = post_normed[at]
        second_part += jnp.sum(scaled * after, axis=0, keepdims=True)
        updated_grad = norm_backward(scaled * gain_second, after, inverses[at, 1:2])
        updated_low = updated_grad.astype(BF16)
        post_scaled[at] = updated_grad
        down_part += dot(hidden_t[:, at], updated_low, 1, 0)
        hidden_grad = dot(updated_low, down_ref[...], 1, 1)
        gate_low = (hidden_grad * gate_coef[at]).astype(BF16)
        up_low[at] = (hidden_grad * up_coef[at]).astype(BF16)
        gate_part += dot(pre_low_t[:, at], gate_low, 1, 0)
        hidden[at] = gate_low

    for t in range(tiles):
        at = slice(t * channels, (t + 1) * channels)
        put(t, down_part[at])
        put(tiles + t, gate_part[:, at])

    def core_copy(wave):
        return remote(
            w_part[wave].at[1 - qi], w_core[wave], pair_sems.at[2 * wave], pair_sems.at[2 * wave + 1], sibling
        )

    if waves > 1:
        core_copy(0).start()

    first_part = jnp.zeros((1, channels), F32)
    up_part = jnp.zeros((channels, hidden_count), F32)
    for start in starts:
        at = slice(start, start + chunk)
        up_part += dot(pre_low_t[:, at], up_low[at], 1, 0)
        pre_scaled = dot(hidden[at], gate_ref[...], 1, 1) + dot(up_low[at], up_ref[...], 1, 1)
        first_part += jnp.sum(pre_scaled * pre_normed[at], axis=0, keepdims=True)
        post_normed[at] = pre_scaled
    for t in range(tiles):
        put(2 * tiles + t, up_part[:, t * channels : (t + 1) * channels])
    core_copy(waves - 1).start()

    tail_part[0:HEADS] = head_part.astype(BF16)
    tail_part[HEADS:] = jnp.concatenate(
        (
            jnp.broadcast_to(first_part, (ALIGN // 2, channels)),
            jnp.broadcast_to(second_part, (ALIGN // 2, channels)),
        ),
        0,
    ).astype(BF16)
    owner = group // 2
    others = me != owner
    tail_core_copy = remote(tail_part, tail_core, tail_sems.at[0], tail_sems.at[1], sibling)
    tail_core_copy.start()

    def tail_copy(slot):
        return remote(tail_sum, tail_recv.at[slot], tail_sems.at[2], tail_recv_sem.at[slot], of_group(owner))

    def tail_back(peer):
        return remote(tail_out, tail_out, tail_send_sem.at[peer], tail_sems.at[3], of_group(peer))

    def w_copy(wave, slot, peer):
        return remote(
            w_sum[wave].at[peer],
            w_recv[wave].at[slot],
            w_send_sem.at[wave * group + peer],
            w_recv_sem.at[wave * group + slot],
            of_group(peer),
        )

    def all_copy(wave, slot, peer):
        at = weight_out[wave].at[qi, slot]
        return remote(
            at, at, all_send_sem.at[wave * group + peer], all_recv_sem.at[wave * group + slot], of_group(peer)
        )

    def fwd_copy(wave, core):
        at = weight_out[wave].at[core]
        return remote(at, at, fwd_send_sem.at[wave], fwd_recv_sem.at[wave], sibling)

    for wave in range(waves):
        core_copy(wave).wait_recv()
        w_sum[wave][...] = (w_part[wave][qi].astype(F32) + w_core[wave][...].astype(F32)).astype(BF16)
        each(group, lambda i: w_copy(wave, me, lax.rem(me + i, group)).start())
    tail_core_copy.wait_recv()
    tail_sum[...] = (tail_part[...].astype(F32) + tail_core[...].astype(F32)).astype(BF16)

    @pl.when(others)
    def _():
        tail_copy(me).start()

    for start in starts:
        at = slice(start, start + chunk)
        inputs_grad = norm_backward(post_normed[at] * gain_first, pre_normed[at], inverses[at, 0:1])
        pair_out[at] = (post_scaled[at] + inputs_grad).astype(BF16)

    def query_wait(i):
        peer = lax.rem(kj + n_kj - i, n_kj)
        query_copy(peer, peer).wait_recv()

    def kv_wait(i):
        peer = lax.rem(cell + n_qi * n_kj - i, n_qi * n_kj)
        kv_copy(peer, peer).wait_recv()

    each(n_kj, query_wait)
    each(n_qi * n_kj, kv_wait)
    for j in range(n_kj):
        at = slice(j * part, (j + 1) * part)
        query_out[:, at] = query_recv[j]
        for out, which in ((key_out, 0), (value_out, 1)):
            total = kv_recv[j, which].astype(F32)
            for i in range(1, n_qi):
                total += kv_recv[i * n_kj + j, which].astype(F32)
            out[:, at] = total.astype(BF16)

    for wave in range(waves):

        def w_add(i, total):
            peer = lax.rem(me + group - i, group)
            w_copy(wave, peer, peer).wait_recv()
            return total + w_recv[wave][peer].astype(F32)

        total = lax.fori_loop(1, group, w_add, w_sum[wave][me].astype(F32))
        weight_out[wave][qi, me] = (total * (1.0 / (rows * n_qi))).astype(BF16)
        each(group, lambda i: all_copy(wave, me, lax.rem(me + i, group)).start())

    @pl.when(jnp.logical_not(others))
    def _():
        def tail_add(i, total):
            peer = lax.rem(me + group - i, group)
            tail_copy(peer).wait_recv()
            return total + tail_recv[peer].astype(F32)

        total = lax.fori_loop(1, group, tail_add, tail_sum[...].astype(F32))
        tail_out[...] = (total * (1.0 / (rows * n_qi))).astype(BF16)
        each(group, lambda i: tail_back(lax.rem(me + i, group)).start())

    for wave in range(waves):

        def all_wait(i):
            peer = lax.rem(me + group - i, group)
            all_copy(wave, peer, peer).wait_recv()

        each(group, all_wait)
        fwd_copy(wave, qi).start()

    @pl.when(others)
    def _():
        tail_back(me).wait_recv()
        tail_copy(me).wait_send()

    @pl.when(jnp.logical_not(others))
    def _():
        each(group, lambda i: tail_back(lax.rem(me + i, group)).wait_send())

    for wave in range(waves):
        fwd_copy(wave, 1 - qi).wait_recv()
        fwd_copy(wave, qi).wait_send()

        def drain(i):
            peer = lax.rem(me + i, group)
            w_copy(wave, me, peer).wait_send()
            all_copy(wave, me, peer).wait_send()

        each(group, drain)
        core_copy(wave).wait_send()
    tail_core_copy.wait_send()

    def drain_group(i):
        peer = lax.rem(me + i, group)
        bias_copy(me, peer).wait_send()
        grad_copy(me, peer).wait_send()

    each(group, drain_group)

    def drain_kj(i):
        peer = lax.rem(kj + i, n_kj)
        tile_copy(kj, peer).wait_send()
        query_copy(kj, peer).wait_send()

    each(n_kj, drain_kj)
    each(n_qi * n_kj, lambda i: kv_copy(cell, lax.rem(cell + i, n_qi * n_kj)).wait_send())


def finish(
    hidden_count,
    parts_of,
    group,
    tail_ref,
    query_ref,
    key_ref,
    value_ref,
    pair_ref,
    query_out,
    key_out,
    value_out,
    pair_out,
    gate_out,
    up_out,
    down_out,
    head_out,
    first_out,
    second_out,
    gate_wide,
    up_wide,
    down_wide,
    head_wide,
    first_wide,
    second_wide,
    sems,
    weight_ref,
):
    copies = []

    def store(src, dst):
        copy = pltpu.make_async_copy(src, dst, sems.at[len(copies)])
        copy.start()
        copies.append(copy)

    store(pair_ref, pair_out)
    store(query_ref, query_out)
    store(key_ref, key_out)
    store(value_ref, value_out)
    channels = tail_ref.shape[1]
    tiles = hidden_count // channels

    def tile(t):
        wave, first = place(parts_of, t * channels)
        block = weight_ref[wave].shape[2]
        count = channels // block
        owner = first // block
        value = weight_ref[wave][owner // group, owner % group : owner % group + count]
        return value.astype(F32).reshape(channels, channels)

    for t in range(tiles):
        down_wide[t * channels : (t + 1) * channels] = tile(t)
    store(down_wide, down_out)
    for t in range(tiles):
        gate_wide[:, t * channels : (t + 1) * channels] = tile(tiles + t)
    store(gate_wide, gate_out)
    for t in range(tiles):
        up_wide[:, t * channels : (t + 1) * channels] = tile(2 * tiles + t)
    store(up_wide, up_out)
    tail = tail_ref[...].astype(F32)
    head_wide[...] = tail[0:HEADS]
    store(head_wide, head_out)
    first_wide[...] = tail[HEADS : HEADS + 1]
    second_wide[...] = tail[HEADS + ALIGN // 2 : HEADS + ALIGN // 2 + 1]
    store(first_wide, first_out)
    store(second_wide, second_out)
    for copy in copies:
        copy.wait()


def local(
    mesh_shape,
    pair_rep,
    query_rows,
    key_rows,
    value_rows,
    output_grad,
    gain_first,
    gate_weight,
    up_weight,
    down_weight,
    gain_second,
    head_weight,
):
    n_noise, n_qi, n_kj = mesh_shape
    rows, block_count, block_rows, channels = pair_rep.shape
    keys = block_count * block_rows
    width = query_rows.shape[2]
    share = rows // n_noise
    count = share * keys
    group = n_noise * n_kj
    hidden_count = gate_weight.shape[1]
    devices = n_qi * group
    if hidden_count % (BLOCK * devices) == 0:
        parts_of = (2 * hidden_count, hidden_count)
    else:
        parts_of = (3 * hidden_count,)
    waves = tuple(
        (n_qi, group, -(-part // (BLOCK * devices)) * BLOCK, channels) for part in parts_of
    )
    tail_shape = (HEADS + ALIGN, channels)
    half = keys // n_qi
    q_half = rows // n_kj
    sizes = (n_noise, n_qi, n_kj, rows, keys, share, parts_of)
    own = HEADS // n_kj
    part = own * HEAD_DIM
    pack = min(own, max(1, LANES // keys))
    vmem = pl.BlockSpec(memory_space=pltpu.VMEM)
    dma = pltpu.SemaphoreType.DMA

    scratch = [
        pltpu.VMEM((rows, width), BF16),
        pltpu.VMEM((keys, width), BF16),
        pltpu.VMEM((keys, width), BF16),
        pltpu.VMEM((rows, width), BF16),
        pltpu.VMEM((1, channels), F32),
        pltpu.VMEM((channels, hidden_count), BF16),
        pltpu.VMEM((channels, hidden_count), BF16),
        pltpu.VMEM((hidden_count, channels), BF16),
        pltpu.VMEM((1, channels), F32),
        pltpu.VMEM((HEADS, channels), BF16),
        pltpu.VMEM((share, block_count, block_rows, channels), BF16),
        pltpu.VMEM((count, channels), F32),
        pltpu.VMEM((count, channels), BF16),
        pltpu.VMEM((channels, count), BF16),
        pltpu.VMEM((count, hidden_count), F32),
        pltpu.VMEM((count, hidden_count), F32),
        pltpu.VMEM((count, hidden_count), BF16),
        pltpu.VMEM((hidden_count, count), BF16),
        pltpu.VMEM((count, hidden_count), BF16),
        pltpu.VMEM((count, channels), F32),
        pltpu.VMEM((count, channels), BF16),
        pltpu.VMEM((count, 128), F32),
        pltpu.VMEM((share, HEADS, keys), F32),
        pltpu.VMEM((n_kj, own // pack, share, pack * keys), BF16),
        pltpu.VMEM((group, own // pack, share, pack * keys), BF16),
        pltpu.VMEM((n_kj, rows, part), BF16),
        pltpu.VMEM((n_kj, rows, part), BF16),
        pltpu.VMEM((n_kj, 2, keys, part), BF16),
        pltpu.VMEM((n_kj, 2, keys, part), BF16),
        pltpu.VMEM((own * rows, part), BF16),
        pltpu.VMEM((own * rows, part), BF16),
        pltpu.VMEM((own * n_kj * keys, part), BF16),
        pltpu.VMEM((own * rows, n_kj * keys), F32),
        pltpu.VMEM((own * rows, n_kj * keys), F32),
        pltpu.VMEM((own * rows, n_kj * keys), BF16),
        pltpu.VMEM((own * rows, n_kj * keys), BF16),
        pltpu.VMEM((rows, own * n_kj * keys), BF16),
        pltpu.VMEM((group, own // pack, share, pack * keys), BF16),
        pltpu.VMEM((group, own // pack, share, pack * keys), BF16),
        pltpu.VMEM((n_kj, own // pack, share, pack * keys), F32),
        pltpu.VMEM((count, channels), F32),
        pltpu.VMEM((n_kj, q_half, part), BF16),
        pltpu.VMEM((n_kj, q_half, part), BF16),
        pltpu.VMEM((n_qi * n_kj, 2, half, part), BF16),
        pltpu.VMEM((n_qi * n_kj, 2, half, part), BF16),
        pltpu.VMEM(tail_shape, BF16),
        pltpu.VMEM(tail_shape, BF16),
        pltpu.VMEM(tail_shape, BF16),
        pltpu.VMEM((group, *tail_shape), BF16),
        dma((11,)),
        dma((group,)),
        dma((group,)),
        dma((n_kj,)),
        dma((n_kj,)),
        dma((group,)),
        dma((group,)),
        dma((n_kj,)),
        dma((n_kj,)),
        dma((n_qi * n_kj,)),
        dma((n_qi * n_kj,)),
        dma((2 * len(waves),)),
        dma((len(waves) * group,)),
        dma((len(waves) * group,)),
        dma((len(waves) * group,)),
        dma((len(waves) * group,)),
        dma((len(waves),)),
        dma((len(waves),)),
        dma((4,)),
        dma((group,)),
        dma((group,)),
    ]
    wave_scratch = [
        [pltpu.VMEM(wave[skip:], BF16) for wave in waves] for skip in (0, 1, 1, 1)
    ]
    scratch += sum(wave_scratch, [])

    def run(*refs):
        count = len(waves)
        outs = refs[16 : 16 + count]
        rest = refs[16 + count :]
        groups = [rest[len(rest) - (4 - i) * count : len(rest) - (3 - i) * count] for i in range(4)]
        kernel(sizes, *refs[:16], *rest[: len(rest) - 4 * count], outs, *groups)

    held = sum(
        math.prod(x.shape) * jnp.dtype(x.dtype).itemsize for x in scratch if x.memory_space == pltpu.VMEM
    )
    hbm = pl.BlockSpec(memory_space=pltpu.HBM)
    query_grad, key_grad, value_grad, pair_grad, tail, *weights = pl.pallas_call(
        run,
        out_shape=(
            jax.ShapeDtypeStruct((q_half, width), BF16),
            jax.ShapeDtypeStruct((half, width), BF16),
            jax.ShapeDtypeStruct((half, width), BF16),
            jax.ShapeDtypeStruct((count, channels), BF16),
            jax.ShapeDtypeStruct(tail_shape, BF16),
            *(jax.ShapeDtypeStruct(wave, BF16) for wave in waves),
        ),
        in_specs=[hbm] * 11,
        out_specs=(vmem,) * (5 + len(waves)),
        scratch_shapes=scratch,
        compiler_params=pltpu.CompilerParams(
            collective_id=0, has_side_effects=True, vmem_limit_bytes=held + held // 8 + 4 * 1024 * 1024
        ),
        name="block_backward",
    )(
        *(
            pltpu.with_memory_space_constraint(x, pltpu.HBM)
            for x in (
                pair_rep,
                query_rows.reshape(rows, width),
                key_rows.reshape(keys, width),
                value_rows.reshape(keys, width),
                output_grad.reshape(rows, width),
                gain_first.reshape(1, channels),
                gate_weight,
                up_weight,
                down_weight,
                gain_second.reshape(1, channels),
                head_weight.T,
            )
        )
    )
    outputs = (query_grad, key_grad, value_grad, pair_grad)

    def finish_all(*refs):
        count = len(waves)
        finish(hidden_count, parts_of, group, *refs[:5], *refs[5 + count :], refs[5 : 5 + count])

    query_grad, key_grad, value_grad, pair_grad, gate_grad, up_grad, down_grad, head_grad, first_grad, second_grad = pl.pallas_call(
        finish_all,
        out_shape=tuple(jax.ShapeDtypeStruct(x.shape, x.dtype) for x in outputs)
        + (
            jax.ShapeDtypeStruct((channels, hidden_count), F32),
            jax.ShapeDtypeStruct((channels, hidden_count), F32),
            jax.ShapeDtypeStruct((hidden_count, channels), F32),
            jax.ShapeDtypeStruct((HEADS, channels), F32),
            jax.ShapeDtypeStruct((1, channels), F32),
            jax.ShapeDtypeStruct((1, channels), F32),
        ),
        in_specs=[vmem] * (5 + len(waves)),
        out_specs=(hbm,) * 10,
        scratch_shapes=[
            pltpu.VMEM((channels, hidden_count), F32),
            pltpu.VMEM((channels, hidden_count), F32),
            pltpu.VMEM((hidden_count, channels), F32),
            pltpu.VMEM((HEADS, channels), F32),
            pltpu.VMEM((1, channels), F32),
            pltpu.VMEM((1, channels), F32),
            dma((10,)),
        ],
        compiler_params=pltpu.CompilerParams(vmem_limit_bytes=8 * 1024 * 1024),
        name="finish_weights",
    )(tail, *outputs, *weights)
    return (
        query_grad[None],
        key_grad[None],
        value_grad[None],
        pair_grad.reshape(1, 1, share, block_count, block_rows, channels),
        gate_grad,
        up_grad,
        down_grad,
        head_grad.T,
        first_grad.reshape(channels),
        second_grad.reshape(channels),
    )


def solution(mesh):
    mesh_shape = (mesh.shape["noise"], mesh.shape["qi"], mesh.shape["kj"])
    return jax.shard_map(
        functools.partial(local, mesh_shape),
        mesh=mesh,
        in_specs=(
            P("qi", None, "kj", None),
            P("noise", "qi", None),
            P("noise", None, "kj", None),
            P("noise", None, "kj", None),
            P("noise", "qi", None),
            P(),
            P(),
            P(),
            P(),
            P(),
            P(),
        ),
        out_specs=(
            P("noise", ("qi", "kj"), None),
            P("noise", ("qi", "kj"), None),
            P("noise", ("qi", "kj"), None),
            P("qi", "noise", None, None, "kj", None),
            P(),
            P(),
            P(),
            P(),
            P(),
            P(),
        ),
        check_vma=False,
    )
```

```python
import functools
import math

import jax
import jax.numpy as jnp
from jax import lax
from jax.experimental import pallas as pl
from jax.experimental.pallas import tpu as pltpu
from jax.sharding import PartitionSpec as P

HEADS = 16
HEAD_DIM = 48
ALIGN = 8
BLOCK = 16
LANES = 128

epsilon = 1e-05
F32 = jnp.float32
BF16 = jnp.bfloat16
MESH = pl.DeviceIdType.MESH


def dot(left, right, left_dim, right_dim):
    return lax.dot_general(
        left, right, (((left_dim,), (right_dim,)), ((), ())), preferred_element_type=F32
    )


def normalize(values):
    center = values - jnp.mean(values, axis=1, keepdims=True)
    inverse = lax.rsqrt(jnp.mean(center * center, axis=1, keepdims=True) + epsilon)
    return center * inverse, inverse


def norm_backward(normed_grad, normed, inverse):
    first_mean = jnp.mean(normed_grad, axis=1, keepdims=True)
    second_mean = jnp.mean(normed_grad * normed, axis=1, keepdims=True)
    return inverse * (normed_grad - first_mean - normed * second_mean)


def place(parts_of, row):
    wave = 0
    while row >= parts_of[wave]:
        row -= parts_of[wave]
        wave += 1
    return wave, row


def kernel(
    sizes,
    pair_hbm,
    q_hbm,
    k_hbm,
    v_hbm,
    g_hbm,
    gain_first_hbm,
    gate_hbm,
    up_hbm,
    down_hbm,
    gain_second_hbm,
    head_hbm,
    query_out,
    key_out,
    value_out,
    pair_out,
    tail_out,
    q_ref,
    k_ref,
    v_ref,
    g_ref,
    gain_first_ref,
    gate_ref,
    up_ref,
    down_ref,
    gain_second_ref,
    head_ref,
    cells,
    pre_normed,
    pre_low,
    pre_low_t,
    gate_coef,
    up_coef,
    hidden,
    hidden_t,
    up_low,
    post_normed,
    post_low,
    inverses,
    bias_rows,
    bias_send,
    bias_all,
    q_cols,
    g_cols,
    kv_send,
    kv_all,
    q_heads,
    g_heads,
    k_heads,
    score,
    attend_grad,
    score_low,
    attend_low,
    score_cat,
    grad_send,
    grad_recv,
    grad_sum,
    post_scaled,
    query_part,
    query_recv,
    kv_part,
    kv_recv,
    tail_part,
    tail_core,
    tail_sum,
    tail_recv,
    input_sems,
    bias_send_sem,
    bias_recv_sem,
    tile_send_sem,
    tile_recv_sem,
    grad_send_sem,
    grad_recv_sem,
    query_send_sem,
    query_recv_sem,
    kv_send_sem,
    kv_recv_sem,
    pair_sems,
    w_send_sem,
    w_recv_sem,
    all_send_sem,
    all_recv_sem,
    fwd_send_sem,
    fwd_recv_sem,
    tail_sems,
    tail_send_sem,
    tail_recv_sem,
    weight_out,
    w_part,
    w_core,
    w_sum,
    w_recv,
):
    n_noise, n_qi, n_kj, rows, keys, share, parts_of = sizes
    waves = len(parts_of)
    group = n_noise * n_kj
    cell_count = share * keys
    chunk = min(256, cell_count)
    scale = HEAD_DIM ** (-0.5)
    noise = lax.axis_index("noise")
    qi = lax.axis_index("qi")
    kj = lax.axis_index("kj")
    me = noise * n_kj + kj
    power = group & (group - 1) == 0
    sibling = {"qi": 1 - qi}
    channels = cells.shape[-1]
    width = q_ref.shape[-1]
    half = keys // n_qi
    q_half = rows // n_kj
    own = HEADS // n_kj
    part = own * HEAD_DIM
    pack = min(own, max(1, LANES // keys))
    packed = own // pack

    def members(p):
        return [p + j * packed for j in range(pack)]

    def remote(src, dst, send, recv, device):
        return pltpu.make_async_remote_copy(
            src_ref=src, dst_ref=dst, send_sem=send, recv_sem=recv, device_id=device, device_id_type=MESH
        )

    def of_group(index):
        return {"noise": index // n_kj, "kj": lax.rem(index, n_kj)}

    def far(i):
        return lax.bitwise_xor(me, group - i) if power else lax.rem(me + i, group)

    def near(i):
        return lax.bitwise_xor(me, i) if power else lax.rem(me + group - i, group)

    def each(count, body):
        def step(i, carry):
            body(i)
            return carry

        lax.fori_loop(1, count, step, 0)

    forward_loads = [
        pltpu.make_async_copy(src, dst, input_sems.at[i])
        for i, (src, dst) in enumerate(
            (
                (pair_hbm.at[pl.ds(noise * share, share)], cells),
                (gain_first_hbm, gain_first_ref),
                (gate_hbm, gate_ref),
                (up_hbm, up_ref),
                (down_hbm, down_ref),
                (gain_second_hbm, gain_second_ref),
                (head_hbm, head_ref),
            )
        )
    ]
    attention_loads = [
        pltpu.make_async_copy(src, dst, input_sems.at[len(forward_loads) + i])
        for i, (src, dst) in enumerate(((q_hbm, q_ref), (k_hbm, k_ref), (g_hbm, g_ref), (v_hbm, v_ref)))
    ]
    for load in forward_loads:
        load.start()

    barrier = pltpu.get_barrier_semaphore()

    def greet(i):
        pl.semaphore_signal(
            barrier, inc=1, device_id=of_group(far(i)), device_id_type=MESH
        )

    each(group, greet)
    pl.semaphore_signal(barrier, inc=1, device_id=sibling, device_id_type=MESH)
    for load in attention_loads:
        load.start()
    for load in forward_loads:
        load.wait()

    gain_first = gain_first_ref[...]
    gain_second = gain_second_ref[...]
    head_t = head_ref[...]
    flat_cells = cells[...].reshape(cell_count, channels)
    for start in range(0, cell_count, chunk):
        at = slice(start, start + chunk)
        inputs = flat_cells[at].astype(F32)
        normed, inverse = normalize(inputs)
        lowered = (normed * gain_first).astype(BF16)
        gate_pre = dot(lowered, gate_ref[...], 1, 0)
        up_pre = dot(lowered, up_ref[...], 1, 0)
        sigmoid = jax.nn.sigmoid(gate_pre)
        silu = gate_pre * sigmoid
        low_hidden = (silu * up_pre).astype(BF16)
        updated = inputs + dot(low_hidden, down_ref[...], 1, 0)
        after, after_inverse = normalize(updated)
        after_low = (after * gain_second).astype(BF16)
        pre_normed[at] = normed
        pre_low[at] = lowered
        gate_coef[at] = up_pre * sigmoid * (1.0 + gate_pre * (1.0 - sigmoid))
        up_coef[at] = silu
        hidden[at] = low_hidden
        post_normed[at] = after
        post_low[at] = after_low
        inverses[at, 0:1] = inverse
        inverses[at, 1:2] = after_inverse
    for i in range(share):
        bias_rows[i] = dot(head_t, post_low[i * keys : (i + 1) * keys], 1, 1)
    for j in range(n_kj):
        for p in range(packed):
            bias_send[j, p] = jnp.concatenate([bias_rows[:, j * own + h, :] for h in members(p)], 1).astype(BF16)

    for load in attention_loads:
        load.wait()
    for j in range(n_kj):
        at = slice(j * part, (j + 1) * part)
        q_cols[j] = q_ref[:, at]
        g_cols[j] = g_ref[:, at]
        kv_send[j, 0] = k_ref[:, at]
        kv_send[j, 1] = v_ref[:, at]

    pl.semaphore_wait(barrier, group)

    def tile_copy(slot, peer):
        return remote(
            kv_send.at[peer], kv_all.at[slot], tile_send_sem.at[peer], tile_recv_sem.at[slot], {"kj": peer}
        )

    def bias_copy(slot, peer):
        return remote(
            bias_send.at[lax.rem(peer, n_kj)],
            bias_all.at[slot],
            bias_send_sem.at[peer],
            bias_recv_sem.at[slot],
            of_group(peer),
        )

    each(n_kj, lambda i: tile_copy(kj, lax.rem(kj + i, n_kj)).start())
    each(group, lambda i: bias_copy(me, far(i)).start())

    kv_all[kj] = kv_send[kj]
    bias_all[me] = bias_send[kj]
    lane = lax.broadcasted_iota(jnp.int32, (1, part), 1)

    def mask(h):
        inside = jnp.logical_and(lane >= h * HEAD_DIM, lane < (h + 1) * HEAD_DIM)
        return jnp.where(inside, 1.0, 0.0).astype(BF16)

    q_own = q_cols[kj]
    g_own = g_cols[kj]
    for h in range(own):
        at = slice(h * rows, (h + 1) * rows)
        q_heads[at] = q_own * mask(h)
        g_heads[at] = g_own * mask(h)
    hidden_t[...] = hidden[...].T
    pre_low_t[...] = pre_low[...].T
    for wave, count in enumerate(parts_of):
        if count < math.prod(w_part[wave].shape[:3]):
            w_part[wave][...] = jnp.zeros(w_part[wave].shape, BF16)

    def tile_wait(i):
        peer = lax.rem(kj + n_kj - i, n_kj)
        tile_copy(peer, peer).wait_recv()

    each(n_kj, tile_wait)
    k_own = kv_all[:, 0].reshape(n_kj * keys, part)
    v_own = kv_all[:, 1].reshape(n_kj * keys, part)
    score[...] = dot(q_heads[...], k_own, 1, 1) * scale
    attend_grad[...] = dot(g_heads[...], v_own, 1, 1)
    for h in range(own):
        k_heads[h * n_kj * keys : (h + 1) * n_kj * keys] = k_own * mask(h)

    def bias_wait(i):
        peer = near(i)
        bias_copy(peer, peer).wait_recv()

    each(group, bias_wait)

    for p in range(packed):
        blocks = [
            jnp.concatenate([bias_all[n * n_kj + j, p] for n in range(n_noise)], 0).astype(F32) for j in range(n_kj)
        ]
        grads = []
        for i, h in enumerate(members(p)):
            at = slice(h * rows, (h + 1) * rows)
            full = score[at] + jnp.concatenate([block[:, i * keys : (i + 1) * keys] for block in blocks], 1)
            expo = jnp.exp(full - jnp.max(full, axis=1, keepdims=True))
            attend = expo * (1.0 / jnp.sum(expo, axis=1, keepdims=True))
            weighed = attend_grad[at]
            score_grad = attend * (weighed - jnp.sum(attend * weighed, axis=1, keepdims=True))
            grads.append(score_grad)
            attend_low[at] = attend.astype(BF16)
            score_low[at] = score_grad.astype(BF16)
            score_cat[:, h * n_kj * keys : (h + 1) * n_kj * keys] = score_grad.astype(BF16)
        for j in range(n_kj):
            piece = jnp.concatenate([grad[:, j * keys : (j + 1) * keys] for grad in grads], 1).astype(BF16)
            for n in range(n_noise):
                grad_send[n * n_kj + j, p] = piece[n * share : (n + 1) * share]

    def grad_copy(slot, peer):
        return remote(
            grad_send.at[peer], grad_recv.at[slot], grad_send_sem.at[peer], grad_recv_sem.at[slot], of_group(peer)
        )

    each(group, lambda i: grad_copy(me, far(i)).start())

    query_all = (dot(score_cat[...], k_heads[...], 1, 0) * scale).astype(BF16)
    for j in range(n_kj):
        query_part[j] = query_all[j * q_half : (j + 1) * q_half]
    key_all = (dot(score_low[...], q_heads[...], 0, 0) * scale).astype(BF16)
    value_all = dot(attend_low[...], g_heads[...], 0, 0).astype(BF16)
    for j in range(n_kj):
        for i in range(n_qi):
            at = slice(j * keys + i * half, j * keys + (i + 1) * half)
            kv_part[i * n_kj + j, 0] = key_all[at]
            kv_part[i * n_kj + j, 1] = value_all[at]

    def query_copy(slot, peer):
        return remote(
            query_part.at[peer], query_recv.at[slot], query_send_sem.at[peer], query_recv_sem.at[slot], {"kj": peer}
        )

    def kv_copy(slot, peer):
        device = {"qi": peer // n_kj, "kj": lax.rem(peer, n_kj)}
        return remote(kv_part.at[peer], kv_recv.at[slot], kv_send_sem.at[peer], kv_recv_sem.at[slot], device)

    cell = qi * n_kj + kj
    each(n_kj, lambda i: query_copy(kj, lax.rem(kj + i, n_kj)).start())
    each(n_qi * n_kj, lambda i: kv_copy(cell, lax.rem(cell + i, n_qi * n_kj)).start())
    query_recv[kj] = query_part[kj]
    kv_recv[cell] = kv_part[cell]

    grad_recv[me] = grad_send[me]

    def grad_wait(i):
        peer = near(i)
        grad_copy(peer, peer).wait_recv()

    each(group, grad_wait)
    for j in range(n_kj):
        total = grad_recv[j].astype(F32)
        for n in range(1, n_noise):
            total += grad_recv[n * n_kj + j].astype(F32)
        grad_sum[j] = total

    head_part = jnp.zeros((HEADS, channels), F32)
    for i in range(share):
        at = slice(i * keys, (i + 1) * keys)
        grad_low = jnp.concatenate(
            [grad_sum[j, :, i, m * keys : (m + 1) * keys] for j in range(n_kj) for m in range(pack)], 0
        ).astype(BF16)
        post_scaled[at] = dot(grad_low, head_t, 0, 0)
        head_part += dot(grad_low, post_low[at], 1, 0)
    hidden_count = gate_ref.shape[1]
    tiles = hidden_count // channels

    def put(t, value):
        wave, first = place(parts_of, t * channels)
        block = w_part[wave].shape[2]
        count = channels // block
        owner = first // block
        w_part[wave][owner // group, owner % group : owner % group + count] = value.astype(BF16).reshape(
            count, block, channels
        )

    starts = range(0, cell_count, chunk)
    second_part = jnp.zeros((1, channels), F32)
    down_part = jnp.zeros((hidden_count, channels), F32)
    gate_part = jnp.zeros((channels, hidden_count), F32)
    for start in starts:
        at = slice(start, start + chunk)
        scaled = post_scaled[at]
        after = post_normed[at]
        second_part += jnp.sum(scaled * after, axis=0, keepdims=True)
        updated_grad = norm_backward(scaled * gain_second, after, inverses[at, 1:2])
        updated_low = updated_grad.astype(BF16)
        post_scaled[at] = updated_grad
        down_part += dot(hidden_t[:, at], updated_low, 1, 0)
        hidden_grad = dot(updated_low, down_ref[...], 1, 1)
        gate_low = (hidden_grad * gate_coef[at]).astype(BF16)
        up_low[at] = (hidden_grad * up_coef[at]).astype(BF16)
        gate_part += dot(pre_low_t[:, at], gate_low, 1, 0)
        hidden[at] = gate_low

    for t in range(tiles):
        at = slice(t * channels, (t + 1) * channels)
        put(t, down_part[at])
        put(tiles + t, gate_part[:, at])

    def core_copy(wave):
        return remote(
            w_part[wave].at[1 - qi], w_core[wave], pair_sems.at[2 * wave], pair_sems.at[2 * wave + 1], sibling
        )

    if waves > 1:
        core_copy(0).start()

    first_part = jnp.zeros((1, channels), F32)
    up_part = jnp.zeros((channels, hidden_count), F32)
    for start in starts:
        at = slice(start, start + chunk)
        up_part += dot(pre_low_t[:, at], up_low[at], 1, 0)
        pre_scaled = dot(hidden[at], gate_ref[...], 1, 1) + dot(up_low[at], up_ref[...], 1, 1)
        first_part += jnp.sum(pre_scaled * pre_normed[at], axis=0, keepdims=True)
        post_normed[at] = pre_scaled
    for t in range(tiles):
        put(2 * tiles + t, up_part[:, t * channels : (t + 1) * channels])
    core_copy(waves - 1).start()

    tail_part[0:HEADS] = head_part.astype(BF16)
    tail_part[HEADS:] = jnp.concatenate(
        (
            jnp.broadcast_to(first_part, (ALIGN // 2, channels)),
            jnp.broadcast_to(second_part, (ALIGN // 2, channels)),
        ),
        0,
    ).astype(BF16)
    owner = group // 2
    others = me != owner
    tail_core_copy = remote(tail_part, tail_core, tail_sems.at[0], tail_sems.at[1], sibling)
    tail_core_copy.start()

    def tail_copy(slot):
        return remote(tail_sum, tail_recv.at[slot], tail_sems.at[2], tail_recv_sem.at[slot], of_group(owner))

    def tail_back(peer):
        return remote(tail_out, tail_out, tail_send_sem.at[peer], tail_sems.at[3], of_group(peer))

    def w_copy(wave, slot, peer):
        return remote(
            w_sum[wave].at[peer],
            w_recv[wave].at[slot],
            w_send_sem.at[wave * group + peer],
            w_recv_sem.at[wave * group + slot],
            of_group(peer),
        )

    def all_copy(wave, slot, peer):
        at = weight_out[wave].at[qi, slot]
        return remote(
            at, at, all_send_sem.at[wave * group + peer], all_recv_sem.at[wave * group + slot], of_group(peer)
        )

    def fwd_copy(wave, core):
        at = weight_out[wave].at[core]
        return remote(at, at, fwd_send_sem.at[wave], fwd_recv_sem.at[wave], sibling)

    for wave in range(waves):
        core_copy(wave).wait_recv()
        w_sum[wave][...] = (w_part[wave][qi].astype(F32) + w_core[wave][...].astype(F32)).astype(BF16)
        each(group, lambda i: w_copy(wave, me, far(i)).start())
    tail_core_copy.wait_recv()
    tail_sum[...] = (tail_part[...].astype(F32) + tail_core[...].astype(F32)).astype(BF16)

    @pl.when(others)
    def _():
        tail_copy(me).start()

    for start in starts:
        at = slice(start, start + chunk)
        inputs_grad = norm_backward(post_normed[at] * gain_first, pre_normed[at], inverses[at, 0:1])
        pair_out[at] = (post_scaled[at] + inputs_grad).astype(BF16)

    def query_wait(i):
        peer = lax.rem(kj + n_kj - i, n_kj)
        query_copy(peer, peer).wait_recv()

    def kv_wait(i):
        peer = lax.rem(cell + n_qi * n_kj - i, n_qi * n_kj)
        kv_copy(peer, peer).wait_recv()

    each(n_kj, query_wait)
    each(n_qi * n_kj, kv_wait)
    for j in range(n_kj):
        at = slice(j * part, (j + 1) * part)
        query_out[:, at] = query_recv[j]
        for out, which in ((key_out, 0), (value_out, 1)):
            total = kv_recv[j, which].astype(F32)
            for i in range(1, n_qi):
                total += kv_recv[i * n_kj + j, which].astype(F32)
            out[:, at] = total.astype(BF16)

    for wave in range(waves):

        def w_add(i, total):
            peer = near(i)
            w_copy(wave, peer, peer).wait_recv()
            return total + w_recv[wave][peer].astype(F32)

        total = lax.fori_loop(1, group, w_add, w_sum[wave][me].astype(F32))
        weight_out[wave][qi, me] = (total * (1.0 / (rows * n_qi))).astype(BF16)
        each(group, lambda i: all_copy(wave, me, far(i)).start())

    @pl.when(jnp.logical_not(others))
    def _():
        def tail_add(i, total):
            peer = near(i)
            tail_copy(peer).wait_recv()
            return total + tail_recv[peer].astype(F32)

        total = lax.fori_loop(1, group, tail_add, tail_sum[...].astype(F32))
        tail_out[...] = (total * (1.0 / (rows * n_qi))).astype(BF16)
        each(group, lambda i: tail_back(far(i)).start())

    for wave in range(waves):

        def all_wait(i):
            peer = near(i)
            all_copy(wave, peer, peer).wait_recv()

        each(group, all_wait)
        fwd_copy(wave, qi).start()

    @pl.when(others)
    def _():
        tail_back(me).wait_recv()
        tail_copy(me).wait_send()

    @pl.when(jnp.logical_not(others))
    def _():
        each(group, lambda i: tail_back(far(i)).wait_send())

    for wave in range(waves):
        fwd_copy(wave, 1 - qi).wait_recv()
        fwd_copy(wave, qi).wait_send()

        def drain(i):
            peer = far(i)
            w_copy(wave, me, peer).wait_send()
            all_copy(wave, me, peer).wait_send()

        each(group, drain)
        core_copy(wave).wait_send()
    tail_core_copy.wait_send()

    def drain_group(i):
        peer = far(i)
        bias_copy(me, peer).wait_send()
        grad_copy(me, peer).wait_send()

    each(group, drain_group)

    def drain_kj(i):
        peer = lax.rem(kj + i, n_kj)
        tile_copy(kj, peer).wait_send()
        query_copy(kj, peer).wait_send()

    each(n_kj, drain_kj)
    each(n_qi * n_kj, lambda i: kv_copy(cell, lax.rem(cell + i, n_qi * n_kj)).wait_send())


def finish(
    hidden_count,
    parts_of,
    group,
    tail_ref,
    query_ref,
    key_ref,
    value_ref,
    pair_ref,
    query_out,
    key_out,
    value_out,
    pair_out,
    gate_out,
    up_out,
    down_out,
    head_out,
    first_out,
    second_out,
    gate_wide,
    up_wide,
    down_wide,
    head_wide,
    first_wide,
    second_wide,
    sems,
    weight_ref,
):
    copies = []

    def store(src, dst):
        copy = pltpu.make_async_copy(src, dst, sems.at[len(copies)])
        copy.start()
        copies.append(copy)

    store(pair_ref, pair_out)
    store(query_ref, query_out)
    store(key_ref, key_out)
    store(value_ref, value_out)
    channels = tail_ref.shape[1]
    tiles = hidden_count // channels

    def tile(t):
        wave, first = place(parts_of, t * channels)
        block = weight_ref[wave].shape[2]
        count = channels // block
        owner = first // block
        value = weight_ref[wave][owner // group, owner % group : owner % group + count]
        return value.astype(F32).reshape(channels, channels)

    for t in range(tiles):
        down_wide[t * channels : (t + 1) * channels] = tile(t)
    store(down_wide, down_out)
    for t in range(tiles):
        gate_wide[:, t * channels : (t + 1) * channels] = tile(tiles + t)
    store(gate_wide, gate_out)
    for t in range(tiles):
        up_wide[:, t * channels : (t + 1) * channels] = tile(2 * tiles + t)
    store(up_wide, up_out)
    tail = tail_ref[...].astype(F32)
    head_wide[...] = tail[0:HEADS]
    store(head_wide, head_out)
    first_wide[...] = tail[HEADS : HEADS + 1]
    second_wide[...] = tail[HEADS + ALIGN // 2 : HEADS + ALIGN // 2 + 1]
    store(first_wide, first_out)
    store(second_wide, second_out)
    for copy in copies:
        copy.wait()


def local(
    mesh_shape,
    pair_rep,
    query_rows,
    key_rows,
    value_rows,
    output_grad,
    gain_first,
    gate_weight,
    up_weight,
    down_weight,
    gain_second,
    head_weight,
):
    n_noise, n_qi, n_kj = mesh_shape
    rows, block_count, block_rows, channels = pair_rep.shape
    keys = block_count * block_rows
    width = query_rows.shape[2]
    share = rows // n_noise
    count = share * keys
    group = n_noise * n_kj
    hidden_count = gate_weight.shape[1]
    devices = n_qi * group
    if hidden_count % (BLOCK * devices) == 0:
        parts_of = (2 * hidden_count, hidden_count)
    else:
        parts_of = (3 * hidden_count,)
    waves = tuple(
        (n_qi, group, -(-part // (BLOCK * devices)) * BLOCK, channels) for part in parts_of
    )
    tail_shape = (HEADS + ALIGN, channels)
    half = keys // n_qi
    q_half = rows // n_kj
    sizes = (n_noise, n_qi, n_kj, rows, keys, share, parts_of)
    own = HEADS // n_kj
    part = own * HEAD_DIM
    pack = min(own, max(1, LANES // keys))
    vmem = pl.BlockSpec(memory_space=pltpu.VMEM)
    dma = pltpu.SemaphoreType.DMA

    scratch = [
        pltpu.VMEM((rows, width), BF16),
        pltpu.VMEM((keys, width), BF16),
        pltpu.VMEM((keys, width), BF16),
        pltpu.VMEM((rows, width), BF16),
        pltpu.VMEM((1, channels), F32),
        pltpu.VMEM((channels, hidden_count), BF16),
        pltpu.VMEM((channels, hidden_count), BF16),
        pltpu.VMEM((hidden_count, channels), BF16),
        pltpu.VMEM((1, channels), F32),
        pltpu.VMEM((HEADS, channels), BF16),
        pltpu.VMEM((share, block_count, block_rows, channels), BF16),
        pltpu.VMEM((count, channels), F32),
        pltpu.VMEM((count, channels), BF16),
        pltpu.VMEM((channels, count), BF16),
        pltpu.VMEM((count, hidden_count), F32),
        pltpu.VMEM((count, hidden_count), F32),
        pltpu.VMEM((count, hidden_count), BF16),
        pltpu.VMEM((hidden_count, count), BF16),
        pltpu.VMEM((count, hidden_count), BF16),
        pltpu.VMEM((count, channels), F32),
        pltpu.VMEM((count, channels), BF16),
        pltpu.VMEM((count, 128), F32),
        pltpu.VMEM((share, HEADS, keys), F32),
        pltpu.VMEM((n_kj, own // pack, share, pack * keys), BF16),
        pltpu.VMEM((group, own // pack, share, pack * keys), BF16),
        pltpu.VMEM((n_kj, rows, part), BF16),
        pltpu.VMEM((n_kj, rows, part), BF16),
        pltpu.VMEM((n_kj, 2, keys, part), BF16),
        pltpu.VMEM((n_kj, 2, keys, part), BF16),
        pltpu.VMEM((own * rows, part), BF16),
        pltpu.VMEM((own * rows, part), BF16),
        pltpu.VMEM((own * n_kj * keys, part), BF16),
        pltpu.VMEM((own * rows, n_kj * keys), F32),
        pltpu.VMEM((own * rows, n_kj * keys), F32),
        pltpu.VMEM((own * rows, n_kj * keys), BF16),
        pltpu.VMEM((own * rows, n_kj * keys), BF16),
        pltpu.VMEM((rows, own * n_kj * keys), BF16),
        pltpu.VMEM((group, own // pack, share, pack * keys), BF16),
        pltpu.VMEM((group, own // pack, share, pack * keys), BF16),
        pltpu.VMEM((n_kj, own // pack, share, pack * keys), F32),
        pltpu.VMEM((count, channels), F32),
        pltpu.VMEM((n_kj, q_half, part), BF16),
        pltpu.VMEM((n_kj, q_half, part), BF16),
        pltpu.VMEM((n_qi * n_kj, 2, half, part), BF16),
        pltpu.VMEM((n_qi * n_kj, 2, half, part), BF16),
        pltpu.VMEM(tail_shape, BF16),
        pltpu.VMEM(tail_shape, BF16),
        pltpu.VMEM(tail_shape, BF16),
        pltpu.VMEM((group, *tail_shape), BF16),
        dma((11,)),
        dma((group,)),
        dma((group,)),
        dma((n_kj,)),
        dma((n_kj,)),
        dma((group,)),
        dma((group,)),
        dma((n_kj,)),
        dma((n_kj,)),
        dma((n_qi * n_kj,)),
        dma((n_qi * n_kj,)),
        dma((2 * len(waves),)),
        dma((len(waves) * group,)),
        dma((len(waves) * group,)),
        dma((len(waves) * group,)),
        dma((len(waves) * group,)),
        dma((len(waves),)),
        dma((len(waves),)),
        dma((4,)),
        dma((group,)),
        dma((group,)),
    ]
    wave_scratch = [
        [pltpu.VMEM(wave[skip:], BF16) for wave in waves] for skip in (0, 1, 1, 1)
    ]
    scratch += sum(wave_scratch, [])

    def run(*refs):
        count = len(waves)
        outs = refs[16 : 16 + count]
        rest = refs[16 + count :]
        groups = [rest[len(rest) - (4 - i) * count : len(rest) - (3 - i) * count] for i in range(4)]
        kernel(sizes, *refs[:16], *rest[: len(rest) - 4 * count], outs, *groups)

    held = sum(
        math.prod(x.shape) * jnp.dtype(x.dtype).itemsize for x in scratch if x.memory_space == pltpu.VMEM
    )
    hbm = pl.BlockSpec(memory_space=pltpu.HBM)
    query_grad, key_grad, value_grad, pair_grad, tail, *weights = pl.pallas_call(
        run,
        out_shape=(
            jax.ShapeDtypeStruct((q_half, width), BF16),
            jax.ShapeDtypeStruct((half, width), BF16),
            jax.ShapeDtypeStruct((half, width), BF16),
            jax.ShapeDtypeStruct((count, channels), BF16),
            jax.ShapeDtypeStruct(tail_shape, BF16),
            *(jax.ShapeDtypeStruct(wave, BF16) for wave in waves),
        ),
        in_specs=[hbm] * 11,
        out_specs=(vmem,) * (5 + len(waves)),
        scratch_shapes=scratch,
        compiler_params=pltpu.CompilerParams(
            collective_id=0, has_side_effects=True, vmem_limit_bytes=held + held // 8 + 4 * 1024 * 1024
        ),
        name="block_backward",
    )(
        *(
            pltpu.with_memory_space_constraint(x, pltpu.HBM)
            for x in (
                pair_rep,
                query_rows.reshape(rows, width),
                key_rows.reshape(keys, width),
                value_rows.reshape(keys, width),
                output_grad.reshape(rows, width),
                gain_first.reshape(1, channels),
                gate_weight,
                up_weight,
                down_weight,
                gain_second.reshape(1, channels),
                head_weight.T,
            )
        )
    )
    outputs = (query_grad, key_grad, value_grad, pair_grad)

    def finish_all(*refs):
        count = len(waves)
        finish(hidden_count, parts_of, group, *refs[:5], *refs[5 + count :], refs[5 : 5 + count])

    query_grad, key_grad, value_grad, pair_grad, gate_grad, up_grad, down_grad, head_grad, first_grad, second_grad = pl.pallas_call(
        finish_all,
        out_shape=tuple(jax.ShapeDtypeStruct(x.shape, x.dtype) for x in outputs)
        + (
            jax.ShapeDtypeStruct((channels, hidden_count), F32),
            jax.ShapeDtypeStruct((channels, hidden_count), F32),
            jax.ShapeDtypeStruct((hidden_count, channels), F32),
            jax.ShapeDtypeStruct((HEADS, channels), F32),
            jax.ShapeDtypeStruct((1, channels), F32),
            jax.ShapeDtypeStruct((1, channels), F32),
        ),
        in_specs=[vmem] * (5 + len(waves)),
        out_specs=(hbm,) * 10,
        scratch_shapes=[
            pltpu.VMEM((channels, hidden_count), F32),
            pltpu.VMEM((channels, hidden_count), F32),
            pltpu.VMEM((hidden_count, channels), F32),
            pltpu.VMEM((HEADS, channels), F32),
            pltpu.VMEM((1, channels), F32),
            pltpu.VMEM((1, channels), F32),
            dma((10,)),
        ],
        compiler_params=pltpu.CompilerParams(vmem_limit_bytes=8 * 1024 * 1024),
        name="finish_weights",
    )(tail, *outputs, *weights)
    return (
        query_grad[None],
        key_grad[None],
        value_grad[None],
        pair_grad.reshape(1, 1, share, block_count, block_rows, channels),
        gate_grad,
        up_grad,
        down_grad,
        head_grad.T,
        first_grad.reshape(channels),
        second_grad.reshape(channels),
    )


def solution(mesh):
    mesh_shape = (mesh.shape["noise"], mesh.shape["qi"], mesh.shape["kj"])
    return jax.shard_map(
        functools.partial(local, mesh_shape),
        mesh=mesh,
        in_specs=(
            P("qi", None, "kj", None),
            P("noise", "qi", None),
            P("noise", None, "kj", None),
            P("noise", None, "kj", None),
            P("noise", "qi", None),
            P(),
            P(),
            P(),
            P(),
            P(),
            P(),
        ),
        out_specs=(
            P("noise", ("qi", "kj"), None),
            P("noise", ("qi", "kj"), None),
            P("noise", ("qi", "kj"), None),
            P("qi", "noise", None, None, "kj", None),
            P(),
            P(),
            P(),
            P(),
            P(),
            P(),
        ),
        check_vma=False,
    )
```

```python
import functools
import math

import jax
import jax.numpy as jnp
from jax import lax
from jax.experimental import pallas as pl
from jax.experimental.pallas import tpu as pltpu
from jax.sharding import PartitionSpec as P

HEADS = 16
HEAD_DIM = 48
ALIGN = 8
BLOCK = 16
UNROLLED = 16
LANES = 128

epsilon = 1e-05
F32 = jnp.float32
BF16 = jnp.bfloat16
MESH = pl.DeviceIdType.MESH


def dot(left, right, left_dim, right_dim):
    return lax.dot_general(
        left, right, (((left_dim,), (right_dim,)), ((), ())), preferred_element_type=F32
    )


def normalize(values):
    center = values - jnp.mean(values, axis=1, keepdims=True)
    inverse = lax.rsqrt(jnp.mean(center * center, axis=1, keepdims=True) + epsilon)
    return center * inverse, inverse


def norm_backward(normed_grad, normed, inverse):
    first_mean = jnp.mean(normed_grad, axis=1, keepdims=True)
    second_mean = jnp.mean(normed_grad * normed, axis=1, keepdims=True)
    return inverse * (normed_grad - first_mean - normed * second_mean)


def place(parts_of, row):
    wave = 0
    while row >= parts_of[wave]:
        row -= parts_of[wave]
        wave += 1
    return wave, row


def kernel(
    sizes,
    pair_hbm,
    q_hbm,
    k_hbm,
    v_hbm,
    g_hbm,
    gain_first_hbm,
    gate_hbm,
    up_hbm,
    down_hbm,
    gain_second_hbm,
    head_hbm,
    query_out,
    key_out,
    value_out,
    pair_out,
    tail_out,
    q_ref,
    k_ref,
    v_ref,
    g_ref,
    gain_first_ref,
    gate_ref,
    up_ref,
    down_ref,
    gain_second_ref,
    head_ref,
    cells,
    pre_normed,
    pre_low,
    pre_low_t,
    gate_coef,
    up_coef,
    hidden,
    hidden_t,
    up_low,
    post_normed,
    post_low,
    inverses,
    bias_rows,
    bias_send,
    bias_all,
    q_cols,
    g_cols,
    kv_send,
    kv_all,
    q_heads,
    g_heads,
    k_heads,
    score,
    attend_grad,
    score_low,
    attend_low,
    score_cat,
    grad_send,
    grad_recv,
    grad_sum,
    post_scaled,
    query_part,
    query_recv,
    kv_part,
    kv_recv,
    tail_part,
    tail_core,
    tail_sum,
    tail_recv,
    input_sems,
    bias_sems,
    tile_send_sem,
    tile_recv_sem,
    grad_sems,
    query_send_sem,
    query_recv_sem,
    kv_send_sem,
    kv_recv_sem,
    pair_sems,
    w_sems,
    all_sems,
    fwd_send_sem,
    fwd_recv_sem,
    tail_sems,
    weight_out,
    w_part,
    w_core,
    w_sum,
    w_recv,
):
    n_noise, n_qi, n_kj, rows, keys, share, parts_of = sizes
    waves = len(parts_of)
    group = n_noise * n_kj
    cell_count = share * keys
    chunk = min(256, cell_count)
    scale = HEAD_DIM ** (-0.5)
    noise = lax.axis_index("noise")
    qi = lax.axis_index("qi")
    kj = lax.axis_index("kj")
    me = noise * n_kj + kj
    sibling = {"qi": 1 - qi}
    channels = cells.shape[-1]
    width = q_ref.shape[-1]
    half = keys // n_qi
    q_half = rows // n_kj
    own = HEADS // n_kj
    part = own * HEAD_DIM
    pack = min(own, max(1, LANES // keys))
    packed = own // pack

    def members(p):
        return [p + j * packed for j in range(pack)]

    def remote(src, dst, send, recv, device):
        return pltpu.make_async_remote_copy(
            src_ref=src, dst_ref=dst, send_sem=send, recv_sem=recv, device_id=device, device_id_type=MESH
        )

    def away(offset):
        if isinstance(offset, int):
            steps = (offset // n_kj, offset % n_kj)
            return {
                name: lax.bitwise_xor(at, step) for name, at, step in zip(("noise", "kj"), (noise, kj), steps) if step
            }
        return {
            "noise": lax.bitwise_xor(noise, lax.div(offset, n_kj)),
            "kj": lax.bitwise_xor(kj, lax.rem(offset, n_kj)),
        }

    def each(count, body):
        if count <= UNROLLED:
            for i in range(1, count):
                body(i)
            return

        def step(i, carry):
            body(i)
            return carry

        lax.fori_loop(1, count, step, 0)

    def added(count, total, term):
        if count <= UNROLLED:
            for i in range(1, count):
                total += term(i)
            return total
        return lax.fori_loop(1, count, lambda i, total: total + term(i), total)

    def moved(view, sems):
        return remote(view, view, sems.at[0], sems.at[1], sibling)

    forward_loads = [
        pltpu.make_async_copy(src, dst, input_sems.at[i])
        for i, (src, dst) in enumerate(
            (
                (pair_hbm.at[pl.ds(noise * share, share)], cells),
                (gain_first_hbm, gain_first_ref),
                (gate_hbm, gate_ref),
                (up_hbm, up_ref),
                (down_hbm, down_ref),
                (gain_second_hbm, gain_second_ref),
                (head_hbm, head_ref),
            )
        )
    ]
    attention_loads = [
        pltpu.make_async_copy(src, dst, input_sems.at[len(forward_loads) + i])
        for i, (src, dst) in enumerate(((q_hbm, q_ref), (k_hbm, k_ref), (g_hbm, g_ref), (v_hbm, v_ref)))
    ]
    for load in forward_loads:
        load.start()

    barrier = pltpu.get_barrier_semaphore()

    def greet(device):
        pl.semaphore_signal(barrier, inc=1, device_id=device, device_id_type=MESH)

    each(group, lambda i: greet(away(group - i)))
    greet(sibling)
    for load in attention_loads:
        load.start()
    for load in forward_loads:
        load.wait()

    gain_first = gain_first_ref[...]
    gain_second = gain_second_ref[...]
    head_t = head_ref[...]
    flat_cells = cells[...].reshape(cell_count, channels)
    for start in range(0, cell_count, chunk):
        at = slice(start, start + chunk)
        inputs = flat_cells[at].astype(F32)
        normed, inverse = normalize(inputs)
        lowered = (normed * gain_first).astype(BF16)
        gate_pre = dot(lowered, gate_ref[...], 1, 0)
        up_pre = dot(lowered, up_ref[...], 1, 0)
        sigmoid = jax.nn.sigmoid(gate_pre)
        silu = gate_pre * sigmoid
        low_hidden = (silu * up_pre).astype(BF16)
        updated = inputs + dot(low_hidden, down_ref[...], 1, 0)
        after, after_inverse = normalize(updated)
        after_low = (after * gain_second).astype(BF16)
        pre_normed[at] = normed
        pre_low[at] = lowered
        gate_coef[at] = up_pre * sigmoid * (1.0 + gate_pre * (1.0 - sigmoid))
        up_coef[at] = silu
        hidden[at] = low_hidden
        post_normed[at] = after
        post_low[at] = after_low
        inverses[at, 0:1] = inverse
        inverses[at, 1:2] = after_inverse
    for i in range(share):
        bias_rows[i] = dot(head_t, post_low[i * keys : (i + 1) * keys], 1, 1)
    for j in range(n_kj):
        for p in range(packed):
            bias_send[j, p] = jnp.concatenate([bias_rows[:, j * own + h, :] for h in members(p)], 1).astype(BF16)

    for load in attention_loads:
        load.wait()
    for j in range(n_kj):
        at = slice(j * part, (j + 1) * part)
        q_cols[j] = q_ref[:, at]
        g_cols[j] = g_ref[:, at]
        kv_send[j, 0] = k_ref[:, at]
        kv_send[j, 1] = v_ref[:, at]

    pl.semaphore_wait(barrier, group)

    def tile_copy(offset):
        return remote(
            kv_send.at[lax.bitwise_xor(kj, offset)],
            kv_all.at[kj],
            tile_send_sem.at[offset],
            tile_recv_sem.at[offset],
            {"kj": lax.bitwise_xor(kj, offset)},
        )

    def bias_copy(offset):
        return remote(
            bias_send.at[lax.bitwise_xor(kj, lax.rem(offset, n_kj))],
            bias_all.at[me],
            bias_sems.at[0],
            bias_sems.at[1],
            away(offset),
        )

    each(n_kj, lambda i: tile_copy(i).start())
    each(group, lambda i: bias_copy(group - i).start())

    kv_all[kj] = kv_send[kj]
    bias_all[me] = bias_send[kj]
    lane = lax.broadcasted_iota(jnp.int32, (1, part), 1)

    def mask(h):
        inside = jnp.logical_and(lane >= h * HEAD_DIM, lane < (h + 1) * HEAD_DIM)
        return jnp.where(inside, 1.0, 0.0).astype(BF16)

    q_own = q_cols[kj]
    g_own = g_cols[kj]
    for h in range(own):
        at = slice(h * rows, (h + 1) * rows)
        q_heads[at] = q_own * mask(h)
        g_heads[at] = g_own * mask(h)
    hidden_t[...] = hidden[...].T
    pre_low_t[...] = pre_low[...].T
    for wave, count in enumerate(parts_of):
        if count < math.prod(w_part[wave].shape[:3]):
            w_part[wave][...] = jnp.zeros(w_part[wave].shape, BF16)

    each(n_kj, lambda i: tile_copy(i).wait_recv())
    k_own = kv_all[:, 0].reshape(n_kj * keys, part)
    v_own = kv_all[:, 1].reshape(n_kj * keys, part)
    score[...] = dot(q_heads[...], k_own, 1, 1) * scale
    attend_grad[...] = dot(g_heads[...], v_own, 1, 1)
    for h in range(own):
        k_heads[h * n_kj * keys : (h + 1) * n_kj * keys] = k_own * mask(h)

    others = pl.ds(1, group - 1)
    moved(bias_all.at[others], bias_sems).wait_recv()

    for p in range(packed):
        blocks = [
            jnp.concatenate([bias_all[n * n_kj + j, p] for n in range(n_noise)], 0).astype(F32) for j in range(n_kj)
        ]
        grads = []
        for i, h in enumerate(members(p)):
            at = slice(h * rows, (h + 1) * rows)
            full = score[at] + jnp.concatenate([block[:, i * keys : (i + 1) * keys] for block in blocks], 1)
            expo = jnp.exp(full - jnp.max(full, axis=1, keepdims=True))
            attend = expo * (1.0 / jnp.sum(expo, axis=1, keepdims=True))
            weighed = attend_grad[at]
            score_grad = attend * (weighed - jnp.sum(attend * weighed, axis=1, keepdims=True))
            grads.append(score_grad)
            attend_low[at] = attend.astype(BF16)
            score_low[at] = score_grad.astype(BF16)
            score_cat[:, h * n_kj * keys : (h + 1) * n_kj * keys] = score_grad.astype(BF16)
        for j in range(n_kj):
            piece = jnp.concatenate([grad[:, j * keys : (j + 1) * keys] for grad in grads], 1).astype(BF16)
            for n in range(n_noise):
                grad_send[n * n_kj + j, p] = piece[n * share : (n + 1) * share]

    def grad_copy(offset):
        return remote(
            grad_send.at[lax.bitwise_xor(me, offset)],
            grad_recv.at[offset],
            grad_sems.at[0],
            grad_sems.at[1],
            away(offset),
        )

    each(group, lambda i: grad_copy(group - i).start())

    query_all = (dot(score_cat[...], k_heads[...], 1, 0) * scale).astype(BF16)
    for j in range(n_kj):
        query_part[j] = query_all[j * q_half : (j + 1) * q_half]
    key_all = (dot(score_low[...], q_heads[...], 0, 0) * scale).astype(BF16)
    value_all = dot(attend_low[...], g_heads[...], 0, 0).astype(BF16)
    for j in range(n_kj):
        for i in range(n_qi):
            at = slice(j * keys + i * half, j * keys + (i + 1) * half)
            kv_part[i * n_kj + j, 0] = key_all[at]
            kv_part[i * n_kj + j, 1] = value_all[at]

    def query_copy(offset):
        return remote(
            query_part.at[lax.bitwise_xor(kj, offset)],
            query_recv.at[kj],
            query_send_sem.at[offset],
            query_recv_sem.at[offset],
            {"kj": lax.bitwise_xor(kj, offset)},
        )

    cell = qi * n_kj + kj

    def kv_copy(offset):
        if isinstance(offset, int):
            steps = (offset // n_kj, offset % n_kj)
        else:
            steps = (lax.div(offset, n_kj), lax.rem(offset, n_kj))
        return remote(
            kv_part.at[lax.bitwise_xor(cell, offset)],
            kv_recv.at[cell],
            kv_send_sem.at[offset],
            kv_recv_sem.at[offset],
            {"qi": lax.bitwise_xor(qi, steps[0]), "kj": lax.bitwise_xor(kj, steps[1])},
        )

    each(n_kj, lambda i: query_copy(i).start())
    each(n_qi * n_kj, lambda i: kv_copy(i).start())
    query_recv[kj] = query_part[kj]
    kv_recv[cell] = kv_part[cell]
    each(n_kj, lambda i: tile_copy(i).wait_send())
    moved(bias_all.at[others], bias_sems).wait_send()

    grad_recv[0] = grad_send[me]
    moved(grad_recv.at[others], grad_sems).wait_recv()
    for j in range(n_kj):
        total = grad_recv[j].astype(F32)
        grad_sum[lax.bitwise_xor(kj, j)] = added(
            n_noise, total, lambda n: grad_recv[n * n_kj + j].astype(F32)
        )

    head_part = jnp.zeros((HEADS, channels), F32)
    for i in range(share):
        at = slice(i * keys, (i + 1) * keys)
        grad_low = jnp.concatenate(
            [grad_sum[j, :, i, m * keys : (m + 1) * keys] for j in range(n_kj) for m in range(pack)], 0
        ).astype(BF16)
        post_scaled[at] = dot(grad_low, head_t, 0, 0)
        head_part += dot(grad_low, post_low[at], 1, 0)
    hidden_count = gate_ref.shape[1]
    tiles = hidden_count // channels

    def put(t, value):
        wave, first = place(parts_of, t * channels)
        block = w_part[wave].shape[2]
        count = channels // block
        owner = first // block
        w_part[wave][owner // group, owner % group : owner % group + count] = value.astype(BF16).reshape(
            count, block, channels
        )

    starts = range(0, cell_count, chunk)
    second_part = jnp.zeros((1, channels), F32)
    down_part = jnp.zeros((hidden_count, channels), F32)
    gate_part = jnp.zeros((channels, hidden_count), F32)
    for start in starts:
        at = slice(start, start + chunk)
        scaled = post_scaled[at]
        after = post_normed[at]
        second_part += jnp.sum(scaled * after, axis=0, keepdims=True)
        updated_grad = norm_backward(scaled * gain_second, after, inverses[at, 1:2])
        updated_low = updated_grad.astype(BF16)
        post_scaled[at] = updated_grad
        down_part += dot(hidden_t[:, at], updated_low, 1, 0)
        hidden_grad = dot(updated_low, down_ref[...], 1, 1)
        gate_low = (hidden_grad * gate_coef[at]).astype(BF16)
        up_low[at] = (hidden_grad * up_coef[at]).astype(BF16)
        gate_part += dot(pre_low_t[:, at], gate_low, 1, 0)
        hidden[at] = gate_low

    for t in range(tiles):
        at = slice(t * channels, (t + 1) * channels)
        put(t, down_part[at])
        put(tiles + t, gate_part[:, at])

    def core_copy(wave):
        return remote(
            w_part[wave].at[1 - qi], w_core[wave], pair_sems.at[2 * wave], pair_sems.at[2 * wave + 1], sibling
        )

    if waves > 1:
        core_copy(0).start()

    first_part = jnp.zeros((1, channels), F32)
    up_part = jnp.zeros((channels, hidden_count), F32)
    for start in starts:
        at = slice(start, start + chunk)
        up_part += dot(pre_low_t[:, at], up_low[at], 1, 0)
        pre_scaled = dot(hidden[at], gate_ref[...], 1, 1) + dot(up_low[at], up_ref[...], 1, 1)
        first_part += jnp.sum(pre_scaled * pre_normed[at], axis=0, keepdims=True)
        post_normed[at] = pre_scaled
    for t in range(tiles):
        put(2 * tiles + t, up_part[:, t * channels : (t + 1) * channels])
    core_copy(waves - 1).start()

    tail_part[0:HEADS] = head_part.astype(BF16)
    tail_part[HEADS:] = jnp.concatenate(
        (
            jnp.broadcast_to(first_part, (ALIGN // 2, channels)),
            jnp.broadcast_to(second_part, (ALIGN // 2, channels)),
        ),
        0,
    ).astype(BF16)
    owner = group // 2
    to_owner = lax.bitwise_xor(me, owner)
    tail_core_copy = remote(tail_part, tail_core, tail_sems.at[0], tail_sems.at[1], sibling)
    tail_core_copy.start()

    def tail_copy():
        device = {"noise": owner // n_kj, "kj": owner % n_kj}
        return remote(tail_sum, tail_recv.at[to_owner], tail_sems.at[2], tail_sems.at[3], device)

    def tail_back(offset):
        return remote(tail_out, tail_out, tail_sems.at[4], tail_sems.at[5], away(offset))

    def w_copy(wave, offset):
        return remote(
            w_sum[wave].at[lax.bitwise_xor(me, offset)],
            w_recv[wave].at[offset],
            w_sems.at[2 * wave],
            w_sems.at[2 * wave + 1],
            away(offset),
        )

    def all_copy(wave, offset):
        at = weight_out[wave].at[qi, me]
        return remote(at, at, all_sems.at[2 * wave], all_sems.at[2 * wave + 1], away(offset))

    def fwd_copy(wave, core):
        at = weight_out[wave].at[core]
        return remote(at, at, fwd_send_sem.at[wave], fwd_recv_sem.at[wave], sibling)

    def pair_of(sems, wave):
        return sems.at[pl.ds(2 * wave, 2)]

    for wave in range(waves):
        core_copy(wave).wait_recv()
        w_sum[wave][...] = (w_part[wave][qi].astype(F32) + w_core[wave][...].astype(F32)).astype(BF16)
        each(group, lambda i: w_copy(wave, group - i).start())
    tail_core_copy.wait_recv()
    tail_sum[...] = (tail_part[...].astype(F32) + tail_core[...].astype(F32)).astype(BF16)

    @pl.when(to_owner != 0)
    def _():
        tail_copy().start()

    for start in starts:
        at = slice(start, start + chunk)
        inputs_grad = norm_backward(post_normed[at] * gain_first, pre_normed[at], inverses[at, 0:1])
        pair_out[at] = (post_scaled[at] + inputs_grad).astype(BF16)

    each(n_kj, lambda i: query_copy(i).wait_recv())
    each(n_qi * n_kj, lambda i: kv_copy(i).wait_recv())
    for j in range(n_kj):
        at = slice(j * part, (j + 1) * part)
        query_out[:, at] = query_recv[j]
        for out, which in ((key_out, 0), (value_out, 1)):
            total = kv_recv[j, which].astype(F32)
            for i in range(1, n_qi):
                total += kv_recv[i * n_kj + j, which].astype(F32)
            out[:, at] = total.astype(BF16)

    each(n_kj, lambda i: query_copy(i).wait_send())
    each(n_qi * n_kj, lambda i: kv_copy(i).wait_send())
    moved(grad_recv.at[others], grad_sems).wait_send()
    for wave in range(waves):
        core_copy(wave).wait_send()
    tail_core_copy.wait_send()

    for wave in range(waves):
        moved(w_recv[wave].at[others], pair_of(w_sems, wave)).wait_recv()
        total = added(group, w_sum[wave][me].astype(F32), lambda i: w_recv[wave][i].astype(F32))
        weight_out[wave][qi, me] = (total * (1.0 / (rows * n_qi))).astype(BF16)
        each(group, lambda i: all_copy(wave, group - i).start())

    @pl.when(to_owner == 0)
    def _():
        moved(tail_recv.at[others], tail_sems.at[pl.ds(2, 2)]).wait_recv()
        total = added(group, tail_sum[...].astype(F32), lambda i: tail_recv[i].astype(F32))
        tail_out[...] = (total * (1.0 / (rows * n_qi))).astype(BF16)
        each(group, lambda i: tail_back(group - i).start())

    for wave in range(waves):
        moved(w_recv[wave].at[others], pair_of(w_sems, wave)).wait_send()
    for wave in range(waves):
        moved(weight_out[wave].at[qi, others], pair_of(all_sems, wave)).wait_recv()
        fwd_copy(wave, qi).start()

    @pl.when(to_owner != 0)
    def _():
        remote(tail_out, tail_out, tail_sems.at[4], tail_sems.at[5], sibling).wait_recv()
        tail_copy().wait_send()

    @pl.when(to_owner == 0)
    def _():
        moved(tail_recv.at[others], tail_sems.at[pl.ds(4, 2)]).wait_send()

    for wave in range(waves):
        moved(weight_out[wave].at[qi, others], pair_of(all_sems, wave)).wait_send()
    for wave in range(waves):
        fwd_copy(wave, 1 - qi).wait_recv()
        fwd_copy(wave, qi).wait_send()


def finish(
    hidden_count,
    parts_of,
    group,
    tail_ref,
    query_ref,
    key_ref,
    value_ref,
    pair_ref,
    query_out,
    key_out,
    value_out,
    pair_out,
    gate_out,
    up_out,
    down_out,
    head_out,
    first_out,
    second_out,
    gate_wide,
    up_wide,
    down_wide,
    head_wide,
    first_wide,
    second_wide,
    sems,
    weight_ref,
):
    copies = []

    def store(src, dst):
        copy = pltpu.make_async_copy(src, dst, sems.at[len(copies)])
        copy.start()
        copies.append(copy)

    store(pair_ref, pair_out)
    store(query_ref, query_out)
    store(key_ref, key_out)
    store(value_ref, value_out)
    channels = tail_ref.shape[1]
    tiles = hidden_count // channels

    def tile(t):
        wave, first = place(parts_of, t * channels)
        block = weight_ref[wave].shape[2]
        count = channels // block
        owner = first // block
        value = weight_ref[wave][owner // group, owner % group : owner % group + count]
        return value.astype(F32).reshape(channels, channels)

    for t in range(tiles):
        down_wide[t * channels : (t + 1) * channels] = tile(t)
    store(down_wide, down_out)
    for t in range(tiles):
        gate_wide[:, t * channels : (t + 1) * channels] = tile(tiles + t)
    store(gate_wide, gate_out)
    for t in range(tiles):
        up_wide[:, t * channels : (t + 1) * channels] = tile(2 * tiles + t)
    store(up_wide, up_out)
    tail = tail_ref[...].astype(F32)
    head_wide[...] = tail[0:HEADS]
    store(head_wide, head_out)
    first_wide[...] = tail[HEADS : HEADS + 1]
    second_wide[...] = tail[HEADS + ALIGN // 2 : HEADS + ALIGN // 2 + 1]
    store(first_wide, first_out)
    store(second_wide, second_out)
    for copy in copies:
        copy.wait()


def local(
    mesh_shape,
    pair_rep,
    query_rows,
    key_rows,
    value_rows,
    output_grad,
    gain_first,
    gate_weight,
    up_weight,
    down_weight,
    gain_second,
    head_weight,
):
    n_noise, n_qi, n_kj = mesh_shape
    rows, block_count, block_rows, channels = pair_rep.shape
    keys = block_count * block_rows
    width = query_rows.shape[2]
    share = rows // n_noise
    count = share * keys
    group = n_noise * n_kj
    hidden_count = gate_weight.shape[1]
    devices = n_qi * group
    if hidden_count % (BLOCK * devices) == 0:
        parts_of = (2 * hidden_count, hidden_count)
    else:
        parts_of = (3 * hidden_count,)
    waves = tuple(
        (n_qi, group, -(-part // (BLOCK * devices)) * BLOCK, channels) for part in parts_of
    )
    tail_shape = (HEADS + ALIGN, channels)
    half = keys // n_qi
    q_half = rows // n_kj
    sizes = (n_noise, n_qi, n_kj, rows, keys, share, parts_of)
    own = HEADS // n_kj
    part = own * HEAD_DIM
    pack = min(own, max(1, LANES // keys))
    vmem = pl.BlockSpec(memory_space=pltpu.VMEM)
    dma = pltpu.SemaphoreType.DMA

    scratch = [
        pltpu.VMEM((rows, width), BF16),
        pltpu.VMEM((keys, width), BF16),
        pltpu.VMEM((keys, width), BF16),
        pltpu.VMEM((rows, width), BF16),
        pltpu.VMEM((1, channels), F32),
        pltpu.VMEM((channels, hidden_count), BF16),
        pltpu.VMEM((channels, hidden_count), BF16),
        pltpu.VMEM((hidden_count, channels), BF16),
        pltpu.VMEM((1, channels), F32),
        pltpu.VMEM((HEADS, channels), BF16),
        pltpu.VMEM((share, block_count, block_rows, channels), BF16),
        pltpu.VMEM((count, channels), F32),
        pltpu.VMEM((count, channels), BF16),
        pltpu.VMEM((channels, count), BF16),
        pltpu.VMEM((count, hidden_count), F32),
        pltpu.VMEM((count, hidden_count), F32),
        pltpu.VMEM((count, hidden_count), BF16),
        pltpu.VMEM((hidden_count, count), BF16),
        pltpu.VMEM((count, hidden_count), BF16),
        pltpu.VMEM((count, channels), F32),
        pltpu.VMEM((count, channels), BF16),
        pltpu.VMEM((count, 128), F32),
        pltpu.VMEM((share, HEADS, keys), F32),
        pltpu.VMEM((n_kj, own // pack, share, pack * keys), BF16),
        pltpu.VMEM((group, own // pack, share, pack * keys), BF16),
        pltpu.VMEM((n_kj, rows, part), BF16),
        pltpu.VMEM((n_kj, rows, part), BF16),
        pltpu.VMEM((n_kj, 2, keys, part), BF16),
        pltpu.VMEM((n_kj, 2, keys, part), BF16),
        pltpu.VMEM((own * rows, part), BF16),
        pltpu.VMEM((own * rows, part), BF16),
        pltpu.VMEM((own * n_kj * keys, part), BF16),
        pltpu.VMEM((own * rows, n_kj * keys), F32),
        pltpu.VMEM((own * rows, n_kj * keys), F32),
        pltpu.VMEM((own * rows, n_kj * keys), BF16),
        pltpu.VMEM((own * rows, n_kj * keys), BF16),
        pltpu.VMEM((rows, own * n_kj * keys), BF16),
        pltpu.VMEM((group, own // pack, share, pack * keys), BF16),
        pltpu.VMEM((group, own // pack, share, pack * keys), BF16),
        pltpu.VMEM((n_kj, own // pack, share, pack * keys), F32),
        pltpu.VMEM((count, channels), F32),
        pltpu.VMEM((n_kj, q_half, part), BF16),
        pltpu.VMEM((n_kj, q_half, part), BF16),
        pltpu.VMEM((n_qi * n_kj, 2, half, part), BF16),
        pltpu.VMEM((n_qi * n_kj, 2, half, part), BF16),
        pltpu.VMEM(tail_shape, BF16),
        pltpu.VMEM(tail_shape, BF16),
        pltpu.VMEM(tail_shape, BF16),
        pltpu.VMEM((group, *tail_shape), BF16),
        dma((11,)),
        dma((2,)),
        dma((n_kj,)),
        dma((n_kj,)),
        dma((2,)),
        dma((n_kj,)),
        dma((n_kj,)),
        dma((n_qi * n_kj,)),
        dma((n_qi * n_kj,)),
        dma((2 * len(waves),)),
        dma((2 * len(waves),)),
        dma((2 * len(waves),)),
        dma((len(waves),)),
        dma((len(waves),)),
        dma((6,)),
    ]
    wave_scratch = [
        [pltpu.VMEM(wave[skip:], BF16) for wave in waves] for skip in (0, 1, 1, 1)
    ]
    scratch += sum(wave_scratch, [])

    def run(*refs):
        count = len(waves)
        outs = refs[16 : 16 + count]
        rest = refs[16 + count :]
        groups = [rest[len(rest) - (4 - i) * count : len(rest) - (3 - i) * count] for i in range(4)]
        kernel(sizes, *refs[:16], *rest[: len(rest) - 4 * count], outs, *groups)

    held = sum(
        math.prod(x.shape) * jnp.dtype(x.dtype).itemsize for x in scratch if x.memory_space == pltpu.VMEM
    )
    hbm = pl.BlockSpec(memory_space=pltpu.HBM)
    query_grad, key_grad, value_grad, pair_grad, tail, *weights = pl.pallas_call(
        run,
        out_shape=(
            jax.ShapeDtypeStruct((q_half, width), BF16),
            jax.ShapeDtypeStruct((half, width), BF16),
            jax.ShapeDtypeStruct((half, width), BF16),
            jax.ShapeDtypeStruct((count, channels), BF16),
            jax.ShapeDtypeStruct(tail_shape, BF16),
            *(jax.ShapeDtypeStruct(wave, BF16) for wave in waves),
        ),
        in_specs=[hbm] * 11,
        out_specs=(vmem,) * (5 + len(waves)),
        scratch_shapes=scratch,
        compiler_params=pltpu.CompilerParams(
            collective_id=0, has_side_effects=True, vmem_limit_bytes=held + held // 8 + 4 * 1024 * 1024
        ),
        name="block_backward",
    )(
        *(
            pltpu.with_memory_space_constraint(x, pltpu.HBM)
            for x in (
                pair_rep,
                query_rows.reshape(rows, width),
                key_rows.reshape(keys, width),
                value_rows.reshape(keys, width),
                output_grad.reshape(rows, width),
                gain_first.reshape(1, channels),
                gate_weight,
                up_weight,
                down_weight,
                gain_second.reshape(1, channels),
                head_weight.T,
            )
        )
    )
    outputs = (query_grad, key_grad, value_grad, pair_grad)

    def finish_all(*refs):
        count = len(waves)
        finish(hidden_count, parts_of, group, *refs[:5], *refs[5 + count :], refs[5 : 5 + count])

    query_grad, key_grad, value_grad, pair_grad, gate_grad, up_grad, down_grad, head_grad, first_grad, second_grad = pl.pallas_call(
        finish_all,
        out_shape=tuple(jax.ShapeDtypeStruct(x.shape, x.dtype) for x in outputs)
        + (
            jax.ShapeDtypeStruct((channels, hidden_count), F32),
            jax.ShapeDtypeStruct((channels, hidden_count), F32),
            jax.ShapeDtypeStruct((hidden_count, channels), F32),
            jax.ShapeDtypeStruct((HEADS, channels), F32),
            jax.ShapeDtypeStruct((1, channels), F32),
            jax.ShapeDtypeStruct((1, channels), F32),
        ),
        in_specs=[vmem] * (5 + len(waves)),
        out_specs=(hbm,) * 10,
        scratch_shapes=[
            pltpu.VMEM((channels, hidden_count), F32),
            pltpu.VMEM((channels, hidden_count), F32),
            pltpu.VMEM((hidden_count, channels), F32),
            pltpu.VMEM((HEADS, channels), F32),
            pltpu.VMEM((1, channels), F32),
            pltpu.VMEM((1, channels), F32),
            dma((10,)),
        ],
        compiler_params=pltpu.CompilerParams(vmem_limit_bytes=8 * 1024 * 1024),
        name="finish_weights",
    )(tail, *outputs, *weights)
    return (
        query_grad[None],
        key_grad[None],
        value_grad[None],
        pair_grad.reshape(1, 1, share, block_count, block_rows, channels),
        gate_grad,
        up_grad,
        down_grad,
        head_grad.T,
        first_grad.reshape(channels),
        second_grad.reshape(channels),
    )


def solution(mesh):
    mesh_shape = (mesh.shape["noise"], mesh.shape["qi"], mesh.shape["kj"])
    return jax.shard_map(
        functools.partial(local, mesh_shape),
        mesh=mesh,
        in_specs=(
            P("qi", None, "kj", None),
            P("noise", "qi", None),
            P("noise", None, "kj", None),
            P("noise", None, "kj", None),
            P("noise", "qi", None),
            P(),
            P(),
            P(),
            P(),
            P(),
            P(),
        ),
        out_specs=(
            P("noise", ("qi", "kj"), None),
            P("noise", ("qi", "kj"), None),
            P("noise", ("qi", "kj"), None),
            P("qi", "noise", None, None, "kj", None),
            P(),
            P(),
            P(),
            P(),
            P(),
            P(),
        ),
        check_vma=False,
    )
```

```python
import functools
import math

import jax
import jax.numpy as jnp
from jax import lax
from jax.experimental import pallas as pl
from jax.experimental.pallas import tpu as pltpu
from jax.sharding import PartitionSpec as P

HEADS = 16
HEAD_DIM = 48
ALIGN = 8
BLOCK = 16
UNROLLED = 16
LANES = 128

epsilon = 1e-05
F32 = jnp.float32
BF16 = jnp.bfloat16
MESH = pl.DeviceIdType.MESH


def dot(left, right, left_dim, right_dim):
    return lax.dot_general(
        left, right, (((left_dim,), (right_dim,)), ((), ())), preferred_element_type=F32
    )


def normalize(values):
    center = values - jnp.mean(values, axis=1, keepdims=True)
    inverse = lax.rsqrt(jnp.mean(center * center, axis=1, keepdims=True) + epsilon)
    return center * inverse, inverse


def norm_backward(normed_grad, normed, inverse):
    first_mean = jnp.mean(normed_grad, axis=1, keepdims=True)
    second_mean = jnp.mean(normed_grad * normed, axis=1, keepdims=True)
    return inverse * (normed_grad - first_mean - normed * second_mean)


def place(parts_of, row):
    wave = 0
    while row >= parts_of[wave]:
        row -= parts_of[wave]
        wave += 1
    return wave, row


def kernel(
    sizes,
    pair_hbm,
    q_hbm,
    k_hbm,
    v_hbm,
    g_hbm,
    gain_first_hbm,
    gate_hbm,
    up_hbm,
    down_hbm,
    gain_second_hbm,
    head_hbm,
    query_out,
    key_out,
    value_out,
    pair_out,
    tail_out,
    q_ref,
    k_ref,
    v_ref,
    g_ref,
    gain_first_ref,
    gate_ref,
    up_ref,
    down_ref,
    gain_second_ref,
    head_ref,
    cells,
    pre_normed,
    pre_low,
    pre_low_t,
    gate_coef,
    up_coef,
    hidden,
    hidden_t,
    up_low,
    updated_low,
    post_normed,
    post_low,
    inverses,
    bias_rows,
    bias_send,
    bias_all,
    q_cols,
    g_cols,
    kv_send,
    kv_all,
    q_heads,
    g_heads,
    k_heads,
    score,
    attend_grad,
    score_low,
    attend_low,
    score_cat,
    grad_send,
    grad_recv,
    grad_sum,
    post_scaled,
    query_part,
    query_recv,
    kv_part,
    kv_recv,
    tail_part,
    tail_core,
    tail_sum,
    tail_recv,
    input_sems,
    bias_sems,
    tile_send_sem,
    tile_recv_sem,
    grad_sems,
    query_send_sem,
    query_recv_sem,
    kv_send_sem,
    kv_recv_sem,
    pair_sems,
    w_sems,
    all_sems,
    fwd_send_sem,
    fwd_recv_sem,
    tail_sems,
    weight_out,
    w_part,
    w_core,
    w_sum,
    w_recv,
):
    n_noise, n_qi, n_kj, rows, keys, share, parts_of = sizes
    waves = len(parts_of)
    group = n_noise * n_kj
    cell_count = share * keys
    chunk = min(256, cell_count)
    scale = HEAD_DIM ** (-0.5)
    noise = lax.axis_index("noise")
    qi = lax.axis_index("qi")
    kj = lax.axis_index("kj")
    me = noise * n_kj + kj
    sibling = {"qi": 1 - qi}
    channels = cells.shape[-1]
    width = q_ref.shape[-1]
    half = keys // n_qi
    q_half = rows // n_kj
    own = HEADS // n_kj
    part = own * HEAD_DIM
    pack = min(own, max(1, LANES // keys))
    packed = own // pack

    def members(p):
        return [p + j * packed for j in range(pack)]

    def remote(src, dst, send, recv, device):
        return pltpu.make_async_remote_copy(
            src_ref=src, dst_ref=dst, send_sem=send, recv_sem=recv, device_id=device, device_id_type=MESH
        )

    def away(offset):
        if isinstance(offset, int):
            steps = (offset // n_kj, offset % n_kj)
            return {
                name: lax.bitwise_xor(at, step) for name, at, step in zip(("noise", "kj"), (noise, kj), steps) if step
            }
        return {
            "noise": lax.bitwise_xor(noise, lax.div(offset, n_kj)),
            "kj": lax.bitwise_xor(kj, lax.rem(offset, n_kj)),
        }

    def each(count, body):
        if count <= UNROLLED:
            for i in range(1, count):
                body(i)
            return

        def step(i, carry):
            body(i)
            return carry

        lax.fori_loop(1, count, step, 0)

    def added(count, total, term):
        if count <= UNROLLED:
            for i in range(1, count):
                total += term(i)
            return total
        return lax.fori_loop(1, count, lambda i, total: total + term(i), total)

    def moved(view, sems):
        return remote(view, view, sems.at[0], sems.at[1], sibling)

    forward_loads = [
        pltpu.make_async_copy(src, dst, input_sems.at[i])
        for i, (src, dst) in enumerate(
            (
                (pair_hbm.at[pl.ds(noise * share, share)], cells),
                (gain_first_hbm, gain_first_ref),
                (gate_hbm, gate_ref),
                (up_hbm, up_ref),
                (down_hbm, down_ref),
                (gain_second_hbm, gain_second_ref),
                (head_hbm, head_ref),
            )
        )
    ]
    attention_loads = [
        pltpu.make_async_copy(src, dst, input_sems.at[len(forward_loads) + i])
        for i, (src, dst) in enumerate(((q_hbm, q_ref), (k_hbm, k_ref), (g_hbm, g_ref), (v_hbm, v_ref)))
    ]
    for load in forward_loads:
        load.start()

    barrier = pltpu.get_barrier_semaphore()

    def greet(device):
        pl.semaphore_signal(barrier, inc=1, device_id=device, device_id_type=MESH)

    each(group, lambda i: greet(away(group - i)))
    greet(sibling)
    for load in attention_loads:
        load.start()
    for load in forward_loads:
        load.wait()

    gain_first = gain_first_ref[...]
    gain_second = gain_second_ref[...]
    head_t = head_ref[...]
    flat_cells = cells[...].reshape(cell_count, channels)
    for start in range(0, cell_count, chunk):
        at = slice(start, start + chunk)
        inputs = flat_cells[at].astype(F32)
        normed, inverse = normalize(inputs)
        lowered = (normed * gain_first).astype(BF16)
        gate_pre = dot(lowered, gate_ref[...], 1, 0)
        up_pre = dot(lowered, up_ref[...], 1, 0)
        sigmoid = jax.nn.sigmoid(gate_pre)
        silu = gate_pre * sigmoid
        low_hidden = (silu * up_pre).astype(BF16)
        updated = inputs + dot(low_hidden, down_ref[...], 1, 0)
        after, after_inverse = normalize(updated)
        after_low = (after * gain_second).astype(BF16)
        pre_normed[at] = normed
        pre_low[at] = lowered
        gate_coef[at] = up_pre * sigmoid * (1.0 + gate_pre * (1.0 - sigmoid))
        up_coef[at] = silu
        hidden[at] = low_hidden
        post_normed[at] = after
        post_low[at] = after_low
        inverses[at, 0:1] = inverse
        inverses[at, 1:2] = after_inverse
    for i in range(share):
        bias_rows[i] = dot(head_t, post_low[i * keys : (i + 1) * keys], 1, 1)
    for j in range(n_kj):
        for p in range(packed):
            bias_send[j, p] = jnp.concatenate([bias_rows[:, j * own + h, :] for h in members(p)], 1).astype(BF16)

    for load in attention_loads:
        load.wait()
    for j in range(n_kj):
        at = slice(j * part, (j + 1) * part)
        q_cols[j] = q_ref[:, at]
        g_cols[j] = g_ref[:, at]
        kv_send[j, 0] = k_ref[:, at]
        kv_send[j, 1] = v_ref[:, at]

    pl.semaphore_wait(barrier, group)

    def tile_copy(offset):
        return remote(
            kv_send.at[lax.bitwise_xor(kj, offset)],
            kv_all.at[kj],
            tile_send_sem.at[offset],
            tile_recv_sem.at[offset],
            {"kj": lax.bitwise_xor(kj, offset)},
        )

    def bias_copy(offset):
        return remote(
            bias_send.at[lax.bitwise_xor(kj, lax.rem(offset, n_kj))],
            bias_all.at[me],
            bias_sems.at[0],
            bias_sems.at[1],
            away(offset),
        )

    each(n_kj, lambda i: tile_copy(i).start())
    each(group, lambda i: bias_copy(group - i).start())

    kv_all[kj] = kv_send[kj]
    bias_all[me] = bias_send[kj]
    lane = lax.broadcasted_iota(jnp.int32, (1, part), 1)

    def mask(h):
        inside = jnp.logical_and(lane >= h * HEAD_DIM, lane < (h + 1) * HEAD_DIM)
        return jnp.where(inside, 1.0, 0.0).astype(BF16)

    q_own = q_cols[kj]
    g_own = g_cols[kj]
    for h in range(own):
        at = slice(h * rows, (h + 1) * rows)
        q_heads[at] = q_own * mask(h)
        g_heads[at] = g_own * mask(h)
    hidden_t[...] = hidden[...].T
    pre_low_t[...] = pre_low[...].T
    for wave, count in enumerate(parts_of):
        if count < math.prod(w_part[wave].shape[:3]):
            w_part[wave][...] = jnp.zeros(w_part[wave].shape, BF16)

    each(n_kj, lambda i: tile_copy(i).wait_recv())
    k_own = kv_all[:, 0].reshape(n_kj * keys, part)
    v_own = kv_all[:, 1].reshape(n_kj * keys, part)
    score[...] = dot(q_heads[...], k_own, 1, 1) * scale
    attend_grad[...] = dot(g_heads[...], v_own, 1, 1)
    for h in range(own):
        k_heads[h * n_kj * keys : (h + 1) * n_kj * keys] = k_own * mask(h)

    others = pl.ds(1, group - 1)
    moved(bias_all.at[others], bias_sems).wait_recv()

    for p in range(packed):
        blocks = [
            jnp.concatenate([bias_all[n * n_kj + j, p] for n in range(n_noise)], 0).astype(F32) for j in range(n_kj)
        ]
        grads = []
        for i, h in enumerate(members(p)):
            at = slice(h * rows, (h + 1) * rows)
            full = score[at] + jnp.concatenate([block[:, i * keys : (i + 1) * keys] for block in blocks], 1)
            expo = jnp.exp(full - jnp.max(full, axis=1, keepdims=True))
            weighed = attend_grad[at]
            inverse = 1.0 / jnp.sum(expo, axis=1, keepdims=True)
            delta = jnp.sum(expo * weighed, axis=1, keepdims=True) * inverse
            attend = expo * inverse
            score_grad = attend * (weighed - delta)
            grads.append(score_grad)
            attend_low[at] = attend.astype(BF16)
            score_low[at] = score_grad.astype(BF16)
            score_cat[:, h * n_kj * keys : (h + 1) * n_kj * keys] = score_grad.astype(BF16)
        for j in range(n_kj):
            piece = jnp.concatenate([grad[:, j * keys : (j + 1) * keys] for grad in grads], 1).astype(BF16)
            for n in range(n_noise):
                grad_send[n * n_kj + j, p] = piece[n * share : (n + 1) * share]

    def grad_copy(offset):
        return remote(
            grad_send.at[lax.bitwise_xor(me, offset)],
            grad_recv.at[offset],
            grad_sems.at[0],
            grad_sems.at[1],
            away(offset),
        )

    each(group, lambda i: grad_copy(group - i).start())

    query_all = (dot(score_cat[...], k_heads[...], 1, 0) * scale).astype(BF16)
    for j in range(n_kj):
        query_part[j] = query_all[j * q_half : (j + 1) * q_half]
    key_all = (dot(score_low[...], q_heads[...], 0, 0) * scale).astype(BF16)
    value_all = dot(attend_low[...], g_heads[...], 0, 0).astype(BF16)
    for j in range(n_kj):
        for i in range(n_qi):
            at = slice(j * keys + i * half, j * keys + (i + 1) * half)
            kv_part[i * n_kj + j, 0] = key_all[at]
            kv_part[i * n_kj + j, 1] = value_all[at]

    def query_copy(offset):
        return remote(
            query_part.at[lax.bitwise_xor(kj, offset)],
            query_recv.at[kj],
            query_send_sem.at[offset],
            query_recv_sem.at[offset],
            {"kj": lax.bitwise_xor(kj, offset)},
        )

    cell = qi * n_kj + kj

    def kv_copy(offset):
        if isinstance(offset, int):
            steps = (offset // n_kj, offset % n_kj)
        else:
            steps = (lax.div(offset, n_kj), lax.rem(offset, n_kj))
        return remote(
            kv_part.at[lax.bitwise_xor(cell, offset)],
            kv_recv.at[cell],
            kv_send_sem.at[offset],
            kv_recv_sem.at[offset],
            {"qi": lax.bitwise_xor(qi, steps[0]), "kj": lax.bitwise_xor(kj, steps[1])},
        )

    each(n_kj, lambda i: query_copy(i).start())
    each(n_qi * n_kj, lambda i: kv_copy(i).start())
    query_recv[kj] = query_part[kj]
    kv_recv[cell] = kv_part[cell]
    each(n_kj, lambda i: tile_copy(i).wait_send())
    moved(bias_all.at[others], bias_sems).wait_send()

    grad_recv[0] = grad_send[me]
    moved(grad_recv.at[others], grad_sems).wait_recv()
    for j in range(n_kj):
        total = grad_recv[j].astype(F32)
        grad_sum[lax.bitwise_xor(kj, j)] = added(
            n_noise, total, lambda n: grad_recv[n * n_kj + j].astype(F32)
        )

    head_part = jnp.zeros((HEADS, channels), F32)
    for i in range(share):
        at = slice(i * keys, (i + 1) * keys)
        grad_low = jnp.concatenate(
            [grad_sum[j, :, i, m * keys : (m + 1) * keys] for j in range(n_kj) for m in range(pack)], 0
        ).astype(BF16)
        post_scaled[at] = dot(grad_low, head_t, 0, 0)
        head_part += dot(grad_low, post_low[at], 1, 0)
    hidden_count = gate_ref.shape[1]
    tiles = hidden_count // channels

    def put(t, value):
        wave, first = place(parts_of, t * channels)
        block = w_part[wave].shape[2]
        count = channels // block
        owner = first // block
        w_part[wave][owner // group, owner % group : owner % group + count] = value.astype(BF16).reshape(
            count, block, channels
        )

    def core_copy(wave):
        return remote(
            w_part[wave].at[1 - qi], w_core[wave], pair_sems.at[2 * wave], pair_sems.at[2 * wave + 1], sibling
        )

    def w_copy(wave, offset):
        return remote(
            w_sum[wave].at[lax.bitwise_xor(me, offset)],
            w_recv[wave].at[offset],
            w_sems.at[2 * wave],
            w_sems.at[2 * wave + 1],
            away(offset),
        )

    def spread(wave):
        core_copy(wave).wait_recv()
        w_sum[wave][...] = (w_part[wave][qi].astype(F32) + w_core[wave][...].astype(F32)).astype(BF16)
        each(group, lambda i: w_copy(wave, group - i).start())

    starts = range(0, cell_count, chunk)
    second_part = jnp.zeros((1, channels), F32)
    down_part = jnp.zeros((hidden_count, channels), F32)
    for start in starts:
        at = slice(start, start + chunk)
        scaled = post_scaled[at]
        after = post_normed[at]
        second_part += jnp.sum(scaled * after, axis=0, keepdims=True)
        updated_grad = norm_backward(scaled * gain_second, after, inverses[at, 1:2])
        post_scaled[at] = updated_grad
        updated_low[at] = updated_grad.astype(BF16)
        down_part += dot(hidden_t[:, at], updated_low[at], 1, 0)
    for t in range(tiles):
        put(t, down_part[t * channels : (t + 1) * channels])
    if waves > 1:
        core_copy(0).start()

    gate_part = jnp.zeros((channels, hidden_count), F32)
    for start in starts:
        at = slice(start, start + chunk)
        hidden_grad = dot(updated_low[at], down_ref[...], 1, 1)
        gate_low = (hidden_grad * gate_coef[at]).astype(BF16)
        up_low[at] = (hidden_grad * up_coef[at]).astype(BF16)
        gate_part += dot(pre_low_t[:, at], gate_low, 1, 0)
        hidden[at] = gate_low
    for t in range(tiles):
        put(tiles + t, gate_part[:, t * channels : (t + 1) * channels])
    if waves > 1:
        core_copy(1).start()

    up_part = jnp.zeros((channels, hidden_count), F32)
    for start in starts:
        at = slice(start, start + chunk)
        up_part += dot(pre_low_t[:, at], up_low[at], 1, 0)
    for t in range(tiles):
        put(2 * tiles + t, up_part[:, t * channels : (t + 1) * channels])
    core_copy(waves - 1).start()
    for wave in range(waves):
        spread(wave)

    first_part = jnp.zeros((1, channels), F32)
    for start in starts:
        at = slice(start, start + chunk)
        pre_scaled = dot(hidden[at], gate_ref[...], 1, 1) + dot(up_low[at], up_ref[...], 1, 1)
        first_part += jnp.sum(pre_scaled * pre_normed[at], axis=0, keepdims=True)
        post_normed[at] = pre_scaled

    tail_part[0:HEADS] = head_part.astype(BF16)
    tail_part[HEADS:] = jnp.concatenate(
        (
            jnp.broadcast_to(first_part, (ALIGN // 2, channels)),
            jnp.broadcast_to(second_part, (ALIGN // 2, channels)),
        ),
        0,
    ).astype(BF16)
    owner = group // 2
    to_owner = lax.bitwise_xor(me, owner)
    tail_core_copy = remote(tail_part, tail_core, tail_sems.at[0], tail_sems.at[1], sibling)
    tail_core_copy.start()

    def tail_copy():
        device = {"noise": owner // n_kj, "kj": owner % n_kj}
        return remote(tail_sum, tail_recv.at[to_owner], tail_sems.at[2], tail_sems.at[3], device)

    def tail_back(offset):
        return remote(tail_out, tail_out, tail_sems.at[4], tail_sems.at[5], away(offset))

    def all_copy(wave, offset):
        at = weight_out[wave].at[qi, me]
        return remote(at, at, all_sems.at[2 * wave], all_sems.at[2 * wave + 1], away(offset))

    def fwd_copy(wave, core):
        at = weight_out[wave].at[core]
        return remote(at, at, fwd_send_sem.at[wave], fwd_recv_sem.at[wave], sibling)

    def pair_of(sems, wave):
        return sems.at[pl.ds(2 * wave, 2)]

    tail_core_copy.wait_recv()
    tail_sum[...] = (tail_part[...].astype(F32) + tail_core[...].astype(F32)).astype(BF16)

    @pl.when(to_owner != 0)
    def _():
        tail_copy().start()

    for start in starts:
        at = slice(start, start + chunk)
        inputs_grad = norm_backward(post_normed[at] * gain_first, pre_normed[at], inverses[at, 0:1])
        pair_out[at] = (post_scaled[at] + inputs_grad).astype(BF16)

    each(n_kj, lambda i: query_copy(i).wait_recv())
    each(n_qi * n_kj, lambda i: kv_copy(i).wait_recv())
    for j in range(n_kj):
        at = slice(j * part, (j + 1) * part)
        query_out[:, at] = query_recv[j]
        for out, which in ((key_out, 0), (value_out, 1)):
            total = kv_recv[j, which].astype(F32)
            for i in range(1, n_qi):
                total += kv_recv[i * n_kj + j, which].astype(F32)
            out[:, at] = total.astype(BF16)

    each(n_kj, lambda i: query_copy(i).wait_send())
    each(n_qi * n_kj, lambda i: kv_copy(i).wait_send())
    moved(grad_recv.at[others], grad_sems).wait_send()
    for wave in range(waves):
        core_copy(wave).wait_send()
    tail_core_copy.wait_send()

    for wave in range(waves):
        moved(w_recv[wave].at[others], pair_of(w_sems, wave)).wait_recv()
        total = added(group, w_sum[wave][me].astype(F32), lambda i: w_recv[wave][i].astype(F32))
        weight_out[wave][qi, me] = (total * (1.0 / (rows * n_qi))).astype(BF16)
        each(group, lambda i: all_copy(wave, group - i).start())

    @pl.when(to_owner == 0)
    def _():
        moved(tail_recv.at[others], tail_sems.at[pl.ds(2, 2)]).wait_recv()
        total = added(group, tail_sum[...].astype(F32), lambda i: tail_recv[i].astype(F32))
        tail_out[...] = (total * (1.0 / (rows * n_qi))).astype(BF16)
        each(group, lambda i: tail_back(group - i).start())

    for wave in range(waves):
        moved(w_recv[wave].at[others], pair_of(w_sems, wave)).wait_send()
    for wave in range(waves):
        moved(weight_out[wave].at[qi, others], pair_of(all_sems, wave)).wait_recv()
        fwd_copy(wave, qi).start()

    @pl.when(to_owner != 0)
    def _():
        remote(tail_out, tail_out, tail_sems.at[4], tail_sems.at[5], sibling).wait_recv()
        tail_copy().wait_send()

    @pl.when(to_owner == 0)
    def _():
        moved(tail_recv.at[others], tail_sems.at[pl.ds(4, 2)]).wait_send()

    for wave in range(waves):
        moved(weight_out[wave].at[qi, others], pair_of(all_sems, wave)).wait_send()
    for wave in range(waves):
        fwd_copy(wave, 1 - qi).wait_recv()
        fwd_copy(wave, qi).wait_send()


def finish(
    hidden_count,
    parts_of,
    group,
    tail_ref,
    query_ref,
    key_ref,
    value_ref,
    pair_ref,
    query_out,
    key_out,
    value_out,
    pair_out,
    gate_out,
    up_out,
    down_out,
    head_out,
    first_out,
    second_out,
    gate_wide,
    up_wide,
    down_wide,
    head_wide,
    first_wide,
    second_wide,
    sems,
    weight_ref,
):
    copies = []

    def store(src, dst):
        copy = pltpu.make_async_copy(src, dst, sems.at[len(copies)])
        copy.start()
        copies.append(copy)

    store(pair_ref, pair_out)
    store(query_ref, query_out)
    store(key_ref, key_out)
    store(value_ref, value_out)
    channels = tail_ref.shape[1]
    tiles = hidden_count // channels

    def tile(t):
        wave, first = place(parts_of, t * channels)
        block = weight_ref[wave].shape[2]
        count = channels // block
        owner = first // block
        value = weight_ref[wave][owner // group, owner % group : owner % group + count]
        return value.astype(F32).reshape(channels, channels)

    for t in range(tiles):
        down_wide[t * channels : (t + 1) * channels] = tile(t)
    store(down_wide, down_out)
    for t in range(tiles):
        gate_wide[:, t * channels : (t + 1) * channels] = tile(tiles + t)
    store(gate_wide, gate_out)
    for t in range(tiles):
        up_wide[:, t * channels : (t + 1) * channels] = tile(2 * tiles + t)
    store(up_wide, up_out)
    tail = tail_ref[...].astype(F32)
    head_wide[...] = tail[0:HEADS]
    store(head_wide, head_out)
    first_wide[...] = tail[HEADS : HEADS + 1]
    second_wide[...] = tail[HEADS + ALIGN // 2 : HEADS + ALIGN // 2 + 1]
    store(first_wide, first_out)
    store(second_wide, second_out)
    for copy in copies:
        copy.wait()


def local(
    mesh_shape,
    pair_rep,
    query_rows,
    key_rows,
    value_rows,
    output_grad,
    gain_first,
    gate_weight,
    up_weight,
    down_weight,
    gain_second,
    head_weight,
):
    n_noise, n_qi, n_kj = mesh_shape
    rows, block_count, block_rows, channels = pair_rep.shape
    keys = block_count * block_rows
    width = query_rows.shape[2]
    share = rows // n_noise
    count = share * keys
    group = n_noise * n_kj
    hidden_count = gate_weight.shape[1]
    devices = n_qi * group
    if hidden_count % (BLOCK * devices) == 0:
        parts_of = (hidden_count, hidden_count, hidden_count)
    else:
        parts_of = (3 * hidden_count,)
    waves = tuple(
        (n_qi, group, -(-part // (BLOCK * devices)) * BLOCK, channels) for part in parts_of
    )
    tail_shape = (HEADS + ALIGN, channels)
    half = keys // n_qi
    q_half = rows // n_kj
    sizes = (n_noise, n_qi, n_kj, rows, keys, share, parts_of)
    own = HEADS // n_kj
    part = own * HEAD_DIM
    pack = min(own, max(1, LANES // keys))
    vmem = pl.BlockSpec(memory_space=pltpu.VMEM)
    dma = pltpu.SemaphoreType.DMA

    scratch = [
        pltpu.VMEM((rows, width), BF16),
        pltpu.VMEM((keys, width), BF16),
        pltpu.VMEM((keys, width), BF16),
        pltpu.VMEM((rows, width), BF16),
        pltpu.VMEM((1, channels), F32),
        pltpu.VMEM((channels, hidden_count), BF16),
        pltpu.VMEM((channels, hidden_count), BF16),
        pltpu.VMEM((hidden_count, channels), BF16),
        pltpu.VMEM((1, channels), F32),
        pltpu.VMEM((HEADS, channels), BF16),
        pltpu.VMEM((share, block_count, block_rows, channels), BF16),
        pltpu.VMEM((count, channels), F32),
        pltpu.VMEM((count, channels), BF16),
        pltpu.VMEM((channels, count), BF16),
        pltpu.VMEM((count, hidden_count), F32),
        pltpu.VMEM((count, hidden_count), F32),
        pltpu.VMEM((count, hidden_count), BF16),
        pltpu.VMEM((hidden_count, count), BF16),
        pltpu.VMEM((count, hidden_count), BF16),
        pltpu.VMEM((count, channels), BF16),
        pltpu.VMEM((count, channels), F32),
        pltpu.VMEM((count, channels), BF16),
        pltpu.VMEM((count, 128), F32),
        pltpu.VMEM((share, HEADS, keys), F32),
        pltpu.VMEM((n_kj, own // pack, share, pack * keys), BF16),
        pltpu.VMEM((group, own // pack, share, pack * keys), BF16),
        pltpu.VMEM((n_kj, rows, part), BF16),
        pltpu.VMEM((n_kj, rows, part), BF16),
        pltpu.VMEM((n_kj, 2, keys, part), BF16),
        pltpu.VMEM((n_kj, 2, keys, part), BF16),
        pltpu.VMEM((own * rows, part), BF16),
        pltpu.VMEM((own * rows, part), BF16),
        pltpu.VMEM((own * n_kj * keys, part), BF16),
        pltpu.VMEM((own * rows, n_kj * keys), F32),
        pltpu.VMEM((own * rows, n_kj * keys), F32),
        pltpu.VMEM((own * rows, n_kj * keys), BF16),
        pltpu.VMEM((own * rows, n_kj * keys), BF16),
        pltpu.VMEM((rows, own * n_kj * keys), BF16),
        pltpu.VMEM((group, own // pack, share, pack * keys), BF16),
        pltpu.VMEM((group, own // pack, share, pack * keys), BF16),
        pltpu.VMEM((n_kj, own // pack, share, pack * keys), F32),
        pltpu.VMEM((count, channels), F32),
        pltpu.VMEM((n_kj, q_half, part), BF16),
        pltpu.VMEM((n_kj, q_half, part), BF16),
        pltpu.VMEM((n_qi * n_kj, 2, half, part), BF16),
        pltpu.VMEM((n_qi * n_kj, 2, half, part), BF16),
        pltpu.VMEM(tail_shape, BF16),
        pltpu.VMEM(tail_shape, BF16),
        pltpu.VMEM(tail_shape, BF16),
        pltpu.VMEM((group, *tail_shape), BF16),
        dma((11,)),
        dma((2,)),
        dma((n_kj,)),
        dma((n_kj,)),
        dma((2,)),
        dma((n_kj,)),
        dma((n_kj,)),
        dma((n_qi * n_kj,)),
        dma((n_qi * n_kj,)),
        dma((2 * len(waves),)),
        dma((2 * len(waves),)),
        dma((2 * len(waves),)),
        dma((len(waves),)),
        dma((len(waves),)),
        dma((6,)),
    ]
    wave_scratch = [
        [pltpu.VMEM(wave[skip:], BF16) for wave in waves] for skip in (0, 1, 1, 1)
    ]
    scratch += sum(wave_scratch, [])

    def run(*refs):
        count = len(waves)
        outs = refs[16 : 16 + count]
        rest = refs[16 + count :]
        groups = [rest[len(rest) - (4 - i) * count : len(rest) - (3 - i) * count] for i in range(4)]
        kernel(sizes, *refs[:16], *rest[: len(rest) - 4 * count], outs, *groups)

    held = sum(
        math.prod(x.shape) * jnp.dtype(x.dtype).itemsize for x in scratch if x.memory_space == pltpu.VMEM
    )
    hbm = pl.BlockSpec(memory_space=pltpu.HBM)
    query_grad, key_grad, value_grad, pair_grad, tail, *weights = pl.pallas_call(
        run,
        out_shape=(
            jax.ShapeDtypeStruct((q_half, width), BF16),
            jax.ShapeDtypeStruct((half, width), BF16),
            jax.ShapeDtypeStruct((half, width), BF16),
            jax.ShapeDtypeStruct((count, channels), BF16),
            jax.ShapeDtypeStruct(tail_shape, BF16),
            *(jax.ShapeDtypeStruct(wave, BF16) for wave in waves),
        ),
        in_specs=[hbm] * 11,
        out_specs=(vmem,) * (5 + len(waves)),
        scratch_shapes=scratch,
        compiler_params=pltpu.CompilerParams(
            collective_id=0, has_side_effects=True, vmem_limit_bytes=held + held // 8 + 4 * 1024 * 1024
        ),
        name="block_backward",
    )(
        *(
            pltpu.with_memory_space_constraint(x, pltpu.HBM)
            for x in (
                pair_rep,
                query_rows.reshape(rows, width),
                key_rows.reshape(keys, width),
                value_rows.reshape(keys, width),
                output_grad.reshape(rows, width),
                gain_first.reshape(1, channels),
                gate_weight,
                up_weight,
                down_weight,
                gain_second.reshape(1, channels),
                head_weight.T,
            )
        )
    )
    outputs = (query_grad, key_grad, value_grad, pair_grad)

    def finish_all(*refs):
        count = len(waves)
        finish(hidden_count, parts_of, group, *refs[:5], *refs[5 + count :], refs[5 : 5 + count])

    query_grad, key_grad, value_grad, pair_grad, gate_grad, up_grad, down_grad, head_grad, first_grad, second_grad = pl.pallas_call(
        finish_all,
        out_shape=tuple(jax.ShapeDtypeStruct(x.shape, x.dtype) for x in outputs)
        + (
            jax.ShapeDtypeStruct((channels, hidden_count), F32),
            jax.ShapeDtypeStruct((channels, hidden_count), F32),
            jax.ShapeDtypeStruct((hidden_count, channels), F32),
            jax.ShapeDtypeStruct((HEADS, channels), F32),
            jax.ShapeDtypeStruct((1, channels), F32),
            jax.ShapeDtypeStruct((1, channels), F32),
        ),
        in_specs=[vmem] * (5 + len(waves)),
        out_specs=(hbm,) * 10,
        scratch_shapes=[
            pltpu.VMEM((channels, hidden_count), F32),
            pltpu.VMEM((channels, hidden_count), F32),
            pltpu.VMEM((hidden_count, channels), F32),
            pltpu.VMEM((HEADS, channels), F32),
            pltpu.VMEM((1, channels), F32),
            pltpu.VMEM((1, channels), F32),
            dma((10,)),
        ],
        compiler_params=pltpu.CompilerParams(vmem_limit_bytes=8 * 1024 * 1024),
        name="finish_weights",
    )(tail, *outputs, *weights)
    return (
        query_grad[None],
        key_grad[None],
        value_grad[None],
        pair_grad.reshape(1, 1, share, block_count, block_rows, channels),
        gate_grad,
        up_grad,
        down_grad,
        head_grad.T,
        first_grad.reshape(channels),
        second_grad.reshape(channels),
    )


def solution(mesh):
    mesh_shape = (mesh.shape["noise"], mesh.shape["qi"], mesh.shape["kj"])
    return jax.shard_map(
        functools.partial(local, mesh_shape),
        mesh=mesh,
        in_specs=(
            P("qi", None, "kj", None),
            P("noise", "qi", None),
            P("noise", None, "kj", None),
            P("noise", None, "kj", None),
            P("noise", "qi", None),
            P(),
            P(),
            P(),
            P(),
            P(),
            P(),
        ),
        out_specs=(
            P("noise", ("qi", "kj"), None),
            P("noise", ("qi", "kj"), None),
            P("noise", ("qi", "kj"), None),
            P("qi", "noise", None, None, "kj", None),
            P(),
            P(),
            P(),
            P(),
            P(),
            P(),
        ),
        check_vma=False,
    )
```

```python
import functools
import math

import jax
import jax.numpy as jnp
from jax import lax
from jax.experimental import pallas as pl
from jax.experimental.pallas import tpu as pltpu
from jax.sharding import PartitionSpec as P

HEADS = 16
HEAD_DIM = 48
ALIGN = 8
BLOCK = 16
UNROLLED = 16
LANES = 128

epsilon = 1e-05
F32 = jnp.float32
BF16 = jnp.bfloat16
MESH = pl.DeviceIdType.MESH


def dot(left, right, left_dim, right_dim):
    return lax.dot_general(
        left, right, (((left_dim,), (right_dim,)), ((), ())), preferred_element_type=F32
    )


def normalize(values):
    center = values - jnp.mean(values, axis=1, keepdims=True)
    inverse = lax.rsqrt(jnp.mean(center * center, axis=1, keepdims=True) + epsilon)
    return center * inverse, inverse


def norm_backward(normed_grad, normed, inverse):
    first_mean = jnp.mean(normed_grad, axis=1, keepdims=True)
    second_mean = jnp.mean(normed_grad * normed, axis=1, keepdims=True)
    return inverse * (normed_grad - first_mean - normed * second_mean)


def place(parts_of, row):
    wave = 0
    while row >= parts_of[wave]:
        row -= parts_of[wave]
        wave += 1
    return wave, row


def kernel(
    sizes,
    pair_hbm,
    q_hbm,
    k_hbm,
    v_hbm,
    g_hbm,
    gain_first_hbm,
    gate_hbm,
    up_hbm,
    down_hbm,
    gain_second_hbm,
    head_hbm,
    query_out,
    key_out,
    value_out,
    pair_out,
    tail_out,
    q_ref,
    k_ref,
    v_ref,
    g_ref,
    gain_first_ref,
    gate_ref,
    up_ref,
    down_ref,
    gain_second_ref,
    head_ref,
    cells,
    pre_normed,
    pre_low,
    pre_low_t,
    gate_coef,
    up_coef,
    hidden,
    hidden_t,
    up_low,
    updated_low,
    post_normed,
    post_low,
    inverses,
    bias_rows,
    bias_send,
    bias_all,
    q_cols,
    g_cols,
    kv_send,
    kv_all,
    q_heads,
    g_heads,
    k_heads,
    score,
    attend_grad,
    score_low,
    attend_low,
    score_cat,
    grad_send,
    grad_recv,
    grad_sum,
    post_scaled,
    query_part,
    query_recv,
    kv_part,
    kv_recv,
    tail_part,
    tail_core,
    tail_sum,
    tail_recv,
    input_sems,
    bias_sems,
    tile_send_sem,
    tile_recv_sem,
    grad_sems,
    query_send_sem,
    query_recv_sem,
    kv_send_sem,
    kv_recv_sem,
    pair_sems,
    w_sems,
    all_sems,
    fwd_send_sem,
    fwd_recv_sem,
    tail_sems,
    weight_out,
    w_part,
    w_core,
    w_sum,
    w_recv,
):
    n_noise, n_qi, n_kj, rows, keys, share, parts_of = sizes
    waves = len(parts_of)
    group = n_noise * n_kj
    cell_count = share * keys
    chunk = min(256, cell_count)
    scale = HEAD_DIM ** (-0.5)
    noise = lax.axis_index("noise")
    qi = lax.axis_index("qi")
    kj = lax.axis_index("kj")
    me = noise * n_kj + kj
    sibling = {"qi": 1 - qi}
    channels = cells.shape[-1]
    width = q_ref.shape[-1]
    half = keys // n_qi
    q_half = rows // n_kj
    own = HEADS // n_kj
    part = own * HEAD_DIM
    pack = min(own, max(1, LANES // keys))
    packed = own // pack

    def members(p):
        return [p + j * packed for j in range(pack)]

    def remote(src, dst, send, recv, device):
        return pltpu.make_async_remote_copy(
            src_ref=src, dst_ref=dst, send_sem=send, recv_sem=recv, device_id=device, device_id_type=MESH
        )

    def away(offset):
        if isinstance(offset, int):
            steps = (offset // n_kj, offset % n_kj)
            return {
                name: lax.bitwise_xor(at, step) for name, at, step in zip(("noise", "kj"), (noise, kj), steps) if step
            }
        return {
            "noise": lax.bitwise_xor(noise, lax.div(offset, n_kj)),
            "kj": lax.bitwise_xor(kj, lax.rem(offset, n_kj)),
        }

    def each(count, body):
        if count <= UNROLLED:
            for i in range(1, count):
                body(i)
            return

        def step(i, carry):
            body(i)
            return carry

        lax.fori_loop(1, count, step, 0)

    def added(count, total, term):
        if count <= UNROLLED:
            for i in range(1, count):
                total += term(i)
            return total
        return lax.fori_loop(1, count, lambda i, total: total + term(i), total)

    def moved(view, sems):
        return remote(view, view, sems.at[0], sems.at[1], sibling)

    forward_loads = [
        pltpu.make_async_copy(src, dst, input_sems.at[i])
        for i, (src, dst) in enumerate(
            (
                (pair_hbm.at[pl.ds(noise * share, share)], cells),
                (gain_first_hbm, gain_first_ref),
                (gate_hbm, gate_ref),
                (up_hbm, up_ref),
                (down_hbm, down_ref),
                (gain_second_hbm, gain_second_ref),
                (head_hbm, head_ref),
            )
        )
    ]
    attention_loads = [
        pltpu.make_async_copy(src, dst, input_sems.at[len(forward_loads) + i])
        for i, (src, dst) in enumerate(((q_hbm, q_ref), (k_hbm, k_ref), (g_hbm, g_ref), (v_hbm, v_ref)))
    ]
    for load in forward_loads:
        load.start()

    barrier = pltpu.get_barrier_semaphore()

    def greet(device):
        pl.semaphore_signal(barrier, inc=1, device_id=device, device_id_type=MESH)

    each(group, lambda i: greet(away(group - i)))
    greet(sibling)
    for load in attention_loads:
        load.start()
    for load in forward_loads:
        load.wait()

    gain_first = gain_first_ref[...]
    gain_second = gain_second_ref[...]
    head_t = head_ref[...]
    flat_cells = cells[...].reshape(cell_count, channels)
    for start in range(0, cell_count, chunk):
        at = slice(start, start + chunk)
        inputs = flat_cells[at].astype(F32)
        normed, inverse = normalize(inputs)
        lowered = (normed * gain_first).astype(BF16)
        gate_pre = dot(lowered, gate_ref[...], 1, 0)
        up_pre = dot(lowered, up_ref[...], 1, 0)
        sigmoid = jax.nn.sigmoid(gate_pre)
        silu = gate_pre * sigmoid
        low_hidden = (silu * up_pre).astype(BF16)
        updated = inputs + dot(low_hidden, down_ref[...], 1, 0)
        after, after_inverse = normalize(updated)
        after_low = (after * gain_second).astype(BF16)
        pre_normed[at] = normed
        pre_low[at] = lowered
        gate_coef[at] = up_pre * sigmoid * (1.0 + gate_pre * (1.0 - sigmoid))
        up_coef[at] = silu
        hidden[at] = low_hidden
        post_normed[at] = after
        post_low[at] = after_low
        inverses[at, 0:1] = inverse
        inverses[at, 1:2] = after_inverse
    for i in range(share):
        bias_rows[i] = dot(head_t, post_low[i * keys : (i + 1) * keys], 1, 1)
    for j in range(n_kj):
        for p in range(packed):
            bias_send[j, p] = jnp.concatenate([bias_rows[:, j * own + h, :] for h in members(p)], 1).astype(BF16)

    for load in attention_loads:
        load.wait()
    for j in range(n_kj):
        at = slice(j * part, (j + 1) * part)
        q_cols[j] = q_ref[:, at]
        g_cols[j] = g_ref[:, at]
        kv_send[j, 0] = k_ref[:, at]
        kv_send[j, 1] = v_ref[:, at]

    pl.semaphore_wait(barrier, group)

    def tile_copy(offset):
        return remote(
            kv_send.at[lax.bitwise_xor(kj, offset)],
            kv_all.at[kj],
            tile_send_sem.at[offset],
            tile_recv_sem.at[offset],
            {"kj": lax.bitwise_xor(kj, offset)},
        )

    def bias_copy(offset):
        return remote(
            bias_send.at[lax.bitwise_xor(kj, lax.rem(offset, n_kj))],
            bias_all.at[me],
            bias_sems.at[0],
            bias_sems.at[1],
            away(offset),
        )

    each(n_kj, lambda i: tile_copy(i).start())
    each(group, lambda i: bias_copy(group - i).start())

    kv_all[kj] = kv_send[kj]
    bias_all[me] = bias_send[kj]
    lane = lax.broadcasted_iota(jnp.int32, (1, part), 1)

    def mask(h):
        inside = jnp.logical_and(lane >= h * HEAD_DIM, lane < (h + 1) * HEAD_DIM)
        return jnp.where(inside, 1.0, 0.0).astype(BF16)

    q_own = q_cols[kj]
    g_own = g_cols[kj]
    for h in range(own):
        at = slice(h * rows, (h + 1) * rows)
        q_heads[at] = q_own * mask(h)
        g_heads[at] = g_own * mask(h)
    hidden_t[...] = hidden[...].T
    pre_low_t[...] = pre_low[...].T
    for wave, count in enumerate(parts_of):
        if count < math.prod(w_part[wave].shape[:3]):
            w_part[wave][...] = jnp.zeros(w_part[wave].shape, BF16)

    each(n_kj, lambda i: tile_copy(i).wait_recv())
    k_own = kv_all[:, 0].reshape(n_kj * keys, part)
    v_own = kv_all[:, 1].reshape(n_kj * keys, part)
    score[...] = dot(q_heads[...], k_own, 1, 1) * scale
    attend_grad[...] = dot(g_heads[...], v_own, 1, 1)
    for h in range(own):
        k_heads[h * n_kj * keys : (h + 1) * n_kj * keys] = k_own * mask(h)

    others = pl.ds(1, group - 1)
    moved(bias_all.at[others], bias_sems).wait_recv()

    for p in range(packed):
        blocks = [
            jnp.concatenate([bias_all[n * n_kj + j, p] for n in range(n_noise)], 0).astype(F32) for j in range(n_kj)
        ]
        grads = []
        for i, h in enumerate(members(p)):
            at = slice(h * rows, (h + 1) * rows)
            full = score[at] + jnp.concatenate([block[:, i * keys : (i + 1) * keys] for block in blocks], 1)
            expo = jnp.exp(full - jnp.max(full, axis=1, keepdims=True))
            weighed = attend_grad[at]
            inverse = 1.0 / jnp.sum(expo, axis=1, keepdims=True)
            delta = jnp.sum(expo * weighed, axis=1, keepdims=True) * inverse
            attend = expo * inverse
            score_grad = attend * (weighed - delta)
            grads.append(score_grad)
            attend_low[at] = attend.astype(BF16)
            score_low[at] = score_grad.astype(BF16)
            score_cat[:, h * n_kj * keys : (h + 1) * n_kj * keys] = score_grad.astype(BF16)
        for j in range(n_kj):
            piece = jnp.concatenate([grad[:, j * keys : (j + 1) * keys] for grad in grads], 1).astype(BF16)
            for n in range(n_noise):
                grad_send[n * n_kj + j, p] = piece[n * share : (n + 1) * share]

    def grad_copy(offset):
        return remote(
            grad_send.at[lax.bitwise_xor(me, offset)],
            grad_recv.at[offset],
            grad_sems.at[0],
            grad_sems.at[1],
            away(offset),
        )

    each(group, lambda i: grad_copy(group - i).start())

    query_all = (dot(score_cat[...], k_heads[...], 1, 0) * scale).astype(BF16)
    for j in range(n_kj):
        query_part[j] = query_all[j * q_half : (j + 1) * q_half]
    key_all = (dot(score_low[...], q_heads[...], 0, 0) * scale).astype(BF16)
    value_all = dot(attend_low[...], g_heads[...], 0, 0).astype(BF16)
    for j in range(n_kj):
        for i in range(n_qi):
            at = slice(j * keys + i * half, j * keys + (i + 1) * half)
            kv_part[i * n_kj + j, 0] = key_all[at]
            kv_part[i * n_kj + j, 1] = value_all[at]

    def query_copy(offset):
        return remote(
            query_part.at[lax.bitwise_xor(kj, offset)],
            query_recv.at[kj],
            query_send_sem.at[offset],
            query_recv_sem.at[offset],
            {"kj": lax.bitwise_xor(kj, offset)},
        )

    cell = qi * n_kj + kj

    def kv_copy(offset):
        if isinstance(offset, int):
            steps = (offset // n_kj, offset % n_kj)
        else:
            steps = (lax.div(offset, n_kj), lax.rem(offset, n_kj))
        return remote(
            kv_part.at[lax.bitwise_xor(cell, offset)],
            kv_recv.at[cell],
            kv_send_sem.at[offset],
            kv_recv_sem.at[offset],
            {"qi": lax.bitwise_xor(qi, steps[0]), "kj": lax.bitwise_xor(kj, steps[1])},
        )

    each(n_kj, lambda i: query_copy(i).start())
    each(n_qi * n_kj, lambda i: kv_copy(i).start())
    query_recv[kj] = query_part[kj]
    kv_recv[cell] = kv_part[cell]
    each(n_kj, lambda i: tile_copy(i).wait_send())
    moved(bias_all.at[others], bias_sems).wait_send()

    grad_recv[0] = grad_send[me]
    moved(grad_recv.at[others], grad_sems).wait_recv()
    for j in range(n_kj):
        total = grad_recv[j].astype(F32)
        grad_sum[lax.bitwise_xor(kj, j)] = added(
            n_noise, total, lambda n: grad_recv[n * n_kj + j].astype(F32)
        )

    head_part = jnp.zeros((HEADS, channels), F32)
    for i in range(share):
        at = slice(i * keys, (i + 1) * keys)
        grad_low = jnp.concatenate(
            [grad_sum[j, :, i, m * keys : (m + 1) * keys] for j in range(n_kj) for m in range(pack)], 0
        ).astype(BF16)
        post_scaled[at] = dot(grad_low, head_t, 0, 0)
        head_part += dot(grad_low, post_low[at], 1, 0)
    hidden_count = gate_ref.shape[1]
    tiles = hidden_count // channels

    def put(t, value):
        wave, first = place(parts_of, t * channels)
        block = w_part[wave].shape[2]
        count = channels // block
        owner = first // block
        w_part[wave][owner // group, owner % group : owner % group + count] = value.astype(BF16).reshape(
            count, block, channels
        )

    def core_copy(wave):
        return remote(
            w_part[wave].at[1 - qi], w_core[wave], pair_sems.at[2 * wave], pair_sems.at[2 * wave + 1], sibling
        )

    def w_copy(wave, offset):
        return remote(
            w_sum[wave].at[lax.bitwise_xor(me, offset)],
            w_recv[wave].at[offset],
            w_sems.at[2 * wave],
            w_sems.at[2 * wave + 1],
            away(offset),
        )

    def spread(wave):
        core_copy(wave).wait_recv()
        w_sum[wave][...] = (w_part[wave][qi].astype(F32) + w_core[wave][...].astype(F32)).astype(BF16)
        each(group, lambda i: w_copy(wave, group - i).start())

    starts = range(0, cell_count, chunk)
    second_part = jnp.zeros((1, channels), F32)
    for start in starts:
        at = slice(start, start + chunk)
        scaled = post_scaled[at]
        after = post_normed[at]
        second_part += jnp.sum(scaled * after, axis=0, keepdims=True)
        updated_grad = norm_backward(scaled * gain_second, after, inverses[at, 1:2])
        post_scaled[at] = updated_grad
        updated_low[at] = updated_grad.astype(BF16)
    down_part = dot(hidden_t[...], updated_low[...], 1, 0)
    for t in range(tiles):
        put(t, down_part[t * channels : (t + 1) * channels])
    if waves > 1:
        core_copy(0).start()

    for start in starts:
        at = slice(start, start + chunk)
        hidden_grad = dot(updated_low[at], down_ref[...], 1, 1)
        gate_low = (hidden_grad * gate_coef[at]).astype(BF16)
        up_low[at] = (hidden_grad * up_coef[at]).astype(BF16)
        hidden[at] = gate_low
    gate_part = dot(pre_low_t[...], hidden[...], 1, 0)
    for t in range(tiles):
        put(tiles + t, gate_part[:, t * channels : (t + 1) * channels])
    if waves > 1:
        core_copy(1).start()

    up_part = dot(pre_low_t[...], up_low[...], 1, 0)
    for t in range(tiles):
        put(2 * tiles + t, up_part[:, t * channels : (t + 1) * channels])
    core_copy(waves - 1).start()
    for wave in range(waves):
        spread(wave)

    first_part = jnp.zeros((1, channels), F32)
    for start in starts:
        at = slice(start, start + chunk)
        pre_scaled = dot(hidden[at], gate_ref[...], 1, 1) + dot(up_low[at], up_ref[...], 1, 1)
        first_part += jnp.sum(pre_scaled * pre_normed[at], axis=0, keepdims=True)
        post_normed[at] = pre_scaled

    tail_part[0:HEADS] = head_part.astype(BF16)
    tail_part[HEADS:] = jnp.concatenate(
        (
            jnp.broadcast_to(first_part, (ALIGN // 2, channels)),
            jnp.broadcast_to(second_part, (ALIGN // 2, channels)),
        ),
        0,
    ).astype(BF16)
    owner = group // 2
    to_owner = lax.bitwise_xor(me, owner)
    tail_core_copy = remote(tail_part, tail_core, tail_sems.at[0], tail_sems.at[1], sibling)
    tail_core_copy.start()

    def tail_copy():
        device = {"noise": owner // n_kj, "kj": owner % n_kj}
        return remote(tail_sum, tail_recv.at[to_owner], tail_sems.at[2], tail_sems.at[3], device)

    def tail_back(offset):
        return remote(tail_out, tail_out, tail_sems.at[4], tail_sems.at[5], away(offset))

    def all_copy(wave, offset):
        at = weight_out[wave].at[qi, me]
        return remote(at, at, all_sems.at[2 * wave], all_sems.at[2 * wave + 1], away(offset))

    def fwd_copy(wave, core):
        at = weight_out[wave].at[core]
        return remote(at, at, fwd_send_sem.at[wave], fwd_recv_sem.at[wave], sibling)

    def pair_of(sems, wave):
        return sems.at[pl.ds(2 * wave, 2)]

    tail_core_copy.wait_recv()
    tail_sum[...] = (tail_part[...].astype(F32) + tail_core[...].astype(F32)).astype(BF16)

    @pl.when(to_owner != 0)
    def _():
        tail_copy().start()

    for start in starts:
        at = slice(start, start + chunk)
        inputs_grad = norm_backward(post_normed[at] * gain_first, pre_normed[at], inverses[at, 0:1])
        pair_out[at] = (post_scaled[at] + inputs_grad).astype(BF16)

    each(n_kj, lambda i: query_copy(i).wait_recv())
    each(n_qi * n_kj, lambda i: kv_copy(i).wait_recv())
    for j in range(n_kj):
        at = slice(j * part, (j + 1) * part)
        query_out[:, at] = query_recv[j]
        for out, which in ((key_out, 0), (value_out, 1)):
            total = kv_recv[j, which].astype(F32)
            for i in range(1, n_qi):
                total += kv_recv[i * n_kj + j, which].astype(F32)
            out[:, at] = total.astype(BF16)

    each(n_kj, lambda i: query_copy(i).wait_send())
    each(n_qi * n_kj, lambda i: kv_copy(i).wait_send())
    moved(grad_recv.at[others], grad_sems).wait_send()
    for wave in range(waves):
        core_copy(wave).wait_send()
    tail_core_copy.wait_send()

    for wave in range(waves):
        moved(w_recv[wave].at[others], pair_of(w_sems, wave)).wait_recv()
        total = added(group, w_sum[wave][me].astype(F32), lambda i: w_recv[wave][i].astype(F32))
        weight_out[wave][qi, me] = (total * (1.0 / (rows * n_qi))).astype(BF16)
        each(group, lambda i: all_copy(wave, group - i).start())

    @pl.when(to_owner == 0)
    def _():
        moved(tail_recv.at[others], tail_sems.at[pl.ds(2, 2)]).wait_recv()
        total = added(group, tail_sum[...].astype(F32), lambda i: tail_recv[i].astype(F32))
        tail_out[...] = (total * (1.0 / (rows * n_qi))).astype(BF16)
        each(group, lambda i: tail_back(group - i).start())

    for wave in range(waves):
        moved(w_recv[wave].at[others], pair_of(w_sems, wave)).wait_send()
    for wave in range(waves):
        moved(weight_out[wave].at[qi, others], pair_of(all_sems, wave)).wait_recv()
        fwd_copy(wave, qi).start()

    @pl.when(to_owner != 0)
    def _():
        remote(tail_out, tail_out, tail_sems.at[4], tail_sems.at[5], sibling).wait_recv()
        tail_copy().wait_send()

    @pl.when(to_owner == 0)
    def _():
        moved(tail_recv.at[others], tail_sems.at[pl.ds(4, 2)]).wait_send()

    for wave in range(waves):
        moved(weight_out[wave].at[qi, others], pair_of(all_sems, wave)).wait_send()
    for wave in range(waves):
        fwd_copy(wave, 1 - qi).wait_recv()
        fwd_copy(wave, qi).wait_send()


def finish(
    hidden_count,
    parts_of,
    group,
    tail_ref,
    query_ref,
    key_ref,
    value_ref,
    pair_ref,
    query_out,
    key_out,
    value_out,
    pair_out,
    gate_out,
    up_out,
    down_out,
    head_out,
    first_out,
    second_out,
    gate_wide,
    up_wide,
    down_wide,
    head_wide,
    first_wide,
    second_wide,
    sems,
    weight_ref,
):
    copies = []

    def store(src, dst):
        copy = pltpu.make_async_copy(src, dst, sems.at[len(copies)])
        copy.start()
        copies.append(copy)

    store(pair_ref, pair_out)
    store(query_ref, query_out)
    store(key_ref, key_out)
    store(value_ref, value_out)
    channels = tail_ref.shape[1]
    tiles = hidden_count // channels

    def tile(t):
        wave, first = place(parts_of, t * channels)
        block = weight_ref[wave].shape[2]
        count = channels // block
        owner = first // block
        value = weight_ref[wave][owner // group, owner % group : owner % group + count]
        return value.astype(F32).reshape(channels, channels)

    for t in range(tiles):
        down_wide[t * channels : (t + 1) * channels] = tile(t)
    store(down_wide, down_out)
    for t in range(tiles):
        gate_wide[:, t * channels : (t + 1) * channels] = tile(tiles + t)
    store(gate_wide, gate_out)
    for t in range(tiles):
        up_wide[:, t * channels : (t + 1) * channels] = tile(2 * tiles + t)
    store(up_wide, up_out)
    tail = tail_ref[...].astype(F32)
    head_wide[...] = tail[0:HEADS]
    store(head_wide, head_out)
    first_wide[...] = tail[HEADS : HEADS + 1]
    second_wide[...] = tail[HEADS + ALIGN // 2 : HEADS + ALIGN // 2 + 1]
    store(first_wide, first_out)
    store(second_wide, second_out)
    for copy in copies:
        copy.wait()


def local(
    mesh_shape,
    pair_rep,
    query_rows,
    key_rows,
    value_rows,
    output_grad,
    gain_first,
    gate_weight,
    up_weight,
    down_weight,
    gain_second,
    head_weight,
):
    n_noise, n_qi, n_kj = mesh_shape
    rows, block_count, block_rows, channels = pair_rep.shape
    keys = block_count * block_rows
    width = query_rows.shape[2]
    share = rows // n_noise
    count = share * keys
    group = n_noise * n_kj
    hidden_count = gate_weight.shape[1]
    devices = n_qi * group
    if hidden_count % (BLOCK * devices) == 0:
        parts_of = (hidden_count, hidden_count, hidden_count)
    else:
        parts_of = (3 * hidden_count,)
    waves = tuple(
        (n_qi, group, -(-part // (BLOCK * devices)) * BLOCK, channels) for part in parts_of
    )
    tail_shape = (HEADS + ALIGN, channels)
    half = keys // n_qi
    q_half = rows // n_kj
    sizes = (n_noise, n_qi, n_kj, rows, keys, share, parts_of)
    own = HEADS // n_kj
    part = own * HEAD_DIM
    pack = min(own, max(1, LANES // keys))
    vmem = pl.BlockSpec(memory_space=pltpu.VMEM)
    dma = pltpu.SemaphoreType.DMA

    scratch = [
        pltpu.VMEM((rows, width), BF16),
        pltpu.VMEM((keys, width), BF16),
        pltpu.VMEM((keys, width), BF16),
        pltpu.VMEM((rows, width), BF16),
        pltpu.VMEM((1, channels), F32),
        pltpu.VMEM((channels, hidden_count), BF16),
        pltpu.VMEM((channels, hidden_count), BF16),
        pltpu.VMEM((hidden_count, channels), BF16),
        pltpu.VMEM((1, channels), F32),
        pltpu.VMEM((HEADS, channels), BF16),
        pltpu.VMEM((share, block_count, block_rows, channels), BF16),
        pltpu.VMEM((count, channels), F32),
        pltpu.VMEM((count, channels), BF16),
        pltpu.VMEM((channels, count), BF16),
        pltpu.VMEM((count, hidden_count), F32),
        pltpu.VMEM((count, hidden_count), F32),
        pltpu.VMEM((count, hidden_count), BF16),
        pltpu.VMEM((hidden_count, count), BF16),
        pltpu.VMEM((count, hidden_count), BF16),
        pltpu.VMEM((count, channels), BF16),
        pltpu.VMEM((count, channels), F32),
        pltpu.VMEM((count, channels), BF16),
        pltpu.VMEM((count, 128), F32),
        pltpu.VMEM((share, HEADS, keys), F32),
        pltpu.VMEM((n_kj, own // pack, share, pack * keys), BF16),
        pltpu.VMEM((group, own // pack, share, pack * keys), BF16),
        pltpu.VMEM((n_kj, rows, part), BF16),
        pltpu.VMEM((n_kj, rows, part), BF16),
        pltpu.VMEM((n_kj, 2, keys, part), BF16),
        pltpu.VMEM((n_kj, 2, keys, part), BF16),
        pltpu.VMEM((own * rows, part), BF16),
        pltpu.VMEM((own * rows, part), BF16),
        pltpu.VMEM((own * n_kj * keys, part), BF16),
        pltpu.VMEM((own * rows, n_kj * keys), F32),
        pltpu.VMEM((own * rows, n_kj * keys), F32),
        pltpu.VMEM((own * rows, n_kj * keys), BF16),
        pltpu.VMEM((own * rows, n_kj * keys), BF16),
        pltpu.VMEM((rows, own * n_kj * keys), BF16),
        pltpu.VMEM((group, own // pack, share, pack * keys), BF16),
        pltpu.VMEM((group, own // pack, share, pack * keys), BF16),
        pltpu.VMEM((n_kj, own // pack, share, pack * keys), F32),
        pltpu.VMEM((count, channels), F32),
        pltpu.VMEM((n_kj, q_half, part), BF16),
        pltpu.VMEM((n_kj, q_half, part), BF16),
        pltpu.VMEM((n_qi * n_kj, 2, half, part), BF16),
        pltpu.VMEM((n_qi * n_kj, 2, half, part), BF16),
        pltpu.VMEM(tail_shape, BF16),
        pltpu.VMEM(tail_shape, BF16),
        pltpu.VMEM(tail_shape, BF16),
        pltpu.VMEM((group, *tail_shape), BF16),
        dma((11,)),
        dma((2,)),
        dma((n_kj,)),
        dma((n_kj,)),
        dma((2,)),
        dma((n_kj,)),
        dma((n_kj,)),
        dma((n_qi * n_kj,)),
        dma((n_qi * n_kj,)),
        dma((2 * len(waves),)),
        dma((2 * len(waves),)),
        dma((2 * len(waves),)),
        dma((len(waves),)),
        dma((len(waves),)),
        dma((6,)),
    ]
    wave_scratch = [
        [pltpu.VMEM(wave[skip:], BF16) for wave in waves] for skip in (0, 1, 1, 1)
    ]
    scratch += sum(wave_scratch, [])

    def run(*refs):
        count = len(waves)
        outs = refs[16 : 16 + count]
        rest = refs[16 + count :]
        groups = [rest[len(rest) - (4 - i) * count : len(rest) - (3 - i) * count] for i in range(4)]
        kernel(sizes, *refs[:16], *rest[: len(rest) - 4 * count], outs, *groups)

    held = sum(
        math.prod(x.shape) * jnp.dtype(x.dtype).itemsize for x in scratch if x.memory_space == pltpu.VMEM
    )
    hbm = pl.BlockSpec(memory_space=pltpu.HBM)
    query_grad, key_grad, value_grad, pair_grad, tail, *weights = pl.pallas_call(
        run,
        out_shape=(
            jax.ShapeDtypeStruct((q_half, width), BF16),
            jax.ShapeDtypeStruct((half, width), BF16),
            jax.ShapeDtypeStruct((half, width), BF16),
            jax.ShapeDtypeStruct((count, channels), BF16),
            jax.ShapeDtypeStruct(tail_shape, BF16),
            *(jax.ShapeDtypeStruct(wave, BF16) for wave in waves),
        ),
        in_specs=[hbm] * 11,
        out_specs=(vmem,) * (5 + len(waves)),
        scratch_shapes=scratch,
        compiler_params=pltpu.CompilerParams(
            collective_id=0, has_side_effects=True, vmem_limit_bytes=held + held // 8 + 4 * 1024 * 1024
        ),
        name="block_backward",
    )(
        *(
            pltpu.with_memory_space_constraint(x, pltpu.HBM)
            for x in (
                pair_rep,
                query_rows.reshape(rows, width),
                key_rows.reshape(keys, width),
                value_rows.reshape(keys, width),
                output_grad.reshape(rows, width),
                gain_first.reshape(1, channels),
                gate_weight,
                up_weight,
                down_weight,
                gain_second.reshape(1, channels),
                head_weight.T,
            )
        )
    )
    outputs = (query_grad, key_grad, value_grad, pair_grad)

    def finish_all(*refs):
        count = len(waves)
        finish(hidden_count, parts_of, group, *refs[:5], *refs[5 + count :], refs[5 : 5 + count])

    query_grad, key_grad, value_grad, pair_grad, gate_grad, up_grad, down_grad, head_grad, first_grad, second_grad = pl.pallas_call(
        finish_all,
        out_shape=tuple(jax.ShapeDtypeStruct(x.shape, x.dtype) for x in outputs)
        + (
            jax.ShapeDtypeStruct((channels, hidden_count), F32),
            jax.ShapeDtypeStruct((channels, hidden_count), F32),
            jax.ShapeDtypeStruct((hidden_count, channels), F32),
            jax.ShapeDtypeStruct((HEADS, channels), F32),
            jax.ShapeDtypeStruct((1, channels), F32),
            jax.ShapeDtypeStruct((1, channels), F32),
        ),
        in_specs=[vmem] * (5 + len(waves)),
        out_specs=(hbm,) * 10,
        scratch_shapes=[
            pltpu.VMEM((channels, hidden_count), F32),
            pltpu.VMEM((channels, hidden_count), F32),
            pltpu.VMEM((hidden_count, channels), F32),
            pltpu.VMEM((HEADS, channels), F32),
            pltpu.VMEM((1, channels), F32),
            pltpu.VMEM((1, channels), F32),
            dma((10,)),
        ],
        compiler_params=pltpu.CompilerParams(vmem_limit_bytes=8 * 1024 * 1024),
        name="finish_weights",
    )(tail, *outputs, *weights)
    return (
        query_grad[None],
        key_grad[None],
        value_grad[None],
        pair_grad.reshape(1, 1, share, block_count, block_rows, channels),
        gate_grad,
        up_grad,
        down_grad,
        head_grad.T,
        first_grad.reshape(channels),
        second_grad.reshape(channels),
    )


def solution(mesh):
    mesh_shape = (mesh.shape["noise"], mesh.shape["qi"], mesh.shape["kj"])
    return jax.shard_map(
        functools.partial(local, mesh_shape),
        mesh=mesh,
        in_specs=(
            P("qi", None, "kj", None),
            P("noise", "qi", None),
            P("noise", None, "kj", None),
            P("noise", None, "kj", None),
            P("noise", "qi", None),
            P(),
            P(),
            P(),
            P(),
            P(),
            P(),
        ),
        out_specs=(
            P("noise", ("qi", "kj"), None),
            P("noise", ("qi", "kj"), None),
            P("noise", ("qi", "kj"), None),
            P("qi", "noise", None, None, "kj", None),
            P(),
            P(),
            P(),
            P(),
            P(),
            P(),
        ),
        check_vma=False,
    )
```
